32 devices in a mesh: segment: 4 (over y, x), dp: 8 (over z, core).
Axes of the slice: x: 2, y: 2, z: 4, core: 2. Of those that a mesh axis runs over, the one named last changes fastest.
Arguments:
- input_tiles: bfloat16 [16, 1024, 276], P('dp'), may hold values from -6 to 6
- truth_fields: bfloat16 [16, 1024, 276], P('dp'), may hold values from -6 to 6
- horizon_group_label: int32 [16], P('dp'), may hold values from 0 to 2
- var_ids: int32 [69], replicated, may hold values from 0 to 68
- spectral_basis: float32 [256, 256], replicated, may hold values from -0.375 to 0.375
- embed_rows: float32 [349, 384], P(None, 'dp'), may hold values from -6 to 6
- qkv_weight: float32 [2, 384, 1152], P(None, 'dp'), may hold values from -0.3125 to 0.3125
- out_weight: float32 [2, 384, 384], P(None, 'dp'), may hold values from -1.25 to 1.25
- up_weight: float32 [2, 384, 1536], P(None, 'dp'), may hold values from -0.3125 to 0.3125
- down_weight: float32 [2, 1536, 384], P(None, None, 'dp'), may hold values from -0.15625 to 0.15625
- ada_weight: float32 [2, 384, 2304], P(None, 'dp'), may hold values from -0.3125 to 0.3125
- head_weight: float32 [384, 276], P('dp'), may hold values from -0.3125 to 0.3125
- embed_momentum: float32 [349, 384], P(None, 'dp'), may hold values from -2.3841858e-06 to 2.3841858e-06
- qkv_momentum: float32 [2, 384, 1152], P(None, 'dp'), may hold values from -2.3841858e-06 to 2.3841858e-06
- out_momentum: float32 [2, 384, 384], P(None, 'dp'), may hold values from -2.3841858e-06 to 2.3841858e-06
- up_momentum: float32 [2, 384, 1536], P(None, 'dp'), may hold values from -2.3841858e-06 to 2.3841858e-06
- down_momentum: float32 [2, 1536, 384], P(None, None, 'dp'), may hold values from -2.3841858e-06 to 2.3841858e-06
- ada_momentum: float32 [2, 384, 2304], P(None, 'dp'), may hold values from -2.3841858e-06 to 2.3841858e-06
- head_momentum: float32 [384, 276], P('dp'), may hold values from -2.3841858e-06 to 2.3841858e-06
- embed_average: float32 [349, 384], P(None, 'dp'), may hold values from -6 to 6
- qkv_average: float32 [2, 384, 1152], P(None, 'dp'), may hold values from -0.3125 to 0.3125
- out_average: float32 [2, 384, 384], P(None, 'dp'), may hold values from -1.25 to 1.25
- up_average: float32 [2, 384, 1536], P(None, 'dp'), may hold values from -0.3125 to 0.3125
- down_average: float32 [2, 1536, 384], P(None, None, 'dp'), may hold values from -0.15625 to 0.15625
- ada_average: float32 [2, 384, 2304], P(None, 'dp'), may hold values from -0.3125 to 0.3125
- head_average: float32 [384, 276], P('dp'), may hold values from -0.3125 to 0.3125
Outputs:
- loss_value: float32 [], replicated
- clip_norm: float32 [], replicated
- embed_next: float32 [349, 384], P(None, 'dp')
- qkv_next: float32 [2, 384, 1152], P(None, 'dp')
- out_next: float32 [2, 384, 384], P(None, 'dp')
- up_next: float32 [2, 384, 1536], P(None, 'dp')
- down_next: float32 [2, 1536, 384], P(None, None, 'dp')
- ada_next: float32 [2, 384, 2304], P(None, 'dp')
- head_next: float32 [384, 276], P('dp')
- embed_momentum_next: float32 [349, 384], P(None, 'dp')
- qkv_momentum_next: float32 [2, 384, 1152], P(None, 'dp')
- out_momentum_next: float32 [2, 384, 384], P(None, 'dp')
- up_momentum_next: float32 [2, 384, 1536], P(None, 'dp')
- down_momentum_next: float32 [2, 1536, 384], P(None, None, 'dp')
- ada_momentum_next: float32 [2, 384, 2304], P(None, 'dp')
- head_momentum_next: float32 [384, 276], P('dp')
- embed_average_next: float32 [349, 384], P(None, 'dp')
- qkv_average_next: float32 [2, 384, 1152], P(None, 'dp')
- out_average_next: float32 [2, 384, 384], P(None, 'dp')
- up_average_next: float32 [2, 384, 1536], P(None, 'dp')
- down_average_next: float32 [2, 1536, 384], P(None, None, 'dp')
- ada_average_next: float32 [2, 384, 2304], P(None, 'dp')
- head_average_next: float32 [384, 276], P('dp')
The draws below stay inside these ranges and needn't reach their ends.
Inputs may be any that keep to these rules, and one draw needn't show every extreme that they name: `horizon_group_label`: 0 stands for 6 h, 1 for 12 h, 2 for 24 h.
All inputs are finite; a program needn't handle non-finite values.
Results may differ from the reference program's by a relative error of at most 0.012.
The reference program's roundings to bfloat16 on the way count: a program that leaves them out, or rounds other values in their place, can miss the bound.
Values may be sent and summed in bfloat16 or wider, within the bound.
No kernel may reach another device: no remote copies, remote signals or barrier semaphores. Data moves between devices by JAX's collectives and lax.ppermute only.
A program may use at most 192 MiB of HBM per device.

```python
import math
import jax
import jax.numpy as jnp
from jax import lax

D = 384
HEADS = 6
HEAD_DIM = 64
FF = 1536
VARS = 69
CHANNELS = 69
LONP = 128
LATP = 8
LAYERS = 2
HORIZON_GROUPS = 3
QB = 512
TILE_FEATURES = 276
EROWS = 349
TILES_PER_MAP = 1024
NLON = 256
PREDICTION_TOTAL = 16
NPARAM = 5548416


def set_ends(array, key, low, high):
    longest = array.shape.index(max(array.shape))
    spots = []
    for shift in (0, 1):
        where = [jax.random.randint(jax.random.fold_in(key, axis), (), 0, length) for axis, length in enumerate(array.shape)]
        where[longest] = (where[longest] + shift) % array.shape[longest]
        spots.append(tuple(where))
    return array.at[spots[0]].set(low).at[spots[1]].set(high)


def shard_levels(stream_key, extent, shards, smallest, high):
    def one(position, parts):
        steps = jax.random.uniform(jax.random.fold_in(jax.random.fold_in(stream_key, 6), position), (parts,), jnp.float32, smallest / len(shards), high / len(shards))
        return jnp.repeat(jnp.exp(steps), extent[position] // parts).reshape((-1,) + (1,) * (len(extent) - position - 1))

    loudness = one(*shards[0])
    for cut in shards[1:]:
        loudness = loudness * one(*cut)
    return loudness


def centred(rng, shape, deviation, bound, split=(), kind=jnp.bfloat16):
    array = jax.random.normal(rng, shape, jnp.float32) * deviation
    if len(split) > 0:
        array = shard_levels(rng, shape, split, -0.22, 0.18) * array
    return jnp.clip(array, min=-bound, max=bound).astype(kind)


def setup_inputs(seed: int = 0) -> dict:
    key_list = jax.random.split(jax.random.key(seed), 27)
    input_tiles = centred(key_list[0], (PREDICTION_TOTAL, TILES_PER_MAP, TILE_FEATURES), 1.0, 6.0, ((0, 8),))
    truth_fields = centred(key_list[1], (PREDICTION_TOTAL, TILES_PER_MAP, TILE_FEATURES), 1.0, 6.0, ((0, 8),))
    horizon_group_label = set_ends(jax.random.randint(key_list[2], (PREDICTION_TOTAL,), 0, HORIZON_GROUPS), jax.random.fold_in(key_list[2], 1), 0, HORIZON_GROUPS - 1).astype(jnp.int32)
    var_ids = set_ends(jax.random.randint(key_list[3], (CHANNELS,), 0, VARS), jax.random.fold_in(key_list[3], 1), 0, VARS - 1).astype(jnp.int32)
    spectral_basis = centred(key_list[4], (NLON, NLON), NLON ** -0.5, 0.375, (), jnp.float32)
    embed_rows = centred(key_list[5], (EROWS, D), 1.0, 6.0, ((1, 8),), jnp.float32)
    qkv_weight = centred(key_list[6], (LAYERS, D, 3 * D), D ** -0.5, 0.3125, ((1, 8),), jnp.float32)
    out_weight = centred(key_list[7], (LAYERS, D, D), (D // 16) ** -0.5, 1.25, ((1, 8),), jnp.float32)
    up_weight = centred(key_list[8], (LAYERS, D, FF), D ** -0.5, 0.3125, ((1, 8),), jnp.float32)
    down_weight = centred(key_list[9], (LAYERS, FF, D), FF ** -0.5, 0.15625, ((2, 8),), jnp.float32)
    ada_weight = centred(key_list[10], (LAYERS, D, 6 * D), D ** -0.5, 0.3125, ((1, 8),), jnp.float32)
    head_weight = centred(key_list[11], (D, TILE_FEATURES), D ** -0.5, 0.3125, ((0, 8),), jnp.float32)
    embed_momentum = centred(key_list[12], (EROWS, D), (0.001 / NPARAM ** 0.5), 2.384185791015625e-06, ((1, 8),), jnp.float32)
    qkv_momentum = centred(key_list[13], (LAYERS, D, 3 * D), (0.001 / NPARAM ** 0.5), 2.384185791015625e-06, ((1, 8),), jnp.float32)
    out_momentum = centred(key_list[14], (LAYERS, D, D), (0.001 / NPARAM ** 0.5), 2.384185791015625e-06, ((1, 8),), jnp.float32)
    up_momentum = centred(key_list[15], (LAYERS, D, FF), (0.001 / NPARAM ** 0.5), 2.384185791015625e-06, ((1, 8),), jnp.float32)
    down_momentum = centred(key_list[16], (LAYERS, FF, D), (0.001 / NPARAM ** 0.5), 2.384185791015625e-06, ((2, 8),), jnp.float32)
    ada_momentum = centred(key_list[17], (LAYERS, D, 6 * D), (0.001 / NPARAM ** 0.5), 2.384185791015625e-06, ((1, 8),), jnp.float32)
    head_momentum = centred(key_list[18], (D, TILE_FEATURES), (0.001 / NPARAM ** 0.5), 2.384185791015625e-06, ((0, 8),), jnp.float32)
    embed_average = centred(key_list[19], (EROWS, D), 1.0, 6.0, ((1, 8),), jnp.float32)
    qkv_average = centred(key_list[20], (LAYERS, D, 3 * D), D ** -0.5, 0.3125, ((1, 8),), jnp.float32)
    out_average = centred(key_list[21], (LAYERS, D, D), (D // 16) ** -0.5, 1.25, ((1, 8),), jnp.float32)
    up_average = centred(key_list[22], (LAYERS, D, FF), D ** -0.5, 0.3125, ((1, 8),), jnp.float32)
    down_average = centred(key_list[23], (LAYERS, FF, D), FF ** -0.5, 0.15625, ((2, 8),), jnp.float32)
    ada_average = centred(key_list[24], (LAYERS, D, 6 * D), D ** -0.5, 0.3125, ((1, 8),), jnp.float32)
    head_average = centred(key_list[25], (D, TILE_FEATURES), D ** -0.5, 0.3125, ((0, 8),), jnp.float32)
    return {"input_tiles": input_tiles, "truth_fields": truth_fields, "horizon_group_label": horizon_group_label, "var_ids": var_ids, "spectral_basis": spectral_basis, "embed_rows": embed_rows, "qkv_weight": qkv_weight, "out_weight": out_weight, "up_weight": up_weight, "down_weight": down_weight, "ada_weight": ada_weight, "head_weight": head_weight, "embed_momentum": embed_momentum, "qkv_momentum": qkv_momentum, "out_momentum": out_momentum, "up_momentum": up_momentum, "down_momentum": down_momentum, "ada_momentum": ada_momentum, "head_momentum": head_momentum, "embed_average": embed_average, "qkv_average": qkv_average, "out_average": out_average, "up_average": up_average, "down_average": down_average, "ada_average": ada_average, "head_average": head_average}


highest = lax.Precision.HIGHEST
eps_norm = 1e-06
clip_limit = 0.001
momentum_keep = 0.9
average_keep = 0.9
embed_boost = 20.0

@jax.custom_vjp
def low(v):
    return lax.optimization_barrier(v.astype(jnp.bfloat16)).astype(jnp.float32)

@jax.custom_vjp
def low_back(v):
    return v

def low_keep(v):
    return (low(v), None)

def low_pass(kept, grad):
    return (grad,)

def back_keep(v):
    return (v, None)

def back_low(kept, grad):
    return (low(grad),)
low.defvjp(low_keep, low_pass)
low_back.defvjp(back_keep, back_low)

def round_both(values):
    return low_back(low(values))

def matmul(left, right):
    return jnp.dot(left, right, precision=highest, preferred_element_type=jnp.float32)

def normalize(values):
    centered = values - lax.optimization_barrier(jnp.mean(values, axis=-1, keepdims=True))
    return centered * lax.rsqrt(lax.optimization_barrier(jnp.mean(centered * centered, axis=-1, keepdims=True)) + eps_norm)

def modulate(values, offset, stretch):
    return normalize(values) * (1.0 + stretch) + offset

def aggregate(rows_float, grid_point_entries, var_ids):
    patch_rows = rows_float[:TILE_FEATURES]
    var_table = rows_float[TILE_FEATURES:TILE_FEATURES + VARS]
    agg_query = rows_float[TILE_FEATURES + VARS]
    one_hot = (var_ids[:, None] == jnp.arange(VARS, dtype=jnp.int32)[None, :]).astype(jnp.float32)
    channel_bases = matmul(one_hot, var_table)
    projected = matmul(patch_rows, agg_query[:, None])[:, 0].reshape(CHANNELS, 4)
    grouped = grid_point_entries.reshape(grid_point_entries.shape[0], CHANNELS, 4)
    scores = lax.optimization_barrier(jnp.sum(grouped * projected[None], axis=-1)) + matmul(channel_bases, agg_query[:, None])[:, 0][None, :]
    weights = jax.nn.softmax(scores * D ** (-0.5), axis=-1)
    spread = (weights[:, :, None] * grouped).reshape(grid_point_entries.shape[0], TILE_FEATURES)
    return (spread, matmul(weights, channel_bases))

def conditioning(ada_float, lead_rows, horizon_hours):
    one_hot = (jnp.arange(HORIZON_GROUPS, dtype=jnp.int32) == horizon_hours).astype(jnp.float32)
    condition = matmul(one_hot[None, :], lead_rows)[0]
    return matmul(jax.nn.silu(condition)[None, :], ada_float)[0].reshape(6, -1)

def split_heads(qkv_rows):
    return qkv_rows.reshape(qkv_rows.shape[0], 3, HEADS, HEAD_DIM).transpose(1, 2, 0, 3)

def spectrum(surface, spectral_basis):
    field_grid = surface.reshape(LATP, LONP, CHANNELS, 2, 2)
    wave_terms = jnp.einsum('plcab,lbk->pcak', field_grid, spectral_basis.reshape(LONP, 2, 2 * LONP), precision=highest)
    return wave_terms[..., :LONP] ** 2 + wave_terms[..., LONP:] ** 2

def attention(qkv_rows):
    sections = split_heads(qkv_rows)
    tokens = qkv_rows.shape[0]
    grouped = sections[0].reshape(HEADS, tokens // QB, QB, HEAD_DIM).transpose(1, 0, 2, 3)

    def one_block(query_block):
        scores = jnp.einsum('hqd,hkd->hqk', query_block, sections[1], precision=highest) * HEAD_DIM ** (-0.5)
        probs = low(jax.nn.softmax(low_back(scores), axis=-1))
        return jnp.einsum('hqk,hkd->hqd', probs, sections[2], precision=highest)
    outputs = lax.map(jax.checkpoint(one_block), grouped)
    return round_both(outputs.transpose(0, 2, 1, 3).reshape(tokens, HEADS * HEAD_DIM))

def block_layer(hidden, layer_weights, modulation):
    qkv_rows_w, out_rows_w, up_rows_w, down_rows_w = layer_weights
    normed = low(modulate(hidden, modulation[0], modulation[1]))
    qkv_rows = round_both(matmul(normed, qkv_rows_w))
    attended = attention(qkv_rows)
    branch_one = low_back(matmul(attended, out_rows_w))
    middle = hidden + modulation[2] * branch_one
    normed_two = low(modulate(middle, modulation[3], modulation[4]))
    hidden_units = low_back(matmul(normed_two, up_rows_w))
    activated = low(jax.nn.gelu(hidden_units, approximate=True))
    branch_two = low_back(matmul(activated, down_rows_w))
    return middle + modulation[5] * branch_two

def reference(input_tiles, truth_fields, horizon_group_label, var_ids, spectral_basis, embed_rows, qkv_weight, out_weight, up_weight, down_weight, ada_weight, head_weight, embed_momentum, qkv_momentum, out_momentum, up_momentum, down_momentum, ada_momentum, head_momentum, embed_average, qkv_average, out_average, up_average, down_average, ada_average, head_average):
    masters = (embed_rows, qkv_weight, out_weight, up_weight, down_weight, ada_weight, head_weight)
    moments = (embed_momentum, qkv_momentum, out_momentum, up_momentum, down_momentum, ada_momentum, head_momentum)
    averages = (embed_average, qkv_average, out_average, up_average, down_average, ada_average, head_average)
    rate_factors = (embed_boost, 1.0, 1.0, 1.0, 1.0, 1.0, 1.0)
    rounded = tuple((low(weight) for weight in masters))
    prediction_group = input_tiles.shape[0]
    lead_start = TILE_FEATURES + VARS + 1

    def error_each_prediction(network_weights_tree, grid_point_entries, truth_tile_matrix, horizon_hours):
        rows_float, qkv_all, out_all, up_all, down_all, ada_all, head_rows = network_weights_tree
        spread, base_term = aggregate(rows_float, grid_point_entries, var_ids)
        hidden = round_both(matmul(low(spread), rows_float[:TILE_FEATURES]) + base_term)
        for layer in range(LAYERS):
            modulation = conditioning(ada_all[layer], rows_float[lead_start:], horizon_hours)
            hidden = round_both(block_layer(hidden, (qkv_all[layer], out_all[layer], up_all[layer], down_all[layer]), modulation))
        flat_rows = low(normalize(hidden))
        predicted = low_back(matmul(flat_rows, head_rows))
        power_gap = spectrum(predicted, spectral_basis) - spectrum(truth_tile_matrix, spectral_basis)
        return jnp.mean(power_gap * power_gap)

    def total_loss(network_weights_tree):

        def accumulate(running_accumulator, minibatch_span):
            return (running_accumulator + jax.checkpoint(error_each_prediction)(network_weights_tree, minibatch_span[0], minibatch_span[1], minibatch_span[2]), None)
        accumulated_result, unused = lax.scan(accumulate, jnp.zeros((), jnp.float32), (input_tiles.astype(jnp.float32), truth_fields.astype(jnp.float32), horizon_group_label))
        return accumulated_result / prediction_group
    loss_value, pullback = jax.vjp(total_loss, rounded)
    gradients = pullback(jnp.ones((), jnp.float32))[0]
    squares = sum((jnp.sum(grad_part * grad_part) for grad_part in gradients))
    grad_norm = jnp.sqrt(squares)
    factor = clip_limit / jnp.maximum(grad_norm, clip_limit)
    params_count = sum((weight.size for weight in masters))
    step_rate = 0.02 * math.sqrt(params_count) / clip_limit
    new_weights, new_moments, new_averages = ([], [], [])
    for weight, moment, average, grad_part, rate_factor in zip(masters, moments, averages, gradients, rate_factors):
        clipped = grad_part * factor
        moment_next = momentum_keep * moment + clipped
        weight_next = weight - step_rate * rate_factor * (clipped + momentum_keep * moment_next)
        new_weights.append(weight_next)
        new_moments.append(moment_next)
        new_averages.append(average_keep * average + (1.0 - average_keep) * weight_next)
    return (loss_value, grad_norm, new_weights[0], new_weights[1], new_weights[2], new_weights[3], new_weights[4], new_weights[5], new_weights[6], new_moments[0], new_moments[1], new_moments[2], new_moments[3], new_moments[4], new_moments[5], new_moments[6], new_averages[0], new_averages[1], new_averages[2], new_averages[3], new_averages[4], new_averages[5], new_averages[6])
```

```python
import math

import jax
import jax.numpy as jnp
from jax import lax
from jax.experimental import pallas as pl
from jax.experimental.pallas import tpu as pltpu
from jax.sharding import Mesh, PartitionSpec as P

D = 384
HEADS = 6
HEAD_DIM = 64
FF = 1536
VARS = 69
CHANNELS = 69
LONP = 128
LATP = 8
LAYERS = 2
GROUPS = 3
PIXELS = 276
LEAD = PIXELS + VARS + 1
EROWS = LEAD + GROUPS
ECOLS = 512
EPS = 1e-06
CLIP = 0.001
KEEP = 0.9
BOOST = 20.0
LABEL_LANE = D - 1
HALF = FF // 2

F32 = jnp.float32
BF16 = jnp.bfloat16
CHIP = ("s", "z", "c")


def dot(a, b):
    return jnp.dot(a, b, preferred_element_type=F32)


def dot_nt(a, b):
    return lax.dot_general(a, b, (((1,), (1,)), ((), ())), preferred_element_type=F32)


def dot_tn(a, b):
    return lax.dot_general(a, b, (((0,), (0,)), ((), ())), preferred_element_type=F32)


def parts(x, count):
    out = []
    for step in range(count):
        piece = x.astype(BF16)
        out.append(piece)
        if step < count - 1:
            x = x - piece.astype(F32)
    return out


def normal(v):
    centered = v - jnp.mean(v, axis=-1, keepdims=True)
    inverse = lax.rsqrt(jnp.mean(centered * centered, axis=-1, keepdims=True) + EPS)
    return centered * inverse, inverse


def normal_back(d_x, x, inverse):
    return inverse * (
        d_x - jnp.mean(d_x, axis=-1, keepdims=True) - x * jnp.mean(d_x * x, axis=-1, keepdims=True)
    )


def lane_below(limit, shape):
    return lax.broadcasted_iota(jnp.int32, shape, len(shape) - 1) < limit


def same_group():
    row = lax.broadcasted_iota(jnp.int32, (D, D), 0)
    col = lax.broadcasted_iota(jnp.int32, (D, D), 1)
    return (row // 4 == col // 4).astype(BF16)


def chosen_table(vid_ref):
    row = lax.broadcasted_iota(jnp.int32, (ECOLS, D), 0)
    return (row - PIXELS == vid_ref[...]).astype(BF16)


def first_of_four(shape):
    lane = lax.broadcasted_iota(jnp.int32, shape, len(shape) - 1)
    return lane % 4 == 0


def cost(flops, size, exps=0):
    return pl.CostEstimate(flops=int(flops), bytes_accessed=int(size), transcendentals=int(exps))


def params(limit=40):
    return pltpu.CompilerParams(vmem_limit_bytes=limit << 20)


def embed_kernel(tiles_ref, emb_ref, vid_ref, out_ref, agg_ref, row_sc, base_sc, bases_sc):
    @pl.when(pl.program_id(0) == 0)
    def _():
        emb = emb_ref[...].astype(F32)
        row = jnp.sum(emb * emb[:, LEAD - 1 : LEAD], axis=0, keepdims=True)
        row_sc[...] = jnp.where(lane_below(PIXELS, (1, D)), row[:, :D], 0.0)
        table = chosen_table(vid_ref)
        wide = jnp.broadcast_to(row, (8, ECOLS))
        base_sc[...] = sum(dot(p, table) for p in parts(wide, 3))[:1]
        bases = dot(emb_ref[...], table)
        bases_sc[...] = jnp.where(first_of_four((D, D)), bases, 0.0).astype(BF16)

    x = tiles_ref[...].astype(F32)
    group = same_group()
    scores = sum(dot(p, group) for p in parts(x * row_sc[...], 3)) + base_sc[...]
    scores = jnp.where(lane_below(PIXELS, scores.shape), scores * D ** (-0.5), -1e30)
    e = jnp.exp(scores - jnp.max(scores, axis=-1, keepdims=True))
    agg = e / (0.25 * jnp.sum(e, axis=-1, keepdims=True))
    agg_ref[...] = agg
    spread = (agg * x).astype(BF16)
    total = dot_nt(spread, emb_ref[:, :D])
    for p in parts(agg, 2):
        total = total + dot_nt(p, bases_sc[...])
    out_ref[...] = total.astype(BF16)


def embed(data, emb, vid4, tokens):
    rows = 256
    return pl.pallas_call(
        embed_kernel,
        grid=(tokens // rows,),
        in_specs=[
            pl.BlockSpec((rows, D), lambda i: (i, 0)),
            pl.BlockSpec((D, ECOLS), lambda i: (0, 0)),
            pl.BlockSpec((1, D), lambda i: (0, 0)),
        ],
        out_specs=[
            pl.BlockSpec((rows, D), lambda i: (i, 0)),
            pl.BlockSpec((rows, D), lambda i: (i, 0)),
        ],
        out_shape=[
            jax.ShapeDtypeStruct((tokens, D), BF16),
            jax.ShapeDtypeStruct((tokens, D), F32),
        ],
        scratch_shapes=[
            pltpu.VMEM((1, D), F32),
            pltpu.VMEM((1, D), F32),
            pltpu.VMEM((D, D), BF16),
        ],
        compiler_params=params(),
        cost_estimate=cost(2e9 * 3, 4e6, 4e5),
        name="embed",
    )(data, emb, vid4)


def embed_back_kernel(dh_ref, tiles_ref, agg_ref, emb_ref, vid_ref, out_ref):
    dh = dh_ref[...]
    x = tiles_ref[...].astype(F32)
    agg = agg_ref[...]
    emb = emb_ref[...]
    table = chosen_table(vid_ref)
    group = same_group()
    bases = dot(emb, table).astype(BF16)
    query = emb[:, LEAD - 1 : LEAD].astype(F32)
    spread = (agg * x).astype(BF16)
    g_patch = dot_tn(dh, spread)
    d_spread = dot(dh, emb[:, :D])
    d_agg = dot(dh, bases)
    for p in parts(d_spread * x, 2):
        d_agg = d_agg + dot(p, group)
    inner = 0.25 * jnp.sum(agg * d_agg, axis=-1, keepdims=True)
    d_scores = agg * (d_agg - inner) * D ** (-0.5)
    d_proj = jnp.sum(d_scores * x, axis=0, keepdims=True)
    d_base = jnp.sum(d_scores, axis=0, keepdims=True)
    d_base = jnp.where(first_of_four(d_base.shape), d_base, 0.0)
    only = first_of_four(agg.shape)
    d_bases = query * d_base
    for p in parts(jnp.where(only, agg, 0.0), 2):
        d_bases = d_bases + dot_tn(dh, p)
    g_table = sum(dot_nt(p, table) for p in parts(d_bases, 2))
    d_query = jnp.sum(
        emb[:, :D].astype(F32) * d_proj + bases.astype(F32) * d_base, axis=-1, keepdims=True
    )
    lane = lax.broadcasted_iota(jnp.int32, (D, ECOLS), 1)
    total = g_table + jnp.where(lane == LEAD - 1, d_query, 0.0)
    first = total[:, :D] + g_patch + query * d_proj
    for j in range(3):
        out_ref[j] = first[:, 128 * j : 128 * j + 128].astype(BF16)
    out_ref[3] = total[:, D:].astype(BF16)


def embed_back(dh, data, agg, emb, vid4):
    rows = dh.shape[0]
    return pl.pallas_call(
        embed_back_kernel,
        grid=(1,),
        in_specs=[
            pl.BlockSpec((rows, D), lambda i: (0, 0)),
            pl.BlockSpec((rows, D), lambda i: (0, 0)),
            pl.BlockSpec((rows, D), lambda i: (0, 0)),
            pl.BlockSpec((D, ECOLS), lambda i: (0, 0)),
            pl.BlockSpec((1, D), lambda i: (0, 0)),
        ],
        out_specs=pl.BlockSpec((4, D, 128), lambda i: (0, 0, 0)),
        out_shape=jax.ShapeDtypeStruct((4, D, 128), BF16),
        compiler_params=params(),
        cost_estimate=cost(3e9, 4e6),
        name="embed_back",
    )(dh, data, agg, emb, vid4)


def qkv_kernel(h_ref, mod_ref, w_ref, normed_ref, qkv_ref):
    x, _ = normal(h_ref[...].astype(F32))
    normed = (x * (1.0 + mod_ref[1:2]) + mod_ref[0:1]).astype(BF16)
    normed_ref[...] = normed
    for j in range(3):
        qkv_ref[:, D * j : D * (j + 1)] = dot(normed, w_ref[j]).astype(BF16)


def qkv_rows(h, start, count, mod, weights):
    rows = 256
    return pl.pallas_call(
        qkv_kernel,
        grid=(count // rows,),
        in_specs=[
            pl.BlockSpec((rows, D), lambda i: (i + start // rows, 0)),
            pl.BlockSpec((8, D), lambda i: (0, 0)),
            pl.BlockSpec((4, D, D), lambda i: (0, 0, 0)),
        ],
        out_specs=[
            pl.BlockSpec((rows, D), lambda i: (i, 0)),
            pl.BlockSpec((rows, 3 * D), lambda i: (i, 0)),
        ],
        out_shape=[
            jax.ShapeDtypeStruct((count, D), BF16),
            jax.ShapeDtypeStruct((count, 3 * D), BF16),
        ],
        compiler_params=params(),
        cost_estimate=cost(2 * count * D * 3 * D, 3e6),
        name="qkv_rows",
    )(h, mod, weights)


def pair_masks():
    low = lane_below(HEAD_DIM, (1, 128))
    return low, jnp.logical_not(low)


def block_kernel(
    h_ref,
    q_ref,
    own_ref,
    other_ref,
    mod_ref,
    w_ref,
    out_ref,
    att_ref,
    lse_ref,
    one_ref,
    mid_ref,
    n2_ref,
    units_ref,
    act_ref,
    two_ref,
):
    zero = jnp.zeros((), BF16)
    rows = h_ref.shape[0]
    lane = lax.broadcasted_iota(jnp.int32, (rows, 128), 1)
    sums = jnp.zeros((rows, 128), F32)
    attended = []
    for pair in range(HEADS // 2):
        a = 128 * pair
        q = q_ref[:, a : a + 128] * 0.125
        keys = jnp.concatenate([own_ref[:, D + a : D + a + 128], other_ref[:, D + a : D + a + 128]])
        vals = jnp.concatenate(
            [own_ref[:, 2 * D + a : 2 * D + a + 128], other_ref[:, 2 * D + a : 2 * D + a + 128]]
        )
        mixed = jnp.zeros((rows, 128), F32)
        for which, mask in enumerate(pair_masks()):
            scores = dot_nt(q, jnp.where(mask, keys, zero))
            top = jnp.max(scores, axis=-1, keepdims=True)
            e = jnp.exp(scores - top)
            total = jnp.sum(e, axis=-1, keepdims=True)
            probs = (e * (1.0 / total)).astype(BF16)
            mixed = mixed + dot(probs, jnp.where(mask, vals, zero))
            sums = jnp.where(lane == 2 * pair + which, top + jnp.log(total), sums)
        attended.append(mixed.astype(BF16))
    lse_ref[...] = sums
    attended = jnp.concatenate(attended, axis=-1)
    att_ref[...] = attended
    one = dot(attended, w_ref[3, :, :D])
    one_ref[...] = one
    middle = h_ref[...].astype(F32) + mod_ref[2:3] * one
    mid_ref[...] = middle
    x, _ = normal(middle)
    n2 = (x * (1.0 + mod_ref[4:5]) + mod_ref[3:4]).astype(BF16)
    n2_ref[...] = n2
    two = jnp.zeros((rows, D), F32)
    for j in range(2):
        units = dot(n2, w_ref[j, :, D:])
        units_ref[:, HALF * j : HALF * (j + 1)] = units
        act = jax.nn.gelu(units, approximate=True).astype(BF16)
        act_ref[:, HALF * j : HALF * (j + 1)] = act
        two = two + dot_nt(act, w_ref[2 + j, :, D:])
    two_ref[...] = two
    out_ref[...] = (middle + mod_ref[5:6] * two).astype(BF16)


def block_forward(h, own, other, mod, weights):
    count, rows = own.shape[0], 256
    row = lambda width: pl.BlockSpec((rows, width), lambda i: (i, 0))
    sds = jax.ShapeDtypeStruct
    return pl.pallas_call(
        block_kernel,
        grid=(count // rows,),
        in_specs=[
            row(D),
            row(D),
            pl.BlockSpec((count, 3 * D), lambda i: (0, 0)),
            pl.BlockSpec((count, 3 * D), lambda i: (0, 0)),
            pl.BlockSpec((8, D), lambda i: (0, 0)),
            pl.BlockSpec((4, D, 3 * D), lambda i: (0, 0, 0)),
        ],
        out_specs=[row(D), row(D), row(128), row(D), row(D), row(D), row(FF), row(FF), row(D)],
        out_shape=[
            sds((count, D), BF16),
            sds((count, D), BF16),
            sds((count, 128), F32),
            sds((count, D), F32),
            sds((count, D), F32),
            sds((count, D), BF16),
            sds((count, FF), F32),
            sds((count, FF), BF16),
            sds((count, D), F32),
        ],
        compiler_params=params(),
        cost_estimate=cost(8e9, 1.2e7, 3e6),
        name="block_forward",
    )(h, own, own, other, mod, weights)


def head_kernel(h_ref, truth_ref, w_ref, fwd_ref, back_ref, dh_ref, g_ref, loss_ref, *, seed):
    count = h_ref.shape[0]
    x, inverse = normal(h_ref[...].astype(F32))
    flat = x.astype(BF16)
    pred = [dot(flat, w_ref[j]) for j in range(4)]
    pred = [jnp.concatenate(pred[:2], axis=-1), jnp.concatenate(pred[2:], axis=-1)]
    row = lax.broadcasted_iota(jnp.int32, (D, 256), 0)
    col = lax.broadcasted_iota(jnp.int32, (D, 256), 1)
    inside = col < PIXELS // 2
    true = []
    for b in range(2):
        pick = jnp.logical_and(row == 2 * col + b, inside).astype(BF16)
        true.append(dot(truth_ref[...], pick).astype(BF16))
    fwd = parts(fwd_ref[...], 2)
    back = parts(back_ref[...], 2)
    entries = LATP * CHANNELS * 2 * LONP
    loss = jnp.zeros((1, 1), F32)
    grads = [[], []]
    for p in range(count // LONP):
        part = slice(p * LONP, (p + 1) * LONP)
        seen = parts(jnp.concatenate([pred[0][part], pred[1][part]], axis=0), 2)
        waves = dot(fwd[0], seen[0]) + (dot(fwd[0], seen[1]) + dot(fwd[1], seen[0]))
        want = jnp.concatenate([true[0][part], true[1][part]], axis=0)
        target = dot(fwd[0], want) + dot(fwd[1], want)
        top, low = waves[:LONP], waves[LONP:]
        gap = (top * top + low * low) - (
            target[:LONP] * target[:LONP] + target[LONP:] * target[LONP:]
        )
        loss = loss + jnp.sum(gap * gap, axis=(0, 1), keepdims=True)
        scaled = gap * (4.0 * seed / entries)
        d_waves = parts(jnp.concatenate([scaled * top, scaled * low], axis=0), 2)
        d_seen = dot(back[0], d_waves[0]) + (dot(back[0], d_waves[1]) + dot(back[1], d_waves[0]))
        d_seen = d_seen.astype(BF16)
        grads[0].append(d_seen[:LONP])
        grads[1].append(d_seen[LONP:])
    loss_ref[...] = jnp.broadcast_to(loss * (seed / entries), loss_ref.shape)
    d_flat = jnp.zeros((count, D), F32)
    for b in range(2):
        whole = jnp.concatenate(grads[b], axis=0)
        for j in range(2):
            piece = whole[:, 128 * j : 128 * (j + 1)]
            d_flat = d_flat + dot_nt(piece, w_ref[2 * b + j])
            g_ref[2 * b + j] = dot_tn(flat, piece).astype(BF16)
    dh_ref[...] = normal_back(d_flat, x, inverse).astype(BF16)


def head(h, data, weights, basis_fwd, basis_back, seed, tokens):
    count = h.shape[0]
    sds = jax.ShapeDtypeStruct
    whole = lambda shape: pl.BlockSpec(shape, lambda i: (0,) * len(shape))
    return pl.pallas_call(
        lambda *refs: head_kernel(*refs, seed=seed),
        grid=(1,),
        in_specs=[
            whole((count, D)),
            pl.BlockSpec((count, D), lambda i: (tokens // count, 0)),
            pl.BlockSpec((4, D, 128), lambda i: (0, 0, 3 * D // 128)),
            whole((256, 256)),
            whole((256, 256)),
        ],
        out_specs=[whole((count, D)), whole((4, D, 128)), whole((8, 128))],
        out_shape=[sds((count, D), BF16), sds((4, D, 128), BF16), sds((8, 128), F32)],
        compiler_params=params(),
        cost_estimate=cost(3e9, 3e6),
        name="head",
    )(h, data, weights, basis_fwd, basis_back)


def gelu_slope(u):
    k = math.sqrt(2.0 / math.pi)
    t = jnp.tanh(k * (u + 0.044715 * (u * u * u)))
    return 0.5 * (1.0 + t) + 0.5 * u * (1.0 - t * t) * k * (1.0 + 3 * 0.044715 * (u * u))


def column_sum(v):
    return jnp.sum(v, axis=0, keepdims=True)


def mlp_back_kernel(
    dout_ref,
    two_ref,
    act_ref,
    units_ref,
    n2_ref,
    mid_ref,
    one_ref,
    att_ref,
    mod_ref,
    w_ref,
    dmid_ref,
    datt_ref,
    g_ref,
    gout_ref,
    dmod_ref,
):
    d_out = dout_ref[...].astype(F32)
    d_two = (mod_ref[5:6] * d_out).astype(BF16)
    g_gate_two = column_sum(d_out * two_ref[...])
    d_n2 = jnp.zeros(d_out.shape, F32)
    n2 = n2_ref[...]
    for j in range(2):
        part = slice(HALF * j, HALF * (j + 1))
        g_ref[2 + j] = dot_tn(d_two, act_ref[:, part]).astype(BF16)
        d_units = (gelu_slope(units_ref[:, part]) * dot(d_two, w_ref[2 + j, :, D:])).astype(BF16)
        g_ref[j] = dot_tn(n2, d_units).astype(BF16)
        d_n2 = d_n2 + dot_nt(d_units, w_ref[j, :, D:])
    x, inverse = normal(mid_ref[...])
    g_shift = column_sum(d_n2)
    g_scale = column_sum(d_n2 * x)
    d_mid = d_out + normal_back(d_n2 * (1.0 + mod_ref[4:5]), x, inverse)
    dmid_ref[...] = d_mid
    d_one = (mod_ref[2:3] * d_mid).astype(BF16)
    g_gate_one = column_sum(d_mid * one_ref[...])
    gout_ref[...] = dot_tn(att_ref[...], d_one).astype(BF16)
    datt_ref[...] = dot_nt(d_one, w_ref[3, :, :D]).astype(BF16)
    blank = jnp.zeros((2, D), F32)
    dmod_ref[...] = jnp.concatenate(
        [blank, g_gate_one, g_shift, g_scale, g_gate_two, blank], axis=0
    )


def mlp_back(d_out, saved, mod, weights):
    attended, lse, one, middle, n2, units, act, two = saved
    count = d_out.shape[0]
    sds = jax.ShapeDtypeStruct
    whole = lambda shape: pl.BlockSpec(shape, lambda i: (0,) * len(shape))
    return pl.pallas_call(
        mlp_back_kernel,
        grid=(1,),
        in_specs=[
            whole((count, D)),
            whole((count, D)),
            whole((count, FF)),
            whole((count, FF)),
            whole((count, D)),
            whole((count, D)),
            whole((count, D)),
            whole((count, D)),
            whole((8, D)),
            whole((4, D, 3 * D)),
        ],
        out_specs=[
            whole((count, D)),
            whole((count, D)),
            whole((4, D, HALF)),
            whole((D, D)),
            whole((8, D)),
        ],
        out_shape=[
            sds((count, D), F32),
            sds((count, D), BF16),
            sds((4, D, HALF), BF16),
            sds((D, D), BF16),
            sds((8, D), F32),
        ],
        compiler_params=params(56),
        cost_estimate=cost(6e9, 1.6e7, 1e6),
        name="mlp_back",
    )(d_out, two, act, units, n2, middle, one, attended, mod, weights)


def attention_back_kernel(q_ref, own_ref, other_ref, lse_ref, datt_ref, dq_ref, dk_ref, dv_ref):
    zero = jnp.zeros((), BF16)
    rows = q_ref.shape[0]
    first = pl.program_id(0) == 0
    for pair in range(HEADS // 2):
        a = 128 * pair
        here = slice(a, a + 128)
        q = q_ref[:, here]
        d_att = datt_ref[:, here]
        keys = jnp.concatenate([own_ref[:, D + a : D + a + 128], other_ref[:, D + a : D + a + 128]])
        vals = jnp.concatenate(
            [own_ref[:, 2 * D + a : 2 * D + a + 128], other_ref[:, 2 * D + a : 2 * D + a + 128]]
        )
        d_q = jnp.zeros((rows, 128), F32)
        d_k = jnp.zeros((keys.shape[0], 128), F32)
        d_v = jnp.zeros((keys.shape[0], 128), F32)
        for which, mask in enumerate(pair_masks()):
            head = 2 * pair + which
            k = jnp.where(mask, keys, zero)
            v = jnp.where(mask, vals, zero)
            scores = dot_nt(q * 0.125, k)
            probs = jnp.exp(scores - lse_ref[:, head : head + 1])
            d_probs = dot_nt(d_att, v)
            inner = jnp.sum(d_probs * probs, axis=-1, keepdims=True)
            d_scores = (probs * (d_probs - inner)).astype(BF16)
            d_q = d_q + dot(d_scores, k)
            d_k = d_k + dot_tn(d_scores, jnp.where(mask, q, zero))
            d_v = d_v + dot_tn(probs.astype(BF16), jnp.where(mask, d_att, zero))
        dq_ref[:, here] = (d_q * 0.125).astype(BF16)

        @pl.when(first)
        def _():
            dk_ref[:, here] = d_k * 0.125
            dv_ref[:, here] = d_v

        @pl.when(jnp.logical_not(first))
        def _():
            dk_ref[:, here] += d_k * 0.125
            dv_ref[:, here] += d_v


def attention_back(own, other, lse, d_att):
    count, rows = own.shape[0], 256
    sds = jax.ShapeDtypeStruct
    return pl.pallas_call(
        attention_back_kernel,
        grid=(count // rows,),
        in_specs=[
            pl.BlockSpec((rows, D), lambda i: (i, 0)),
            pl.BlockSpec((count, 3 * D), lambda i: (0, 0)),
            pl.BlockSpec((count, 3 * D), lambda i: (0, 0)),
            pl.BlockSpec((rows, 128), lambda i: (i, 0)),
            pl.BlockSpec((rows, D), lambda i: (i, 0)),
        ],
        out_specs=[
            pl.BlockSpec((rows, D), lambda i: (i, 0)),
            pl.BlockSpec((2 * count, D), lambda i: (0, 0)),
            pl.BlockSpec((2 * count, D), lambda i: (0, 0)),
        ],
        out_shape=[
            sds((count, D), BF16),
            sds((2 * count, D), F32),
            sds((2 * count, D), F32),
        ],
        compiler_params=params(),
        cost_estimate=cost(8e9, 8e6, 3e6),
        name="attention_back",
    )(own, own, other, lse, d_att)


def qkv_back_kernel(
    dq_ref, dk_ref, dv_ref, got_ref, normed_ref, h_ref, dmid_ref, gout_ref, mod_ref, w_ref,
    dh_ref, g_ref, dmod_ref,
):
    normed = normed_ref[...]
    d_k = (dk_ref[...] + got_ref[0]).astype(BF16)
    d_v = (dv_ref[...] + got_ref[1]).astype(BF16)
    d_n = jnp.zeros(normed.shape, F32)
    for j, piece in enumerate((dq_ref[...], d_k, d_v)):
        g_ref[j] = dot_tn(normed, piece).astype(BF16)
        d_n = d_n + dot_nt(piece, w_ref[j])
    g_ref[3] = gout_ref[...]
    x, inverse = normal(h_ref[...].astype(F32))
    g_shift = column_sum(d_n)
    g_scale = column_sum(d_n * x)
    dh_ref[...] = (
        dmid_ref[...] + normal_back(d_n * (1.0 + mod_ref[1:2]), x, inverse)
    ).astype(BF16)
    dmod_ref[...] = jnp.concatenate([g_shift, g_scale, jnp.zeros((6, D), F32)], axis=0)


def qkv_back(d_q, d_k, d_v, got, normed, h, d_mid, g_out, mod, weights):
    count = d_q.shape[0]
    sds = jax.ShapeDtypeStruct
    whole = lambda shape: pl.BlockSpec(shape, lambda i: (0,) * len(shape))
    return pl.pallas_call(
        qkv_back_kernel,
        grid=(1,),
        in_specs=[
            whole((count, D)),
            whole((count, D)),
            whole((count, D)),
            whole((2, count, D)),
            whole((count, D)),
            whole((count, D)),
            whole((count, D)),
            whole((D, D)),
            whole((8, D)),
            whole((4, D, D)),
        ],
        out_specs=[whole((count, D)), whole((4, D, D)), whole((8, D))],
        out_shape=[sds((count, D), BF16), sds((4, D, D), BF16), sds((8, D), F32)],
        compiler_params=params(),
        cost_estimate=cost(2e9, 8e6),
        name="qkv_back",
    )(d_q, d_k, d_v, got, normed, h, d_mid, g_out, mod, weights)


def swap(x, axis, size, by):
    return lax.ppermute(x, axis, [(i, i ^ by) for i in range(size)])


def place_kernel(where_ref, *refs, columns, rows):
    out_ref, sems = refs[-2], refs[-1]
    inputs = refs[:-2]
    s, z, c = where_ref[0], where_ref[1], where_ref[2]
    copies = []
    index = 0
    for jc in range(2):
        for js in range(columns):
            source = inputs[jc * columns + js]
            for jz in range(source.shape[0]):
                row = ((z ^ jz) * 2 + (c ^ jc)) * rows
                at = pl.ds(pl.multiple_of(row, rows), rows)
                target = out_ref.at[s ^ js, at] if columns > 1 else out_ref.at[at]
                copies.append(pltpu.make_async_copy(source.at[jz], target, sems.at[index]))
                index += 1
    for copy in copies:
        copy.start()
    for copy in copies:
        copy.wait()


def placed(where, own, got):
    columns, (zs, rows, width) = len(own), own[0].shape
    full = (zs * 2 * rows, width)
    shape = (columns,) + full if columns > 1 else full
    return pl.pallas_call(
        lambda *refs: place_kernel(*refs, columns=columns, rows=rows),
        in_specs=[pl.BlockSpec(memory_space=pltpu.SMEM)]
        + [pl.BlockSpec(memory_space=pl.ANY)] * (2 * columns),
        out_specs=pl.BlockSpec(memory_space=pl.ANY),
        out_shape=jax.ShapeDtypeStruct(shape, BF16),
        scratch_shapes=[pltpu.SemaphoreType.DMA((2 * columns * zs,))],
        cost_estimate=cost(0, 4 * math.prod(shape)),
        name="placed",
    )(where, *own, *got)


class Plain:
    def __init__(self, sizes):
        self.sizes = sizes

    def rows(self, x):
        return lax.all_gather(x, ("z", "c"), axis=0, tiled=True)

    def columns(self, x):
        return lax.all_gather(x, ("z", "c"), axis=1, tiled=True)

    def total(self, x, axes):
        return lax.psum(x, axes)

    def reduced(self, g):
        own = lax.psum_scatter(g.astype(F32), ("z", "c"), scatter_dimension=1, tiled=True)
        return lax.psum(own, "s")


class Squares(Plain):
    def __init__(self, sizes):
        super().__init__(sizes)
        self.s = lax.axis_index("s")
        self.z = lax.axis_index("z")
        self.c = lax.axis_index("c")
        self.where = jnp.stack([self.s, self.z, self.c]).astype(jnp.int32)

    def across(self, x, axis):
        return [swap(x, axis, 4, by) for by in (1, 2, 3)]

    def rows(self, x):
        own = jnp.stack([x] + self.across(x, "z"))
        return placed(self.where, [own], [swap(own, "c", 2, 1)])

    def columns(self, x):
        mine = lax.dynamic_index_in_dim(x, self.s, 0, keepdims=False)
        stack = jnp.stack([mine] + self.across(mine, "z"))
        own = [stack] + self.across(stack, "s")
        got = swap(jnp.stack(own), "c", 2, 1)
        return placed(self.where, own, [got[j] for j in range(4)])

    def total(self, x, axes):
        for axis in ("c", "s", "z"):
            if axis not in axes:
                continue
            if axis == "c":
                x = x + swap(x, "c", 2, 1)
            else:
                one, two, three = self.across(x, axis)
                x = (x + one) + (two + three)
        return x

    def scattered(self, x, axis, at):
        kept = lax.dynamic_index_in_dim(x, at, 0, keepdims=False).astype(F32)
        for by in (1, 2, 3):
            sent = lax.dynamic_index_in_dim(x, at ^ by, 0, keepdims=False)
            kept = kept + swap(sent, axis, 4, by).astype(F32)
        return kept.astype(BF16)

    def reduced(self, g):
        width = g.shape[-1]
        split = g.reshape(4, 4, 2, g.shape[1] // 8, width)
        kept = lax.dynamic_index_in_dim(split, self.c, 2, keepdims=False)
        sent = lax.dynamic_index_in_dim(split, 1 - self.c, 2, keepdims=False)
        x = (kept.astype(F32) + swap(sent, "c", 2, 1).astype(F32)).astype(BF16)
        x = self.scattered(x, "s", self.s)
        x = self.scattered(x, "z", self.z)
        one, two, three = self.across(x, "s")
        odd, high = self.s % 2 == 1, self.s >= 2
        pairs = [jnp.where(odd, b, a) for a, b in ((x, one), (one, x), (two, three), (three, two))]
        order = [jnp.where(high, pairs[i ^ 2], pairs[i]) for i in range(4)]
        return jnp.stack(order).astype(F32)


def layer_bundle(qkv, out, up, down_t, extra):
    pieces = []
    for j in range(4):
        first = qkv[:, D * j : D * (j + 1)] if j < 3 else out
        source = up if j < 2 else down_t
        second = source[:, HALF * (j % 2) : HALF * (j % 2 + 1)]
        row = [first, second] + ([extra[j]] if extra is not None else [])
        pieces.append(jnp.concatenate(row, axis=-1))
    return jnp.stack(pieces)


def per_device(sizes, *arrays):
    (tiles_in, truth_in, labels, var_ids, basis) = arrays[:5]
    masters, moments, averages = arrays[5:12], arrays[12:19], arrays[19:26]
    embed_w, qkv_w, out_w, up_w, down_w, ada_w, head_w = masters
    segments, dp = sizes["s"], sizes["z"] * 2
    micro, tokens = tiles_in.shape[0], tiles_in.shape[1]
    half = tokens // 2
    assert segments == 2 * micro
    rows = D // dp
    move = Squares(sizes) if segments == 4 and sizes["z"] == 4 else Plain(sizes)
    s, c = lax.axis_index("s"), lax.axis_index("c")

    emb_t = jnp.pad(embed_w.astype(BF16).T, ((0, 0), (0, ECOLS - EROWS)))
    down_t = down_w.astype(BF16).transpose(0, 2, 1)
    head_b = head_w.astype(BF16).reshape(rows, PIXELS // 2, 2)
    head_b = jnp.pad(head_b, ((0, 0), (0, 256 - PIXELS // 2), (0, 0)))
    head_b = [head_b[:, 128 * (j % 2) : 128 * (j % 2) + 128, j // 2] for j in range(4)]
    qkv_b, out_b, up_b = qkv_w.astype(BF16), out_w.astype(BF16), up_w.astype(BF16)
    bundles = [
        layer_bundle(qkv_b[l], out_b[l], up_b[l], down_t[l], head_b if l == 1 else None)
        for l in range(LAYERS)
    ]

    which = s % micro
    tiles = lax.dynamic_index_in_dim(tiles_in, which, 0, keepdims=False)
    truth = lax.dynamic_index_in_dim(truth_in, which, 0, keepdims=False)
    label = lax.dynamic_index_in_dim(labels, which, 0, keepdims=False)

    def seen_from(core):
        first = lax.dynamic_slice_in_dim(tiles, core * half, half)
        second = lax.dynamic_slice_in_dim(tiles, (1 - core) * half, half)
        third = lax.dynamic_slice_in_dim(truth, core * half, half)
        x = jnp.concatenate([first, second, third])
        x = jnp.pad(x, ((0, 0), (0, D - PIXELS)))
        lane = lax.broadcasted_iota(jnp.int32, x.shape, 1)
        return jnp.where(lane == LABEL_LANE, label.astype(BF16), x)

    pairs = []
    for a in range(segments):
        for b in range(sizes["z"]):
            base = (a * sizes["z"] + b) * 2
            pairs.append((base + a // micro, base + 1 - a // micro))
    sent = lax.ppermute(seen_from(1 - c), CHIP, pairs)
    data = jnp.where(c == s // micro, seen_from(c), sent)
    label = data[0, LABEL_LANE].astype(jnp.int32)

    emb = move.rows(emb_t)

    lead = embed_w[LEAD:].astype(BF16).astype(F32)
    ada = ada_w.astype(BF16).astype(F32)
    silu = jax.nn.silu(lead)
    mods = jnp.einsum("gd,ldm->lgm", silu, ada, precision=lax.Precision.HIGHEST)
    mods = jnp.pad(mods.reshape(LAYERS * GROUPS, 6 * D), ((0, 2), (0, 0)))
    mods = move.total(mods, ("z", "c"))

    def modulation(layer):
        row = lax.dynamic_index_in_dim(mods, layer * GROUPS + label, 0, keepdims=False)
        return jnp.pad(row.reshape(6, D), ((0, 2), (0, 0)))

    weights = [move.columns(b) for b in bundles]

    vid4 = jnp.pad(jnp.repeat(var_ids, 4), (0, D - PIXELS), constant_values=-1)[None].astype(
        jnp.int32
    )
    h0, agg = embed(data, emb, vid4, tokens)

    def forward(h, h_own, oth, oth_start, layer):
        mod = modulation(layer)
        normed, own = qkv_rows(h, 0, half, mod, weights[layer])
        _, other = qkv_rows(oth, oth_start, half, mod, weights[layer])
        out, *saved = block_forward(h, own, other, mod, weights[layer])
        return out, (mod, normed, own, other, saved)

    h1, kept0 = forward(h0, h0, h0, half, 0)
    h1_other = swap(h1, "c", 2, 1)
    h2, kept1 = forward(h1, h1, h1_other, 0, 1)

    forecasts = micro * dp
    by_column = basis.reshape(LONP, 2, 2 * LONP).transpose(1, 0, 2).reshape(2 * LONP, 2 * LONP)
    d_h2, g_head, loss = head(h2, data, weights[1], by_column.T, by_column, 1.0 / forecasts, tokens)

    def backward(d_out, h, kept, layer):
        mod, normed, own, other, saved = kept
        d_mid, d_att, g_ff, g_out, dmod = mlp_back(d_out, saved, mod, weights[layer])
        d_q, d_k, d_v = attention_back(own, other, saved[1], d_att)
        got = swap(jnp.stack([d_k[half:], d_v[half:]]), "c", 2, 1)
        d_h, g_att, dmod_one = qkv_back(
            d_q, d_k, d_v, got, normed, h, d_mid, g_out, mod, weights[layer]
        )
        return d_h, g_ff, g_att, (dmod + dmod_one)[:6].reshape(6 * D)

    d_h1, g_ff1, g_att1, dmod1 = backward(d_h2, h1, kept1, 1)
    got_ff1 = move.reduced(jnp.concatenate([g_ff1, g_head], axis=-1))
    got_att1 = move.reduced(g_att1)
    d_h0, g_ff0, g_att0, dmod0 = backward(d_h1, h0, kept0, 0)
    got_ff0 = move.reduced(g_ff0)
    g_emb = embed_back(d_h0, data, agg, emb, vid4)
    got_att0 = move.reduced(jnp.concatenate([g_att0, g_emb], axis=-1))

    hot = (jnp.arange(GROUPS) == label).astype(F32)[:, None]
    sums = jnp.concatenate([hot * dmod0[None], hot * dmod1[None]])
    sums = jnp.concatenate([sums, jnp.broadcast_to(loss[:1, :1], (2, 6 * D))])
    sums = move.total(sums, ("s", "z", "c"))
    loss_value = sums[LAYERS * GROUPS, 0]
    by_lead = sums[: LAYERS * GROUPS].reshape(LAYERS, GROUPS, 6 * D)
    highest = lax.Precision.HIGHEST
    g_ada = jnp.einsum("gd,lgm->ldm", silu, by_lead, precision=highest)
    d_silu = jnp.einsum("ldm,lgm->gd", ada, by_lead, precision=highest)
    gate = jax.nn.sigmoid(lead)
    g_lead = d_silu * (gate * (1.0 + lead * (1.0 - gate)))

    ff = [got_ff0[..., :HALF], got_ff1[..., :HALF]]
    att = [got_att0[..., :D], got_att1]
    spread = lambda x: x.transpose(1, 0, 2).reshape(rows, -1)
    g_qkv = jnp.stack([spread(x[:3]) for x in att])
    g_out = jnp.stack([x[3] for x in att])
    g_up = jnp.stack([spread(x[:2]) for x in ff])
    g_down = jnp.stack([spread(x[2:]).T for x in ff])
    g_embed = spread(got_att0[..., D:]).T[:EROWS]
    g_embed = jnp.concatenate([g_embed[:LEAD], g_lead])
    g_hw = got_ff1[..., HALF:].reshape(2, 2, rows, 128).transpose(2, 1, 3, 0)
    g_hw = g_hw.reshape(rows, 256, 2)[:, : PIXELS // 2].reshape(rows, PIXELS)
    grads = (g_embed, g_qkv, g_out, g_up, g_down, g_ada, g_hw)

    squares = sum(jnp.sum(g * g) for g in grads)
    squares = move.total(jnp.full((8, 128), squares, F32), ("z", "c"))[0, 0]
    norm = jnp.sqrt(squares)
    factor = CLIP / jnp.maximum(norm, CLIP)
    count = sum(w.size for w in masters) * dp
    rate = 0.02 * math.sqrt(count) / CLIP
    new_w, new_m, new_a = [], [], []
    for i, (w, m, a, g) in enumerate(zip(masters, moments, averages, grads)):
        g = g * factor
        m = KEEP * m + g
        w = w - rate * (BOOST if i == 0 else 1.0) * (g + KEEP * m)
        new_w.append(w)
        new_m.append(m)
        new_a.append(KEEP * a + (1.0 - KEEP) * w)
    return (loss_value, norm, *new_w, *new_m, *new_a)


def solution(mesh):
    segments, dp = mesh.shape["segment"], mesh.shape["dp"]
    sizes = {"s": segments, "z": dp // 2, "c": 2}
    split = Mesh(mesh.devices.reshape(segments, dp // 2, 2), CHIP)
    d = ("z", "c")
    weights = (
        P(None, d),
        P(None, d, None),
        P(None, d, None),
        P(None, d, None),
        P(None, None, d),
        P(None, d, None),
        P(d, None),
    )
    return jax.shard_map(
        lambda *arrays: per_device(sizes, *arrays),
        mesh=split,
        in_specs=(P(d, None, None), P(d, None, None), P(d), P(), P()) + weights * 3,
        out_specs=(P(), P()) + weights * 3,
        check_vma=False,
    )
```

```python
import math

import jax
import jax.numpy as jnp
from jax import lax
from jax.experimental import pallas as pl
from jax.experimental.pallas import tpu as pltpu
from jax.sharding import Mesh, PartitionSpec as P

D = 384
HEADS = 6
HEAD_DIM = 64
FF = 1536
VARS = 69
CHANNELS = 69
LONP = 128
LATP = 8
LAYERS = 2
GROUPS = 3
PIXELS = 276
LEAD = PIXELS + VARS + 1
EROWS = LEAD + GROUPS
ECOLS = 512
EPS = 1e-06
CLIP = 0.001
KEEP = 0.9
BOOST = 20.0
LABEL_LANE = D - 1
HALF = FF // 2

F32 = jnp.float32
BF16 = jnp.bfloat16
CHIP = ("s", "z", "c")


def dot(a, b):
    return jnp.dot(a, b, preferred_element_type=F32)


def dot_nt(a, b):
    return lax.dot_general(a, b, (((1,), (1,)), ((), ())), preferred_element_type=F32)


def dot_tn(a, b):
    return lax.dot_general(a, b, (((0,), (0,)), ((), ())), preferred_element_type=F32)


def parts(x, count):
    out = []
    for step in range(count):
        piece = x.astype(BF16)
        out.append(piece)
        if step < count - 1:
            x = x - piece.astype(F32)
    return out


def normal(v):
    centered = v - jnp.mean(v, axis=-1, keepdims=True)
    inverse = lax.rsqrt(jnp.mean(centered * centered, axis=-1, keepdims=True) + EPS)
    return centered * inverse, inverse


def normal_back(d_x, x, inverse):
    return inverse * (
        d_x - jnp.mean(d_x, axis=-1, keepdims=True) - x * jnp.mean(d_x * x, axis=-1, keepdims=True)
    )


def lane_below(limit, shape):
    return lax.broadcasted_iota(jnp.int32, shape, len(shape) - 1) < limit


def same_group():
    row = lax.broadcasted_iota(jnp.int32, (D, D), 0)
    col = lax.broadcasted_iota(jnp.int32, (D, D), 1)
    return (row // 4 == col // 4).astype(BF16)


def chosen_table(vid_ref):
    row = lax.broadcasted_iota(jnp.int32, (ECOLS, D), 0)
    return (row - PIXELS == vid_ref[...]).astype(BF16)


def first_of_four(shape):
    lane = lax.broadcasted_iota(jnp.int32, shape, len(shape) - 1)
    return lane % 4 == 0

def cost(flops, size, exps=0):
    return pl.CostEstimate(flops=int(flops), bytes_accessed=int(size), transcendentals=int(exps))


VMEM = pl.BlockSpec(memory_space=pltpu.VMEM)
SMEM = pl.BlockSpec(memory_space=pltpu.SMEM)
ANY = pl.BlockSpec(memory_space=pl.ANY)


def call(kernel, name, outs, inputs, estimate, scratch=(), limit=24, spaces=None, out_space=VMEM):
    return pl.pallas_call(
        kernel,
        in_specs=[SMEM] + (spaces or [VMEM] * (len(inputs) - 1)),
        out_specs=[out_space] * len(outs),
        out_shape=[jax.ShapeDtypeStruct(shape, kind) for shape, kind in outs],
        scratch_shapes=list(scratch),
        compiler_params=pltpu.CompilerParams(vmem_limit_bytes=limit << 20),
        cost_estimate=estimate,
        name=name,
    )(*inputs)


def rows_at(index, size):
    return pl.ds(pl.multiple_of(index * size, size), size)


CHUNK = 256
AT_S, AT_Z, AT_C, AT_WHICH, AT_OWN = range(5)


def embed_kernel(
    at_ref, tiles_ref, got_ref, emb_ref, vid_ref, out_ref, agg_ref, x_ref, wide_sc
):
    tokens = got_ref.shape[0]
    emb = emb_ref[...].astype(F32)
    row = jnp.sum(emb * emb[:, LEAD - 1 : LEAD], axis=0, keepdims=True)
    proj = jnp.where(lane_below(PIXELS, (1, D)), row[:, :D], 0.0)
    table = chosen_table(vid_ref)
    base = sum(dot(p, table) for p in parts(jnp.broadcast_to(row, (8, ECOLS)), 3))[:1]
    bases = dot(emb_ref[...], table)
    bases = jnp.where(first_of_four((D, D)), bases, 0.0).astype(BF16)
    group = same_group()
    wide_sc[...] = jnp.zeros_like(wide_sc)
    mine = at_ref[AT_OWN] == 1

    def step(i, carry):
        source = lax.rem(i * CHUNK + at_ref[AT_C] * (tokens // 2), tokens)
        source = pl.ds(pl.multiple_of(source, CHUNK), CHUNK)
        here = rows_at(i, CHUNK)
        own = tiles_ref[at_ref[AT_WHICH], source, :]
        wide_sc[:, :PIXELS] = jnp.where(mine, own, got_ref[source, :])
        x = wide_sc[...].astype(F32)
        scores = sum(dot(p, group) for p in parts(x * proj, 3)) + base
        scores = jnp.where(lane_below(PIXELS, scores.shape), scores * D ** (-0.5), -1e30)
        e = jnp.exp(scores - jnp.max(scores, axis=-1, keepdims=True))
        agg = e / (0.25 * jnp.sum(e, axis=-1, keepdims=True))

        @pl.when(i < tokens // 2 // CHUNK)
        def _():
            agg_ref[here, :] = agg
            x_ref[here, :] = wide_sc[...]

        total = dot_nt((agg * x).astype(BF16), emb_ref[:, :D])
        for p in parts(agg, 2):
            total = total + dot_nt(p, bases)
        out_ref[here, :] = total.astype(BF16)
        return carry

    lax.fori_loop(0, tokens // CHUNK, step, 0)


def embed(at, tiles, got, emb, vid4):
    tokens = got.shape[0]
    return call(
        embed_kernel,
        "embed",
        [((tokens, D), BF16), ((tokens // 2, D), F32), ((tokens // 2, D), BF16)],
        [at, tiles, got, emb, vid4],
        cost(6e9, 4e6, 4e5),
        [pltpu.VMEM((CHUNK, D), BF16)],
    )


def embed_back_kernel(at_ref, dh_ref, x_ref, agg_ref, emb_ref, vid_ref, *outs, cut):
    dh = dh_ref[...]
    x = x_ref[...].astype(F32)
    agg = agg_ref[...]
    emb = emb_ref[...]
    table = chosen_table(vid_ref)
    group = same_group()
    bases = dot(emb, table).astype(BF16)
    query = emb[:, LEAD - 1 : LEAD].astype(F32)
    spread = (agg * x).astype(BF16)
    g_patch = dot_tn(dh, spread)
    d_spread = dot(dh, emb[:, :D])
    d_agg = dot(dh, bases)
    for p in parts(d_spread * x, 2):
        d_agg = d_agg + dot(p, group)
    inner = 0.25 * jnp.sum(agg * d_agg, axis=-1, keepdims=True)
    d_scores = agg * (d_agg - inner) * D ** (-0.5)
    d_proj = jnp.sum(d_scores * x, axis=0, keepdims=True)
    d_base = jnp.sum(d_scores, axis=0, keepdims=True)
    d_base = jnp.where(first_of_four(d_base.shape), d_base, 0.0)
    d_bases = query * d_base
    for p in parts(jnp.where(first_of_four(agg.shape), agg, 0.0), 2):
        d_bases = d_bases + dot_tn(dh, p)
    g_table = sum(dot_nt(p, table) for p in parts(d_bases, 2))
    d_query = jnp.sum(
        emb[:, :D].astype(F32) * d_proj + bases.astype(F32) * d_base, axis=-1, keepdims=True
    )
    lane = lax.broadcasted_iota(jnp.int32, (D, ECOLS), 1)
    total = g_table + jnp.where(lane == LEAD - 1, d_query, 0.0)
    first = total[:, :D] + g_patch + query * d_proj
    for j in range(3):
        cut.write(at_ref, outs, j, 0, first[:, 128 * j : 128 * j + 128])
    cut.write(at_ref, outs, 3, 0, total[:, D:])


def embed_back(at, cut, dh, x, agg, emb, vid4):
    return call(
        lambda *refs: embed_back_kernel(*refs[: 6 + cut.outputs], cut=cut.on(refs[6 + cut.outputs :])),
        "embed_back",
        cut.shapes(128),
        [at, dh, x, agg, emb, vid4],
        cost(3e9, 4e6),
        cut.scratch(128),
    )


class Cut:
    def __init__(self, pairs, rows, split):
        self.pairs, self.rows, self.split = pairs, rows, split
        self.outputs = 2 if split else 1
        self.buffer = None

    def shapes(self, width):
        if self.split:
            return [((4 * self.pairs, self.rows, width), BF16)] * 2
        return [((4, D, width), BF16)]

    def scratch(self, width):
        return [pltpu.VMEM((D, width), F32)] if self.split else []

    def on(self, scratch):
        other = Cut(self.pairs, self.rows, self.split)
        other.buffer = scratch[0] if self.split else None
        return other

    def write(self, at_ref, outs, quarter, lane, value):
        width = value.shape[-1]
        cols = slice(lane, lane + width)
        if not self.split:
            outs[0][quarter, :, cols] = value.astype(BF16)
            return
        self.buffer[:, :width] = value
        core = at_ref[AT_C]
        for z in range(self.pairs):
            for ref, which in ((outs[0], core), (outs[1], 1 - core)):
                part = self.buffer[rows_at(2 * z + which, self.rows), :width]
                ref[quarter * self.pairs + z, :, cols] = part.astype(BF16)


def qkv_kernel(at_ref, h_ref, mod_ref, w_ref, normed_ref, qkv_ref, *, start):
    def step(i, carry):
        here = rows_at(i, CHUNK)
        x, _ = normal(h_ref[pl.ds(pl.multiple_of(start + i * CHUNK, CHUNK), CHUNK), :].astype(F32))
        normed = (x * (1.0 + mod_ref[1:2]) + mod_ref[0:1]).astype(BF16)
        normed_ref[here, :] = normed
        for j in range(3):
            qkv_ref[here, D * j : D * (j + 1)] = dot(normed, w_ref[j, :, :D]).astype(BF16)
        return carry

    lax.fori_loop(0, qkv_ref.shape[0] // CHUNK, step, 0)


def qkv_rows(at, h, start, count, mod, weights):
    return call(
        lambda *refs: qkv_kernel(*refs, start=start),
        "qkv_rows",
        [((count, D), BF16), ((count, 3 * D), BF16)],
        [at, h, mod, weights],
        cost(2 * count * D * 3 * D, 3e6),
    )


def pair_masks():
    low = lane_below(HEAD_DIM, (1, 128))
    return low, jnp.logical_not(low)


def both(own_ref, other_ref, lane):
    here = slice(lane, lane + 128)
    return jnp.concatenate([own_ref[:, here], other_ref[:, here]])


def gelu_and_slope(u):
    k = math.sqrt(2.0 / math.pi)
    t = jnp.tanh(k * (u + 0.044715 * (u * u * u)))
    cdf = 0.5 * (1.0 + t)
    return u * cdf, cdf + 0.5 * u * (1.0 - t * t) * k * (1.0 + 3 * 0.044715 * (u * u))


def block_kernel(
    at_ref, h_ref, own_ref, other_ref, mod_ref, w_ref,
    out_ref, att_ref, mix_ref, lse_ref, one_ref, mid_ref, n2_ref, slope_ref, act_ref, two_ref,
):
    zero = jnp.zeros((), BF16)
    lane = lax.broadcasted_iota(jnp.int32, (CHUNK, 128), 1)

    def step(i, carry):
        here = rows_at(i, CHUNK)
        sums = jnp.zeros((CHUNK, 128), F32)
        for pair in range(HEADS // 2):
            a = 128 * pair
            q = own_ref[here, a : a + 128] * 0.125
            keys = both(own_ref, other_ref, D + a)
            vals = both(own_ref, other_ref, 2 * D + a)
            mixed = jnp.zeros((CHUNK, 128), F32)
            for which, mask in enumerate(pair_masks()):
                scores = dot_nt(q, jnp.where(mask, keys, zero))
                top = jnp.max(scores, axis=-1, keepdims=True)
                e = jnp.exp(scores - top)
                total = jnp.sum(e, axis=-1, keepdims=True)
                mixed = mixed + dot(e.astype(BF16), jnp.where(mask, vals, zero)) * (1.0 / total)
                sums = jnp.where(lane == 2 * pair + which, top + jnp.log(total), sums)
            mix_ref[here, a : a + 128] = mixed
            att_ref[here, a : a + 128] = mixed.astype(BF16)
        lse_ref[here, :] = sums
        one = dot(att_ref[here, :], w_ref[3, :, :D])
        one_ref[here, :] = one
        middle = h_ref[here, :].astype(F32) + mod_ref[2:3] * one
        mid_ref[here, :] = middle
        x, _ = normal(middle)
        n2 = (x * (1.0 + mod_ref[4:5]) + mod_ref[3:4]).astype(BF16)
        n2_ref[here, :] = n2
        two = jnp.zeros((CHUNK, D), F32)
        for j in range(2):
            part = slice(HALF * j, HALF * (j + 1))
            act, slope = gelu_and_slope(dot(n2, w_ref[j, :, D : 3 * D]))
            slope_ref[here, part] = slope
            act = act.astype(BF16)
            act_ref[here, part] = act
            two = two + dot_nt(act, w_ref[2 + j, :, D : 3 * D])
        two_ref[here, :] = two
        out_ref[here, :] = (middle + mod_ref[5:6] * two).astype(BF16)
        return carry

    lax.fori_loop(0, out_ref.shape[0] // CHUNK, step, 0)


def block_forward(at, h, own, other, mod, weights):
    count = own.shape[0]
    wide = [(D, BF16), (D, BF16), (D, F32), (128, F32), (D, F32), (D, F32), (D, BF16)]
    wide += [(FF, F32), (FF, BF16), (D, F32)]
    return call(
        block_kernel,
        "block_forward",
        [((count, width), kind) for width, kind in wide],
        [at, h, own, other, mod, weights],
        cost(8e9, 1.2e7, 3e6),
    )


def head_kernel(
    at_ref, h_ref, truth_ref, got_ref, w_ref, fwd_ref, back_ref,
    dh_ref, loss_ref, *outs, seed, cut,
):
    count = h_ref.shape[0]
    x, inverse = normal(h_ref[...].astype(F32))
    flat = x.astype(BF16)
    hw = [w_ref[j, :, 3 * D : 3 * D + 128] for j in range(4)]
    pred = [dot(flat, w) for w in hw]
    pred = [jnp.concatenate(pred[:2], axis=-1), jnp.concatenate(pred[2:], axis=-1)]
    row = lax.broadcasted_iota(jnp.int32, (PIXELS, 256), 0)
    col = lax.broadcasted_iota(jnp.int32, (PIXELS, 256), 1)
    here = rows_at(at_ref[AT_C], count)
    mine = at_ref[AT_OWN] == 1
    truth = jnp.where(mine, truth_ref[at_ref[AT_WHICH], here, :], got_ref[here, :])
    true = [dot(truth, (row == 2 * col + b).astype(BF16)).astype(BF16) for b in range(2)]
    fwd = parts(fwd_ref[...], 2)
    back = parts(back_ref[...], 2)
    entries = LATP * CHANNELS * 2 * LONP
    loss = jnp.zeros((1, 1), F32)
    grads = [[], []]
    for p in range(count // LONP):
        part = slice(p * LONP, (p + 1) * LONP)
        seen = parts(jnp.concatenate([pred[0][part], pred[1][part]], axis=0), 2)
        waves = dot(fwd[0], seen[0]) + (dot(fwd[0], seen[1]) + dot(fwd[1], seen[0]))
        want = jnp.concatenate([true[0][part], true[1][part]], axis=0)
        target = dot(fwd[0], want) + dot(fwd[1], want)
        top, low = waves[:LONP], waves[LONP:]
        gap = (top * top + low * low) - (
            target[:LONP] * target[:LONP] + target[LONP:] * target[LONP:]
        )
        loss = loss + jnp.sum(gap * gap, axis=(0, 1), keepdims=True)
        scaled = gap * (4.0 * seed / entries)
        d_waves = parts(jnp.concatenate([scaled * top, scaled * low], axis=0), 2)
        d_seen = dot(back[0], d_waves[0]) + (dot(back[0], d_waves[1]) + dot(back[1], d_waves[0]))
        d_seen = d_seen.astype(BF16)
        grads[0].append(d_seen[:LONP])
        grads[1].append(d_seen[LONP:])
    loss_ref[...] = jnp.broadcast_to(loss * (seed / entries), loss_ref.shape)
    d_flat = jnp.zeros((count, D), F32)
    for b in range(2):
        whole = jnp.concatenate(grads[b], axis=0)
        for j in range(2):
            piece = whole[:, 128 * j : 128 * (j + 1)]
            d_flat = d_flat + dot_nt(piece, hw[2 * b + j])
            cut.write(at_ref, outs, 2 * b + j, 0, dot_tn(flat, piece))
    dh_ref[...] = normal_back(d_flat, x, inverse).astype(BF16)


def head(at, cut, h, truth, got, weights, basis_fwd, basis_back, seed):
    count = h.shape[0]
    n = 9 + cut.outputs
    return call(
        lambda *refs: head_kernel(*refs[:n], seed=seed, cut=cut.on(refs[n:])),
        "head",
        [((count, D), BF16), ((8, 128), F32)] + cut.shapes(128),
        [at, h, truth, got, weights, basis_fwd, basis_back],
        cost(3e9, 3e6),
        cut.scratch(128),
    )


def column_sum(v):
    return jnp.sum(v, axis=0, keepdims=True)


def mlp_back_kernel(
    at_ref, dout_ref, two_ref, act_ref, slope_ref, n2_ref, mid_ref, one_ref, att_ref, mod_ref, w_ref,
    dmid_ref, datt_ref, gout_ref, dmod_ref, *outs, cut,
):
    d_out = dout_ref[...].astype(F32)
    d_two = (mod_ref[5:6] * d_out).astype(BF16)
    g_gate_two = column_sum(d_out * two_ref[...])
    d_n2 = jnp.zeros(d_out.shape, F32)
    n2 = n2_ref[...]
    for j in range(2):
        part = slice(HALF * j, HALF * (j + 1))
        d_units = (slope_ref[:, part] * dot(d_two, w_ref[2 + j, :, D : 3 * D])).astype(BF16)
        d_n2 = d_n2 + dot_nt(d_units, w_ref[j, :, D : 3 * D])
        cut.write(at_ref, outs, j, 0, dot_tn(n2, d_units))
        cut.write(at_ref, outs, 2 + j, 0, dot_tn(d_two, act_ref[:, part]))
    x, inverse = normal(mid_ref[...])
    g_shift = column_sum(d_n2)
    g_scale = column_sum(d_n2 * x)
    d_mid = d_out + normal_back(d_n2 * (1.0 + mod_ref[4:5]), x, inverse)
    dmid_ref[...] = d_mid
    d_one = (mod_ref[2:3] * d_mid).astype(BF16)
    g_gate_one = column_sum(d_mid * one_ref[...])
    gout_ref[...] = dot_tn(att_ref[...], d_one)
    datt_ref[...] = dot_nt(d_one, w_ref[3, :, :D]).astype(BF16)
    blank = jnp.zeros((2, D), F32)
    dmod_ref[...] = jnp.concatenate(
        [blank, g_gate_one, g_shift, g_scale, g_gate_two, blank], axis=0
    )


def mlp_back(at, cut, d_out, saved, mod, weights):
    attended, mixed, lse, one, middle, n2, slope, act, two = saved
    count = d_out.shape[0]
    n = 15 + cut.outputs
    return call(
        lambda *refs: mlp_back_kernel(*refs[:n], cut=cut.on(refs[n:])),
        "mlp_back",
        [((count, D), F32), ((count, D), BF16), ((D, D), F32), ((8, D), F32)] + cut.shapes(HALF),
        [at, d_out, two, act, slope, n2, middle, one, attended, mod, weights],
        cost(6e9, 1.6e7),
        cut.scratch(HALF),
    )


def attention_back_kernel(
    at_ref, own_ref, other_ref, lse_ref, mix_ref, datt_ref, dq_ref, dk_ref, dv_ref, send_ref,
    dk_sc, dv_sc,
):
    zero = jnp.zeros((), BF16)
    count = own_ref.shape[0]
    dk_sc[...] = jnp.zeros_like(dk_sc)
    dv_sc[...] = jnp.zeros_like(dv_sc)

    def step(i, carry):
        rows = rows_at(i, CHUNK)
        for pair in range(HEADS // 2):
            a = 128 * pair
            here = slice(a, a + 128)
            q = own_ref[rows, here]
            d_att = datt_ref[rows, here]
            keys = both(own_ref, other_ref, D + a)
            vals = both(own_ref, other_ref, 2 * D + a)
            dots = d_att.astype(F32) * mix_ref[rows, here]
            d_q = jnp.zeros((CHUNK, 128), F32)
            d_k = jnp.zeros((keys.shape[0], 128), F32)
            d_v = jnp.zeros((keys.shape[0], 128), F32)
            for which, mask in enumerate(pair_masks()):
                head = 2 * pair + which
                k = jnp.where(mask, keys, zero)
                v = jnp.where(mask, vals, zero)
                inner = jnp.sum(jnp.where(mask, dots, 0.0), axis=-1, keepdims=True)
                probs = jnp.exp(dot_nt(q * 0.125, k) - lse_ref[rows, head : head + 1])
                d_scores = (probs * (dot_nt(d_att, v) - inner)).astype(BF16)
                d_q = d_q + dot(d_scores, k)
                d_k = d_k + dot_tn(d_scores, jnp.where(mask, q, zero))
                d_v = d_v + dot_tn(probs.astype(BF16), jnp.where(mask, d_att, zero))
            dq_ref[rows, here] = (d_q * 0.125).astype(BF16)
            dk_sc[:, here] += d_k * 0.125
            dv_sc[:, here] += d_v
        return carry

    lax.fori_loop(0, count // CHUNK, step, 0)
    dk_ref[...] = dk_sc[:count]
    dv_ref[...] = dv_sc[:count]
    send_ref[0] = dk_sc[count:].astype(BF16)
    send_ref[1] = dv_sc[count:].astype(BF16)


def attention_back(at, own, other, lse, mixed, d_att):
    count = own.shape[0]
    return call(
        attention_back_kernel,
        "attention_back",
        [((count, D), BF16), ((count, D), F32), ((count, D), F32), ((2, count, D), BF16)],
        [at, own, other, lse, mixed, d_att],
        cost(8e9, 8e6, 3e6),
        [pltpu.VMEM((2 * count, D), F32)] * 2,
    )


def qkv_back_kernel(
    at_ref, dq_ref, dk_ref, dv_ref, got_ref, normed_ref, h_ref, dmid_ref, gout_ref, mod_ref, w_ref,
    dh_ref, dmod_ref, *outs, cut,
):
    count = dq_ref.shape[0]
    normed = normed_ref[...]
    d_k = (dk_ref[...] + got_ref[0].astype(F32)).astype(BF16)
    d_v = (dv_ref[...] + got_ref[1].astype(F32)).astype(BF16)
    d_n = jnp.zeros(normed.shape, F32)
    for j, piece in enumerate((dq_ref[...], d_k, d_v)):
        d_n = d_n + dot_nt(piece, w_ref[j, :, :D])
        cut.write(at_ref, outs, j, 0, dot_tn(normed, piece))
    cut.write(at_ref, outs, 3, 0, gout_ref[...])
    x, inverse = normal(h_ref[:count].astype(F32))
    g_shift = column_sum(d_n)
    g_scale = column_sum(d_n * x)
    dh_ref[...] = (
        dmid_ref[...] + normal_back(d_n * (1.0 + mod_ref[1:2]), x, inverse)
    ).astype(BF16)
    dmod_ref[...] = jnp.concatenate([g_shift, g_scale, jnp.zeros((6, D), F32)], axis=0)


def qkv_back(at, cut, d_q, d_k, d_v, got, normed, h, d_mid, g_out, mod, weights):
    count = d_q.shape[0]
    n = 13 + cut.outputs
    return call(
        lambda *refs: qkv_back_kernel(*refs[:n], cut=cut.on(refs[n:])),
        "qkv_back",
        [((count, D), BF16), ((8, D), F32)] + cut.shapes(D),
        [at, d_q, d_k, d_v, got, normed, h, d_mid, g_out, mod, weights],
        cost(2e9, 8e6),
        cut.scratch(D),
    )


def swap(x, axis, size, by):
    return lax.ppermute(x, axis, [(i, i ^ by) for i in range(size)])


def place_kernel(at_ref, *refs, columns, rows):
    out_ref, sems = refs[-2], refs[-1]
    inputs = refs[:-2]
    s, z, c = at_ref[AT_S], at_ref[AT_Z], at_ref[AT_C]
    copies = []
    index = 0
    for jc in range(2):
        for js in range(columns):
            source = inputs[jc * columns + js]
            for jz in range(source.shape[0]):
                at = rows_at((z ^ jz) * 2 + (c ^ jc), rows)
                target = out_ref.at[s ^ js, at] if columns > 1 else out_ref.at[at]
                copies.append(pltpu.make_async_copy(source.at[jz], target, sems.at[index]))
                index += 1
    for copy in copies:
        copy.start()
    for copy in copies:
        copy.wait()


def placed(at, own, got):
    columns, (zs, rows, width) = len(own), own[0].shape
    full = (zs * 2 * rows, width)
    shape = (columns,) + full if columns > 1 else full
    return call(
        lambda *refs: place_kernel(*refs, columns=columns, rows=rows),
        "placed",
        [(shape, BF16)],
        [at, *own, *got],
        cost(0, 4 * math.prod(shape)),
        [pltpu.SemaphoreType.DMA((2 * columns * zs,))],
        limit=4,
        spaces=[ANY] * (2 * columns),
    )[0]


def add_core_kernel(at_ref, kept_ref, got_ref, own_ref, *sends):
    zs = own_ref.shape[0]
    for j in range(4):
        here = pl.ds((at_ref[AT_S] ^ j) * zs, zs)
        value = kept_ref[here].astype(F32) + got_ref[here].astype(F32)
        if j == 0:
            own_ref[...] = value
        else:
            sends[j - 1][...] = value.astype(BF16)


def add_segment_kernel(at_ref, own_ref, a_ref, b_ref, c_ref, kept_ref, *sends):
    total = own_ref[...] + a_ref[...].astype(F32) + b_ref[...].astype(F32) + c_ref[...].astype(F32)
    own_ref_shape = total.shape
    del own_ref_shape
    for z in range(4):
        for j in range(4):

            @pl.when((at_ref[AT_Z] ^ j) == z)
            def _(z=z, j=j):
                if j == 0:
                    kept_ref[...] = total[z]
                else:
                    sends[j - 1][...] = total[z].astype(BF16)


def add_plane_kernel(at_ref, own_ref, a_ref, b_ref, c_ref, out_ref):
    total = own_ref[...] + a_ref[...].astype(F32) + b_ref[...].astype(F32) + c_ref[...].astype(F32)
    out_ref[...] = total.astype(BF16)


class Plain:
    split = False

    def __init__(self, sizes, at):
        self.sizes, self.at = sizes, at

    def rows(self, x):
        return lax.all_gather(x, ("z", "c"), axis=0, tiled=True)

    def columns(self, x):
        return lax.all_gather(x, ("z", "c"), axis=1, tiled=True)

    def total(self, x, axes):
        return lax.psum(x, axes)

    def reduced(self, g):
        own = lax.psum_scatter(g.astype(F32), ("z", "c"), scatter_dimension=1, tiled=True)
        return lax.psum(own, "s")


class Squares(Plain):
    split = True

    def across(self, x, axis):
        return [swap(x, axis, 4, by) for by in (1, 2, 3)]

    def rows(self, x):
        own = jnp.stack([x] + self.across(x, "z"))
        return placed(self.at, [own], [swap(own, "c", 2, 1)])

    def columns(self, x):
        mine = lax.dynamic_index_in_dim(x, self.at[AT_S], 0, keepdims=False)
        stack = jnp.stack([mine] + self.across(mine, "z"))
        own = [stack] + self.across(stack, "s")
        return placed(self.at, own, [swap(x, "c", 2, 1) for x in own])

    def total(self, x, axes):
        for axis in ("c", "s", "z"):
            if axis not in axes:
                continue
            if axis == "c":
                x = x + swap(x, "c", 2, 1)
            else:
                one, two, three = self.across(x, axis)
                x = (x + one) + (two + three)
        return x

    def reduced(self, kept, sent):
        count, rows, width = kept.shape
        zs = count // 4
        full, one = (zs, rows, width), (rows, width)
        got = swap(sent, "c", 2, 1)
        own, *sends = call(
            add_core_kernel, "add_core", [(full, F32)] + [(full, BF16)] * 3,
            [self.at, kept, got], cost(0, 8 * math.prod(kept.shape)),
        )
        got = [swap(x, "s", 4, j + 1) for j, x in enumerate(sends)]
        own, *sends = call(
            add_segment_kernel, "add_segment", [(one, F32)] + [(one, BF16)] * 3,
            [self.at, own, *got], cost(0, 12 * math.prod(full)),
        )
        got = [swap(x, "z", 4, j + 1) for j, x in enumerate(sends)]
        (x,) = call(
            add_plane_kernel, "add_plane", [(one, BF16)],
            [self.at, own, *got], cost(0, 12 * math.prod(one)),
        )
        one, two, three = self.across(x, "s")
        s = self.at[AT_S]
        odd, high = s % 2 == 1, s >= 2
        pairs = [jnp.where(odd, b, a) for a, b in ((x, one), (one, x), (two, three), (three, two))]
        order = [jnp.where(high, pairs[i ^ 2], pairs[i]) for i in range(4)]
        return jnp.stack(order).astype(F32)


def layer_bundle(qkv, out, up, down_t, extra):
    pieces = []
    for j in range(4):
        first = qkv[:, D * j : D * (j + 1)] if j < 3 else out
        source = up if j < 2 else down_t
        second = source[:, HALF * (j % 2) : HALF * (j % 2 + 1)]
        row = [first, second] + ([extra[j]] if extra is not None else [])
        pieces.append(jnp.concatenate(row, axis=-1))
    return jnp.stack(pieces)


def per_device(sizes, *arrays):
    (tiles_in, truth_in, labels, var_ids, basis) = arrays[:5]
    masters, moments, averages = arrays[5:12], arrays[12:19], arrays[19:26]
    embed_w, qkv_w, out_w, up_w, down_w, ada_w, head_w = masters
    segments, dp = sizes["s"], sizes["z"] * 2
    micro, tokens = tiles_in.shape[0], tiles_in.shape[1]
    half = tokens // 2
    assert segments == 2 * micro
    rows = D // dp
    s, z, c = (lax.axis_index(name) for name in CHIP)
    which, owner = s % micro, s // micro
    is_owner = c == owner
    at = jnp.stack([s, z, c, which, is_owner]).astype(jnp.int32)
    move = (Squares if segments == 4 and sizes["z"] == 4 else Plain)(sizes, at)
    cut = Cut(sizes["z"], rows, move.split)

    pairs = []
    for a in range(segments):
        for b in range(sizes["z"]):
            base = (a * sizes["z"] + b) * 2
            pairs.append((base + a // micro, base + 1 - a // micro))
    label = lax.dynamic_index_in_dim(labels, which, 0, keepdims=False)
    label = jnp.broadcast_to(label, (8, 128)).astype(jnp.int32)
    label = jnp.where(is_owner, label, lax.ppermute(label, CHIP, pairs))[0, 0]
    pick = lambda x: lax.dynamic_index_in_dim(x, which, 0, keepdims=False)
    tiles_got = lax.ppermute(pick(tiles_in), CHIP, pairs)
    truth_got = lax.ppermute(pick(truth_in), CHIP, pairs)

    emb_t = jnp.pad(embed_w.astype(BF16).T, ((0, 0), (0, ECOLS - EROWS)))
    down_t = down_w.astype(BF16).transpose(0, 2, 1)
    wide = jnp.arange(512)
    source = 2 * (wide % 256) + wide // 256
    to_head = (jnp.arange(PIXELS)[:, None] == source[None]) & (wide % 256 < PIXELS // 2)[None]
    to_head = to_head.astype(BF16)
    head_b = dot(head_w.astype(BF16), to_head).astype(BF16)
    head_b = [head_b[:, 128 * j : 128 * j + 128] for j in range(4)]
    qkv_b, out_b, up_b = qkv_w.astype(BF16), out_w.astype(BF16), up_w.astype(BF16)
    bundles = [
        layer_bundle(qkv_b[l], out_b[l], up_b[l], down_t[l], head_b if l == 1 else None)
        for l in range(LAYERS)
    ]

    emb = move.rows(emb_t)

    lead = embed_w[LEAD:].astype(BF16).astype(F32)
    ada = ada_w.astype(BF16).astype(F32)
    silu = jax.nn.silu(lead)
    mods = jnp.einsum("gd,ldm->lgm", silu, ada, precision=lax.Precision.HIGHEST)
    mods = jnp.pad(mods.reshape(LAYERS * GROUPS, 6 * D), ((0, 2), (0, 0)))
    mods = move.total(mods, ("z", "c"))

    def modulation(layer):
        row = lax.dynamic_index_in_dim(mods, layer * GROUPS + label, 0, keepdims=False)
        return jnp.pad(row.reshape(6, D), ((0, 2), (0, 0)))

    weights = [move.columns(b) for b in bundles]

    vid4 = jnp.pad(jnp.repeat(var_ids, 4), (0, D - PIXELS), constant_values=-1)[None].astype(
        jnp.int32
    )
    h0, agg, x_own = embed(at, tiles_in, tiles_got, emb, vid4)

    def forward(h, oth, oth_start, layer):
        mod = modulation(layer)
        normed, own = qkv_rows(at, h, 0, half, mod, weights[layer])
        _, other = qkv_rows(at, oth, oth_start, half, mod, weights[layer])
        out, *saved = block_forward(at, h, own, other, mod, weights[layer])
        return out, (mod, normed, own, other, saved)

    h1, kept0 = forward(h0, h0, half, 0)
    h2, kept1 = forward(h1, swap(h1, "c", 2, 1), 0, 1)

    forecasts = micro * dp
    by_column = basis.reshape(LONP, 2, 2 * LONP).transpose(1, 0, 2).reshape(2 * LONP, 2 * LONP)
    d_h2, loss, *g_head = head(
        at, cut, h2, truth_in, truth_got, weights[1], by_column.T, by_column, 1.0 / forecasts
    )

    def backward(d_out, h, kept, layer):
        mod, normed, own, other, saved = kept
        d_mid, d_att, g_out, dmod, *g_ff = mlp_back(at, cut, d_out, saved, mod, weights[layer])
        d_q, d_k, d_v, send = attention_back(at, own, other, saved[2], saved[1], d_att)
        got = swap(send, "c", 2, 1)
        d_h, dmod_one, *g_att = qkv_back(
            at, cut, d_q, d_k, d_v, got, normed, h, d_mid, g_out, mod, weights[layer]
        )
        return d_h, g_ff, g_att, (dmod + dmod_one)[:6].reshape(6 * D)

    def joined(one, two):
        return [jnp.concatenate([a, b], axis=-1) for a, b in zip(one, two)]

    d_h1, g_ff1, g_att1, dmod1 = backward(d_h2, h1, kept1, 1)
    got_ff1 = move.reduced(*joined(g_ff1, g_head))
    got_att1 = move.reduced(*g_att1)
    d_h0, g_ff0, g_att0, dmod0 = backward(d_h1, h0, kept0, 0)
    got_ff0 = move.reduced(*g_ff0)
    g_emb = embed_back(at, cut, d_h0, x_own, agg, emb, vid4)
    got_att0 = move.reduced(*joined(g_att0, g_emb))

    hot = (jnp.arange(GROUPS) == label).astype(F32)[:, None]
    sums = jnp.concatenate([hot * dmod0[None], hot * dmod1[None]])
    sums = jnp.concatenate([sums, jnp.broadcast_to(loss[:1, :1], (2, 6 * D))])
    sums = move.total(sums, ("s", "z", "c"))
    loss_value = sums[LAYERS * GROUPS, 0]
    by_lead = sums[: LAYERS * GROUPS].reshape(LAYERS, GROUPS, 6 * D)
    highest = lax.Precision.HIGHEST
    g_ada = jnp.einsum("gd,lgm->ldm", silu, by_lead, precision=highest)
    d_silu = jnp.einsum("ldm,lgm->gd", ada, by_lead, precision=highest)
    gate = jax.nn.sigmoid(lead)
    g_lead = d_silu * (gate * (1.0 + lead * (1.0 - gate)))

    ff = [got_ff0[..., :HALF], got_ff1[..., :HALF]]
    att = [got_att0[..., :D], got_att1]
    spread = lambda x: jnp.concatenate(list(x), axis=-1)
    g_qkv = jnp.stack([spread(x[:3]) for x in att])
    g_out = jnp.stack([x[3] for x in att])
    g_up = jnp.stack([spread(x[:2]) for x in ff])
    g_down = jnp.stack([spread(x[2:]).T for x in ff])
    g_embed = spread(got_att0[..., D:]).T[:EROWS]
    g_embed = jnp.concatenate([g_embed[:LEAD], g_lead])
    g_hw = lax.dot_general(
        spread(got_ff1[..., HALF:]), to_head.astype(F32), (((1,), (1,)), ((), ())), precision=highest
    )
    grads = (g_embed, g_qkv, g_out, g_up, g_down, g_ada, g_hw)

    squares = sum(jnp.sum(g * g) for g in grads)
    squares = move.total(jnp.full((8, 128), squares, F32), ("z", "c"))[0, 0]
    norm = jnp.sqrt(squares)
    factor = CLIP / jnp.maximum(norm, CLIP)
    count = sum(w.size for w in masters) * dp
    rate = 0.02 * math.sqrt(count) / CLIP
    new_w, new_m, new_a = [], [], []
    for i, (w, m, a, g) in enumerate(zip(masters, moments, averages, grads)):
        g = g * factor
        m = KEEP * m + g
        w = w - rate * (BOOST if i == 0 else 1.0) * (g + KEEP * m)
        new_w.append(w)
        new_m.append(m)
        new_a.append(KEEP * a + (1.0 - KEEP) * w)
    return (loss_value, norm, *new_w, *new_m, *new_a)


def solution(mesh):
    segments, dp = mesh.shape["segment"], mesh.shape["dp"]
    sizes = {"s": segments, "z": dp // 2, "c": 2}
    split = Mesh(mesh.devices.reshape(segments, dp // 2, 2), CHIP)
    d = ("z", "c")
    weights = (
        P(None, d),
        P(None, d, None),
        P(None, d, None),
        P(None, d, None),
        P(None, None, d),
        P(None, d, None),
        P(d, None),
    )
    return jax.shard_map(
        lambda *arrays: per_device(sizes, *arrays),
        mesh=split,
        in_specs=(P(d, None, None), P(d, None, None), P(d), P(), P()) + weights * 3,
        out_specs=(P(), P()) + weights * 3,
        check_vma=False,
    )
```

```python
import math

import jax
import jax.numpy as jnp
from jax import lax
from jax.experimental import pallas as pl
from jax.experimental.pallas import tpu as pltpu
from jax.sharding import Mesh, PartitionSpec as P

D = 384
HEADS = 6
HEAD_DIM = 64
FF = 1536
VARS = 69
CHANNELS = 69
LONP = 128
LATP = 8
LAYERS = 2
GROUPS = 3
PIXELS = 276
LEAD = PIXELS + VARS + 1
EROWS = LEAD + GROUPS
ECOLS = 512
EPS = 1e-06
CLIP = 0.001
KEEP = 0.9
BOOST = 20.0
LABEL_LANE = D - 1
HALF = FF // 2

F32 = jnp.float32
BF16 = jnp.bfloat16
CHIP = ("s", "z", "c")


def dot(a, b):
    return jnp.dot(a, b, preferred_element_type=F32)


def dot_nt(a, b):
    return lax.dot_general(a, b, (((1,), (1,)), ((), ())), preferred_element_type=F32)


def dot_tn(a, b):
    return lax.dot_general(a, b, (((0,), (0,)), ((), ())), preferred_element_type=F32)


def parts(x, count):
    out = []
    for step in range(count):
        piece = x.astype(BF16)
        out.append(piece)
        if step < count - 1:
            x = x - piece.astype(F32)
    return out


def normal(v):
    centered = v - jnp.mean(v, axis=-1, keepdims=True)
    inverse = lax.rsqrt(jnp.mean(centered * centered, axis=-1, keepdims=True) + EPS)
    return centered * inverse, inverse


def normal_back(d_x, x, inverse):
    return inverse * (
        d_x - jnp.mean(d_x, axis=-1, keepdims=True) - x * jnp.mean(d_x * x, axis=-1, keepdims=True)
    )


def lane_below(limit, shape):
    return lax.broadcasted_iota(jnp.int32, shape, len(shape) - 1) < limit


def sublane(shape):
    return lax.broadcasted_iota(jnp.int32, shape, 0)


def same_group():
    col = lax.broadcasted_iota(jnp.int32, (D, D), 1)
    return (sublane((D, D)) // 4 == col // 4).astype(BF16)


def chosen_table(vid_ref):
    return (sublane((ECOLS, D)) - PIXELS == vid_ref[...]).astype(BF16)


def first_of_four(shape):
    return sublane(shape) % 4 == 0


def cost(flops, size, exps=0):
    return pl.CostEstimate(flops=int(flops), bytes_accessed=int(size), transcendentals=int(exps))


VMEM = pl.BlockSpec(memory_space=pltpu.VMEM)
SMEM = pl.BlockSpec(memory_space=pltpu.SMEM)
ANY = pl.BlockSpec(memory_space=pl.ANY)
CHUNK = 256
AT_S, AT_Z, AT_C, AT_OWN, AT_LABEL = range(5)


def call(kernel, name, outs, inputs, estimate, scratch=(), limit=24, in_space=VMEM, out_spaces=None):
    return pl.pallas_call(
        kernel,
        in_specs=[SMEM] + [in_space] * (len(inputs) - 1),
        out_specs=out_spaces or [VMEM] * len(outs),
        out_shape=[jax.ShapeDtypeStruct(shape, kind) for shape, kind in outs],
        scratch_shapes=list(scratch),
        compiler_params=pltpu.CompilerParams(vmem_limit_bytes=limit << 20),
        cost_estimate=estimate,
        name=name,
    )(*inputs)


def rows_at(index, size):
    return pl.ds(pl.multiple_of(index * size, size), size)


def after(x, *others):
    return lax.optimization_barrier((x, others))[0]


def column_sum(v):
    return jnp.sum(v, axis=0, keepdims=True)


class Cut:
    def __init__(self, pairs, rows, split):
        self.pairs, self.rows, self.split = pairs, rows, split
        self.outputs = 2
        self.buffer = None

    def shapes(self, width, extra=False):
        if self.split:
            return [((4 * self.pairs + extra, self.rows, width), BF16)] * 2
        return [((4, D, width), BF16), ((1, 48, width), BF16)]

    def scratch(self, width):
        return [pltpu.VMEM((D, width), F32)]

    def on(self, buffer):
        other = Cut(self.pairs, self.rows, self.split)
        other.buffer = buffer
        return other

    def write(self, at_ref, outs, quarter, lane, value):
        width = value.shape[-1]
        cols = slice(lane, lane + width)
        if not self.split:
            outs[0][quarter, :, cols] = value.astype(BF16)
            return
        self.buffer[:, :width] = value
        core = at_ref[AT_C]
        for z in range(self.pairs):
            for ref, which in ((outs[0], core), (outs[1], 1 - core)):
                part = self.buffer[rows_at(2 * z + which, self.rows), :width]
                ref[quarter * self.pairs + z, :, cols] = part.astype(BF16)

    def write_extra(self, outs, value):
        value = value.astype(BF16)
        if self.split:
            outs[0][4 * self.pairs] = value
            outs[1][4 * self.pairs] = value
        else:
            outs[1][0] = value


def embed_kernel(
    at_ref, own_ref, got_ref, emb_ref, vid_ref,
    out_ref, agg_ref, x_ref, embk_ref, x_sc, bases_sc,
):
    tokens = own_ref.shape[1]
    half = tokens // 2
    emb = emb_ref[...]
    embk_ref[...] = emb.astype(F32).T.astype(BF16)
    query = jnp.broadcast_to(emb[:, LEAD - 1 : LEAD].astype(F32), (D, 128)).astype(BF16)
    by_row = dot_tn(emb, query)
    table = chosen_table(vid_ref)
    inside = sublane((D, 1)) < PIXELS
    proj = jnp.where(inside, by_row[:D, :1], 0.0)
    base = sum(dot_tn(table, p) for p in parts(by_row, 3))[:, :1]
    bases = dot_tn(table, embk_ref[...])
    bases_sc[...] = jnp.where(first_of_four((D, D)), bases, 0.0).astype(BF16)
    group = same_group()
    x_sc[...] = jnp.zeros_like(x_sc)
    x_sc[:PIXELS] = jnp.where(at_ref[AT_OWN] == 1, own_ref[...], got_ref[...])

    def step(i, carry):
        here = rows_at(i, CHUNK)
        source = lax.rem(i * CHUNK + at_ref[AT_C] * half, tokens)
        packed = x_sc[:, pl.ds(pl.multiple_of(source, CHUNK), CHUNK)]
        x = packed.astype(F32)
        scores = sum(dot(group, p) for p in parts(x * proj, 3)) + base
        scores = jnp.where(inside, scores * D ** (-0.5), -1e30)
        e = jnp.exp(scores - jnp.max(scores, axis=0, keepdims=True))
        agg = e * (4.0 / column_sum(e))

        @pl.when(i < half // CHUNK)
        def _():
            agg_ref[:, here] = agg
            x_ref[:, here] = packed

        total = dot_tn((agg * x).astype(BF16), embk_ref[:D])
        for p in parts(agg, 2):
            total = total + dot_tn(p, bases_sc[...])
        out_ref[here, :] = total.astype(BF16)
        return carry

    lax.fori_loop(0, tokens // CHUNK, step, 0)


def embed(at, own, got, emb, vid4):
    tokens = own.shape[1]
    return call(
        embed_kernel,
        "embed",
        [
            ((tokens, D), BF16),
            ((D, tokens // 2), F32),
            ((D, tokens // 2), BF16),
            ((ECOLS, D), BF16),
        ],
        [at, own, got, emb, vid4],
        cost(3e9, 4e6, 4e5),
        [pltpu.VMEM((D, tokens), BF16), pltpu.VMEM((D, D), BF16)],
    )


def embed_back(dh, x_ref, agg_ref, embk_ref, vid_ref):
    x = x_ref[...].astype(F32)
    agg = agg_ref[...]
    embk = embk_ref[:D]
    table = chosen_table(vid_ref)
    bases = dot_tn(table, embk_ref[...]).astype(BF16)
    query = embk_ref[LEAD - 1 : LEAD, :].astype(F32)
    g_patch = dot((agg * x).astype(BF16), dh)
    d_agg = dot_nt(bases, dh)
    group = same_group()
    for p in parts(dot_nt(embk, dh) * x, 2):
        d_agg = d_agg + dot(group, p)
    inner = 0.25 * column_sum(agg * d_agg)
    d_scores = agg * (d_agg - inner) * D ** (-0.5)
    d_proj = jnp.sum(d_scores * x, axis=-1, keepdims=True)
    d_base = jnp.sum(d_scores, axis=-1, keepdims=True)
    d_base = jnp.where(first_of_four(d_base.shape), d_base, 0.0)
    d_bases = d_base * query
    for p in parts(jnp.where(first_of_four((D, 1)), agg, 0.0), 2):
        d_bases = d_bases + dot(p, dh)
    g_table = sum(dot(table, p) for p in parts(d_bases, 2))
    d_query = column_sum(embk.astype(F32) * d_proj) + column_sum(bases.astype(F32) * d_base)
    total = g_table + jnp.where(sublane((ECOLS, 1)) == LEAD - 1, d_query, 0.0)
    return jnp.concatenate([total[:D] + g_patch + d_proj * query, total[D:]], axis=0)


def mod_row(mods_ref, at_ref, layer, index):
    row = layer * GROUPS + at_ref[AT_LABEL]
    return mods_ref[pl.ds(row, 1), D * index : D * (index + 1)]


def first_norm(h, mods_ref, at_ref, layer):
    x, inverse = normal(h.astype(F32))
    scale = 1.0 + mod_row(mods_ref, at_ref, layer, 1)
    return (x * scale + mod_row(mods_ref, at_ref, layer, 0)).astype(BF16), x, inverse


def pair_masks():
    low = lane_below(HEAD_DIM, (1, 128))
    return low, jnp.logical_not(low)


def both(own_ref, other_ref, lane):
    here = slice(lane, lane + 128)
    return jnp.concatenate([own_ref[:, here], other_ref[:, here]])


def attend(here, q_ref, own_ref, other_ref, att_ref, lse_ref):
    zero = jnp.zeros((), BF16)
    lane = lax.broadcasted_iota(jnp.int32, (CHUNK, 128), 1)
    sums = jnp.zeros((CHUNK, 128), F32)
    for pair in range(HEADS // 2):
        a = 128 * pair
        q = q_ref[here, a : a + 128] * 0.125
        keys = both(own_ref, other_ref, a)
        vals = both(own_ref, other_ref, D + a)
        mixed = jnp.zeros((CHUNK, 128), F32)
        for which, mask in enumerate(pair_masks()):
            scores = dot_nt(q, jnp.where(mask, keys, zero))
            top = jnp.max(scores, axis=-1, keepdims=True)
            e = jnp.exp(scores - top)
            total = jnp.sum(e, axis=-1, keepdims=True)
            mixed = mixed + dot(e.astype(BF16), jnp.where(mask, vals, zero)) * (1.0 / total)
            sums = jnp.where(lane == 2 * pair + which, top + jnp.log(total), sums)
        att_ref[here, a : a + 128] = mixed.astype(BF16)
    lse_ref[here, :] = sums


def gelu_and_slope(u):
    k = math.sqrt(2.0 / math.pi)
    t = jnp.tanh(k * (u + 0.044715 * (u * u * u)))
    cdf = 0.5 * (1.0 + t)
    return u * cdf, cdf + 0.5 * u * (1.0 - t * t) * k * (1.0 + 3 * 0.044715 * (u * u))


def feed_forward(here, h, one, mods_ref, at_ref, layer, w_ref, act_ref, slope_ref, n2_ref=None):
    middle = h.astype(F32) + mod_row(mods_ref, at_ref, layer, 2) * one
    x, _ = normal(middle)
    scale = 1.0 + mod_row(mods_ref, at_ref, layer, 4)
    n2 = (x * scale + mod_row(mods_ref, at_ref, layer, 3)).astype(BF16)
    if n2_ref is not None:
        n2_ref[here, :] = n2
    two = jnp.zeros((CHUNK, D), F32)
    for j in range(2):
        part = slice(HALF * j, HALF * (j + 1))
        act, slope = gelu_and_slope(dot(n2, w_ref[j, :, D : 3 * D]))
        slope_ref[here, part] = slope.astype(slope_ref.dtype)
        act = act.astype(BF16)
        act_ref[here, part] = act
        two = two + dot_nt(act, w_ref[2 + j, :, D : 3 * D])
    return middle, two, middle + mod_row(mods_ref, at_ref, layer, 5) * two


def feed_back(
    here, d_out, one, two, middle, slope_ref, mods_ref, at_ref, layer, w_ref,
    dunits_ref, dtwo_ref, done_ref, dmid_ref, datt_ref, dmod_ref, n2_ref=None,
):
    d_out = d_out.astype(F32)
    d_two = (mod_row(mods_ref, at_ref, layer, 5) * d_out).astype(BF16)
    dtwo_ref[here, :] = d_two
    d_n2 = jnp.zeros(d_out.shape, F32)
    for j in range(2):
        part = slice(HALF * j, HALF * (j + 1))
        slope = slope_ref[here, part].astype(F32)
        d_units = (slope * dot(d_two, w_ref[2 + j, :, D : 3 * D])).astype(BF16)
        dunits_ref[here, part] = d_units
        d_n2 = d_n2 + dot_nt(d_units, w_ref[j, :, D : 3 * D])
    x, inverse = normal(middle)
    scale = 1.0 + mod_row(mods_ref, at_ref, layer, 4)
    if n2_ref is not None:
        n2_ref[here, :] = (x * scale + mod_row(mods_ref, at_ref, layer, 3)).astype(BF16)
    d_mid = d_out + normal_back(d_n2 * scale, x, inverse)
    dmid_ref[here, :] = d_mid
    d_one = (mod_row(mods_ref, at_ref, layer, 2) * d_mid).astype(BF16)
    done_ref[here, :] = d_one
    datt_ref[here, :] = dot_nt(d_one, w_ref[3, :, :D]).astype(BF16)
    dmod_ref[2:3] += column_sum(d_mid * one)
    dmod_ref[3:4] += column_sum(d_n2)
    dmod_ref[4:5] += column_sum(d_n2 * x)
    dmod_ref[5:6] += column_sum(d_out * two)


def feed_gradients(at_ref, cut, outs, lane, n2_ref, dunits_ref, dtwo_ref, act_ref):
    for j in range(2):
        part = slice(HALF * j, HALF * (j + 1))
        cut.write(at_ref, outs, j, lane, dot_tn(n2_ref[...], dunits_ref[:, part]))
        cut.write(at_ref, outs, 2 + j, lane, dot_tn(dtwo_ref[...], act_ref[:, part]))


def rows_scratch(count, widths):
    return [pltpu.VMEM((count, width), BF16) for width in widths]


def block_kernel(
    at_ref, h_ref, mods_ref, w_ref,
    out_ref, q_out, own_out, other_out, att_out, lse_out, one_out, mid_out, slope_out, act_out, two_out,
    q_ref, own_ref, other_ref, att_ref, lse_ref, one_ref, mid_ref, slope_ref, act_ref, two_ref, sems,
):
    count = out_ref.shape[0]
    steps = count // CHUNK

    def project(i, carry):
        here = rows_at(i, CHUNK)
        normed, _, _ = first_norm(h_ref[here, :], mods_ref, at_ref, 0)
        q_ref[here, :] = dot(normed, w_ref[0, :, :D]).astype(BF16)
        for j in range(2):
            own_ref[here, D * j : D * (j + 1)] = dot(normed, w_ref[j + 1, :, :D]).astype(BF16)
        return carry

    lax.fori_loop(0, steps, project, 0)

    def project_other(i, carry):
        here = rows_at(i, CHUNK)
        normed, _, _ = first_norm(h_ref[rows_at(i + steps, CHUNK), :], mods_ref, at_ref, 0)
        for j in range(2):
            other_ref[here, D * j : D * (j + 1)] = dot(normed, w_ref[j + 1, :, :D]).astype(BF16)
        return carry

    lax.fori_loop(0, steps, project_other, 0)
    early = [
        pltpu.make_async_copy(ref, out, sems.at[2, i])
        for i, (ref, out) in enumerate(((q_ref, q_out), (own_ref, own_out), (other_ref, other_out)))
    ]
    for copy in early:
        copy.start()
    kept = (
        (att_ref, att_out), (lse_ref, lse_out), (one_ref, one_out), (mid_ref, mid_out),
        (slope_ref, slope_out), (act_ref, act_out), (two_ref, two_out),
    )

    def copies(i):
        here = rows_at(i, CHUNK)
        return [
            pltpu.make_async_copy(ref.at[here], out.at[here], sems.at[i, k])
            for k, (ref, out) in enumerate(kept)
        ]

    def step(i, carry):
        here = rows_at(i, CHUNK)
        attend(here, q_ref, own_ref, other_ref, att_ref, lse_ref)
        one = dot(att_ref[here, :], w_ref[3, :, :D])
        one_ref[here, :] = one.astype(BF16)
        middle, two, out = feed_forward(
            here, h_ref[here, :], one, mods_ref, at_ref, 0, w_ref, act_ref, slope_ref
        )
        mid_ref[here, :] = middle
        two_ref[here, :] = two.astype(BF16)
        out_ref[here, :] = out.astype(BF16)
        for copy in copies(i):
            copy.start()
        return carry

    lax.fori_loop(0, steps, step, 0)
    for copy in early:
        copy.wait()
    for i in range(steps):
        for copy in copies(i):
            copy.wait()


def block_forward(at, h, mods, weights):
    count = h.shape[0] // 2
    kept = [(D, BF16), (2 * D, BF16), (2 * D, BF16), (D, BF16), (128, F32), (D, BF16), (D, F32)]
    kept += [(FF, BF16), (FF, BF16), (D, BF16)]
    kept = [((count, width), kind) for width, kind in kept]
    return call(
        block_kernel,
        "block_forward",
        [((count, D), BF16)] + kept,
        [at, h, mods, weights],
        cost(6e9, 1.2e7, 3e6),
        [pltpu.VMEM(shape, kind) for shape, kind in kept] + [pltpu.SemaphoreType.DMA((3, 7))],
        limit=28,
        out_spaces=[VMEM] + [ANY] * len(kept),
    )


def qkv_kernel(at_ref, h_ref, mods_ref, w_ref, q_ref, kv_ref):
    def step(i, carry):
        here = rows_at(i, CHUNK)
        normed, _, _ = first_norm(h_ref[here, :], mods_ref, at_ref, 1)
        q_ref[here, :] = dot(normed, w_ref[0, :, :D]).astype(BF16)
        for j in range(2):
            kv_ref[here, D * j : D * (j + 1)] = dot(normed, w_ref[j + 1, :, :D]).astype(BF16)
        return carry

    lax.fori_loop(0, q_ref.shape[0] // CHUNK, step, 0)


def qkv_rows(at, h, mods, weights):
    count = h.shape[0]
    return call(
        qkv_kernel,
        "qkv_rows",
        [((count, D), BF16), ((count, 2 * D), BF16)],
        [at, h, mods, weights],
        cost(1e9, 3e6),
    )


def turn_kernel(
    at_ref, h_ref, q_ref, own_ref, other_ref, mods_ref, w_ref, truth_ref, got_ref, basis_ref,
    dmid_ref, datt_ref, att_ref, lse_ref, gout_ref, dmod_ref, loss_ref, keep_ref, send_ref,
    act_ref, dunits_ref, dtwo_ref, n2_ref, done_ref, flat_ref, dpred_ref, true_ref, slope_ref,
    basis_sc, buffer, *, seed, cut,
):
    count = h_ref.shape[0]
    outs = (keep_ref, send_ref)
    entries = LATP * CHANNELS * 2 * LONP
    dmod_ref[...] = jnp.zeros_like(dmod_ref)
    loss_ref[...] = jnp.zeros_like(loss_ref)
    row = lax.broadcasted_iota(jnp.int32, (PIXELS, 256), 0)
    col = lax.broadcasted_iota(jnp.int32, (PIXELS, 256), 1)
    lanes = rows_at(at_ref[AT_C], count)
    truth = jnp.where(at_ref[AT_OWN] == 1, truth_ref[:, lanes], got_ref[:, lanes])
    for b in range(2):
        picked = dot_tn(truth, (row == 2 * col + b).astype(BF16))
        true_ref[:, 256 * b : 256 * b + 256] = picked.astype(BF16)
    to = lax.broadcasted_iota(jnp.int32, (256, 256), 0)
    source = lax.broadcasted_iota(jnp.int32, (256, 256), 1)
    order = (source == 2 * (to % LONP) + to // LONP).astype(BF16)
    for i, p in enumerate(parts(basis_ref[...], 2)):
        basis_sc[i] = dot(order, p).astype(BF16)

    def step(i, carry):
        here = rows_at(i, CHUNK)
        attend(here, q_ref, own_ref, other_ref, att_ref, lse_ref)
        one = dot(att_ref[here, :], w_ref[3, :, :D])
        middle, two, h2 = feed_forward(
            here, h_ref[here, :], one, mods_ref, at_ref, 1, w_ref, act_ref, slope_ref, n2_ref
        )
        x, inverse = normal(h2.astype(BF16).astype(F32))
        flat = x.astype(BF16)
        flat_ref[here, :] = flat
        hw = [w_ref[j, :, 3 * D : 3 * D + 128] for j in range(4)]
        pred = [dot(flat, w) for w in hw]
        pred = [jnp.concatenate(pred[:2], axis=-1), jnp.concatenate(pred[2:], axis=-1)]
        hi, lo = basis_sc[0], basis_sc[1]
        grads = [[], []]
        loss = jnp.zeros((1, 1), F32)
        for p in range(CHUNK // LONP):
            part = slice(p * LONP, (p + 1) * LONP)
            fine = rows_at(i * (CHUNK // LONP) + p, LONP)
            seen = parts(jnp.concatenate([pred[0][part], pred[1][part]], axis=0), 2)
            waves = dot_tn(hi, seen[0]) + (dot_tn(hi, seen[1]) + dot_tn(lo, seen[0]))
            want = jnp.concatenate([true_ref[fine, :256], true_ref[fine, 256:]], axis=0)
            target = dot_tn(hi, want) + dot_tn(lo, want)
            top, low = waves[:LONP], waves[LONP:]
            gap = (top * top + low * low) - (
                target[:LONP] * target[:LONP] + target[LONP:] * target[LONP:]
            )
            loss = loss + jnp.sum(gap * gap, axis=(0, 1), keepdims=True)
            scaled = gap * (4.0 * seed / entries)
            d_waves = parts(jnp.concatenate([scaled * top, scaled * low], axis=0), 2)
            d_seen = dot(hi, d_waves[0]) + (dot(hi, d_waves[1]) + dot(lo, d_waves[0]))
            d_seen = d_seen.astype(BF16)
            grads[0].append(d_seen[:LONP])
            grads[1].append(d_seen[LONP:])
        loss_ref[...] += jnp.broadcast_to(loss * (seed / entries), loss_ref.shape)
        d_flat = jnp.zeros((CHUNK, D), F32)
        for b in range(2):
            whole = jnp.concatenate(grads[b], axis=0)
            dpred_ref[here, 256 * b : 256 * b + 256] = whole
            for j in range(2):
                d_flat = d_flat + dot_nt(whole[:, 128 * j : 128 * j + 128], hw[2 * b + j])
        d_h2 = normal_back(d_flat, x, inverse).astype(BF16)
        feed_back(
            here, d_h2, one, two, middle, slope_ref, mods_ref, at_ref, 1, w_ref,
            dunits_ref, dtwo_ref, done_ref, dmid_ref, datt_ref, dmod_ref,
        )
        return carry

    lax.fori_loop(0, count // CHUNK, step, 0)
    cut = cut.on(buffer)
    feed_gradients(at_ref, cut, outs, 0, n2_ref, dunits_ref, dtwo_ref, act_ref)
    for j in range(4):
        cut.write(at_ref, outs, j, HALF, dot_tn(flat_ref[...], dpred_ref[:, 128 * j : 128 * j + 128]))
    gout_ref[...] = dot_tn(att_ref[...], done_ref[...])


def turn(at, cut, h, q, own, other, mods, weights, truth, got, basis, seed):
    count = h.shape[0]
    return call(
        lambda *refs: turn_kernel(*refs, seed=seed, cut=cut),
        "turn",
        [
            ((count, D), F32),
            ((count, D), BF16),
            ((count, D), BF16),
            ((count, 128), F32),
            ((D, D), F32),
            ((8, D), F32),
            ((8, 128), F32),
        ]
        + cut.shapes(HALF + 128),
        [at, h, q, own, other, mods, weights, truth, got, basis],
        cost(1.2e10, 1.2e7, 4e6),
        rows_scratch(count, [FF, FF, D, D, D, D, 512, 512])
        + [pltpu.VMEM((count, FF), F32), pltpu.VMEM((2, 256, 256), BF16)]
        + cut.scratch(HALF),
        limit=32,
    )


def attention_back_kernel(
    at_ref, q_ref, own_ref, other_ref, lse_ref, att_ref, datt_ref, dq_ref, dk_ref, dv_ref, send_ref,
    dk_sc, dv_sc,
):
    zero = jnp.zeros((), BF16)
    count = q_ref.shape[0]
    dk_sc[...] = jnp.zeros_like(dk_sc)
    dv_sc[...] = jnp.zeros_like(dv_sc)

    def step(i, carry):
        rows = rows_at(i, CHUNK)
        for pair in range(HEADS // 2):
            a = 128 * pair
            here = slice(a, a + 128)
            q = q_ref[rows, here]
            d_att = datt_ref[rows, here]
            keys = both(own_ref, other_ref, a)
            vals = both(own_ref, other_ref, D + a)
            dots = d_att.astype(F32) * att_ref[rows, here].astype(F32)
            d_q = jnp.zeros((CHUNK, 128), F32)
            d_k = jnp.zeros((keys.shape[0], 128), F32)
            d_v = jnp.zeros((keys.shape[0], 128), F32)
            for which, mask in enumerate(pair_masks()):
                head = 2 * pair + which
                k = jnp.where(mask, keys, zero)
                v = jnp.where(mask, vals, zero)
                inner = jnp.sum(jnp.where(mask, dots, 0.0), axis=-1, keepdims=True)
                probs = jnp.exp(dot_nt(q * 0.125, k) - lse_ref[rows, head : head + 1])
                d_scores = (probs * (dot_nt(d_att, v) - inner)).astype(BF16)
                d_q = d_q + dot(d_scores, k)
                d_k = d_k + dot_tn(d_scores, jnp.where(mask, q, zero))
                d_v = d_v + dot_tn(probs.astype(BF16), jnp.where(mask, d_att, zero))
            dq_ref[rows, here] = (d_q * 0.125).astype(BF16)
            dk_sc[:, here] += d_k * 0.125
            dv_sc[:, here] += d_v
        return carry

    lax.fori_loop(0, count // CHUNK, step, 0)
    dk_ref[...] = dk_sc[:count]
    dv_ref[...] = dv_sc[:count]
    send_ref[0] = dk_sc[count:].astype(BF16)
    send_ref[1] = dv_sc[count:].astype(BF16)


def attention_back(at, q, own, other, lse, att, d_att):
    count = q.shape[0]
    return call(
        attention_back_kernel,
        "attention_back",
        [((count, D), BF16), ((count, D), F32), ((count, D), F32), ((2, count, D), BF16)],
        [at, q, own, other, lse, att, d_att],
        cost(6e9, 8e6, 3e6),
        [pltpu.VMEM((2 * count, D), F32)] * 2,
    )


def qkv_back(
    at_ref, cut, outs, lane, layer, dq_ref, dk_ref, dv_ref, got_ref, h_ref, dmid_ref, gout_ref, mods_ref, w_ref,
):
    count = dq_ref.shape[0]
    normed, x, inverse = first_norm(h_ref[:count], mods_ref, at_ref, layer)
    d_k = (dk_ref[...] + got_ref[0].astype(F32)).astype(BF16)
    d_v = (dv_ref[...] + got_ref[1].astype(F32)).astype(BF16)
    d_n = jnp.zeros((count, D), F32)
    for j, piece in enumerate((dq_ref[...], d_k, d_v)):
        d_n = d_n + dot_nt(piece, w_ref[j, :, :D])
        cut.write(at_ref, outs, j, lane, dot_tn(normed, piece))
    cut.write(at_ref, outs, 3, lane, gout_ref[...])
    scale = 1.0 + mod_row(mods_ref, at_ref, layer, 1)
    d_h = dmid_ref[...] + normal_back(d_n * scale, x, inverse)
    return d_h.astype(BF16), column_sum(d_n), column_sum(d_n * x)


def between_kernel(
    at_ref, dq_ref, dk_ref, dv_ref, got_ref, h_ref, dmid_ref, gout_ref, dmod_ref, mods_ref, w1_ref,
    one_ref, two_ref, mid_ref, slope_ref, act_ref, att_ref, w0_ref,
    dmid_out, datt_out, gout_out, dmod_out, dmod_next, keep_ref, send_ref,
    dh_sc, dunits_ref, dtwo_ref, n2_ref, done_ref, buffer, *, cut,
):
    outs = (keep_ref, send_ref)
    cut = cut.on(buffer)
    d_h, shift, scale = qkv_back(
        at_ref, cut, outs, 0, 1, dq_ref, dk_ref, dv_ref, got_ref, h_ref, dmid_ref, gout_ref, mods_ref, w1_ref,
    )
    dmod_out[...] = dmod_ref[...]
    dmod_out[0:1] = shift
    dmod_out[1:2] = scale
    dh_sc[...] = d_h
    dmod_next[...] = jnp.zeros_like(dmod_next)

    def step(i, carry):
        here = rows_at(i, CHUNK)
        feed_back(
            here, dh_sc[here, :], one_ref[here, :].astype(F32), two_ref[here, :].astype(F32),
            mid_ref[here, :], slope_ref, mods_ref, at_ref, 0, w0_ref,
            dunits_ref, dtwo_ref, done_ref, dmid_out, datt_out, dmod_next, n2_ref,
        )
        return carry

    lax.fori_loop(0, dh_sc.shape[0] // CHUNK, step, 0)
    feed_gradients(at_ref, cut, outs, D, n2_ref, dunits_ref, dtwo_ref, act_ref)
    gout_out[...] = dot_tn(att_ref[...], done_ref[...])


def between(at, cut, grads, h, d_mid, g_out, dmod, mods, w1, kept, w0):
    att, one, mid, slope, act, two = kept
    count = d_mid.shape[0]
    return call(
        lambda *refs: between_kernel(*refs, cut=cut),
        "between",
        [((count, D), F32), ((count, D), BF16), ((D, D), F32), ((8, D), F32), ((8, D), F32)]
        + cut.shapes(D + HALF),
        [at, *grads, h, d_mid, g_out, dmod, mods, w1, one, two, mid, slope, act, att, w0],
        cost(6e9, 2e7),
        rows_scratch(count, [D, FF, D, D, D]) + cut.scratch(HALF),
        limit=28,
    )


def last_kernel(
    at_ref, dq_ref, dk_ref, dv_ref, got_ref, h_ref, dmid_ref, gout_ref, dmod0_ref, dmod1_ref, loss_ref,
    mods_ref, w_ref, x_ref, agg_ref, embk_ref, vid_ref, keep_ref, send_ref, sums_sc, buffer, *, cut,
):
    outs = (keep_ref, send_ref)
    cut = cut.on(buffer)
    d_h, shift, scale = qkv_back(
        at_ref, cut, outs, 0, 0, dq_ref, dk_ref, dv_ref, got_ref, h_ref, dmid_ref, gout_ref, mods_ref, w_ref,
    )
    sums_sc[...] = jnp.zeros_like(sums_sc)
    for group in range(GROUPS):
        hot = (at_ref[AT_LABEL] == group).astype(F32)
        for layer, ref in enumerate((dmod0_ref, dmod1_ref)):
            at = 8 * (GROUPS * layer + group)
            sums_sc[at : at + 8, :D] = ref[...] * hot
        sums_sc[8 * group : 8 * group + 1, :D] = shift * hot
        sums_sc[8 * group + 1 : 8 * group + 2, :D] = scale * hot
    loss = loss_ref[0:1, 0:1]
    top = loss.astype(BF16).astype(F32)
    sums_sc[6:7, :] = jnp.broadcast_to(top, (1, ECOLS))
    sums_sc[7:8, :] = jnp.broadcast_to(loss - top, (1, ECOLS))
    cut.write_extra(outs, sums_sc[...])
    g = embed_back(d_h, x_ref, agg_ref, embk_ref, vid_ref).T
    for j in range(4):
        cut.write(at_ref, outs, j, D, g[:, 128 * j : 128 * j + 128])


def last(at, cut, grads, h, d_mid, g_out, dmod0, dmod1, loss, mods, w0, x, agg, embk, vid4):
    return call(
        lambda *refs: last_kernel(*refs, cut=cut),
        "last",
        cut.shapes(ECOLS, True),
        [at, *grads, h, d_mid, g_out, dmod0, dmod1, loss, mods, w0, x, agg, embk, vid4],
        cost(4e9, 1e7),
        [pltpu.VMEM((48, ECOLS), F32)] + cut.scratch(D),
        limit=28,
    )


def swap(x, axis, size, by):
    return lax.ppermute(x, axis, [(i, i ^ by) for i in range(size)])


def place_kernel(at_ref, *refs, columns, rows):
    out_ref, sems = refs[-2], refs[-1]
    inputs = refs[:-2]
    s, z, c = at_ref[AT_S], at_ref[AT_Z], at_ref[AT_C]
    copies = []
    index = 0
    for jc in range(2):
        for js in range(columns):
            source = inputs[jc * columns + js]
            for jz in range(source.shape[0]):
                at = rows_at((z ^ jz) * 2 + (c ^ jc), rows)
                target = out_ref.at[s ^ js, at] if columns > 1 else out_ref.at[at]
                copies.append(pltpu.make_async_copy(source.at[jz], target, sems.at[index]))
                index += 1
    for copy in copies:
        copy.start()
    for copy in copies:
        copy.wait()


def placed(at, own, got):
    columns, (zs, rows, width) = len(own), own[0].shape
    full = (zs * 2 * rows, width)
    shape = (columns,) + full if columns > 1 else full
    return call(
        lambda *refs: place_kernel(*refs, columns=columns, rows=rows),
        "placed",
        [(shape, BF16)],
        [at, *own, *got],
        cost(0, 4 * math.prod(shape)),
        [pltpu.SemaphoreType.DMA((2 * columns * zs,))],
        limit=4,
        in_space=ANY,
    )[0]


def two_rows(v):
    loss = v[6:7] + v[7:8]
    top = loss.astype(BF16).astype(F32)
    row = sublane(v.shape)
    return jnp.where(row == 6, top, jnp.where(row == 7, loss - top, v)).astype(BF16)


def add_core_kernel(at_ref, kept_ref, got_ref, own_ref, *sends):
    zs = 4
    for j in range(4):
        here = pl.ds((at_ref[AT_S] ^ j) * zs, zs)
        value = kept_ref[here].astype(F32) + got_ref[here].astype(F32)
        if j == 0:
            own_ref[:zs] = value
        else:
            sends[j - 1][:zs] = value.astype(BF16)
    if own_ref.shape[0] > zs:
        value = two_rows(kept_ref[4 * zs].astype(F32) + got_ref[4 * zs].astype(F32))
        own_ref[zs] = value.astype(F32)
        for send in sends:
            send[zs] = value


def summed(refs, at):
    a, b, c, d = (ref[at].astype(F32) for ref in refs)
    return (a + b) + (c + d)


def add_segment_kernel(at_ref, own_ref, a_ref, b_ref, c_ref, kept_ref, *sends):
    refs = (own_ref, a_ref, b_ref, c_ref)
    for j in range(4):
        value = summed(refs, at_ref[AT_Z] ^ j)
        if j == 0:
            kept_ref[0] = value
        else:
            sends[j - 1][0] = value.astype(BF16)
    if kept_ref.shape[0] > 1:
        value = two_rows(summed(refs, 4))
        kept_ref[1] = value.astype(F32)
        for send in sends:
            send[1] = value


def add_plane_kernel(at_ref, own_ref, a_ref, b_ref, c_ref, out_ref, *more):
    refs = (own_ref, a_ref, b_ref, c_ref)
    out_ref[...] = summed(refs, 0).astype(BF16)
    if more:
        more[0][...] = summed(refs, 1)


class Plain:
    split = False

    def __init__(self, sizes, at):
        self.sizes, self.at = sizes, at
        self.order = at.at[AT_S].set(0)

    def rows(self, x, ready):
        return lax.all_gather(x, ("z", "c"), axis=0, tiled=True)

    def columns(self, bundles, ready):
        return [lax.all_gather(x, ("z", "c"), axis=1, tiled=True) for x in bundles]

    def total(self, x):
        return lax.psum(x, ("z", "c"))

    def core(self, g):
        own = lax.psum_scatter(g[0].astype(F32), ("z", "c"), scatter_dimension=1, tiled=True)
        return lax.psum(own, "s"), lax.psum(g[1][0].astype(F32), CHIP)

    def segment(self, x):
        return x

    def plane(self, x):
        return x

    def shared(self, xs):
        return [[x[0][j].astype(BF16) for j in range(4)] for x in xs]


class Squares(Plain):
    split = True

    def __init__(self, sizes, at):
        self.sizes, self.at, self.order = sizes, at, at

    def across(self, x, axis):
        return [swap(x, axis, 4, by) for by in (1, 2, 3)]

    def rows(self, x, ready):
        own = jnp.stack([x] + self.across(x, "z"))
        return placed(self.at, [own], [swap(own, "c", 2, 1)])

    def columns(self, bundles, ready):
        out, wait = [], ()
        for x in bundles:
            mine = lax.dynamic_index_in_dim(x, self.at[AT_S], 0, keepdims=False)
            stack = jnp.stack([mine] + self.across(after(mine, *wait), "z"))
            own = [stack] + self.across(after(stack, *wait), "s")
            out.append((own, [swap(y, "c", 2, 1) for y in own]))
            wait = (stack,)
        return [placed(self.at, own, got) for own, got in out]

    def total(self, x):
        one, two, three = self.across(x, "z")
        x = (x + one) + (two + three)
        return x + swap(x, "c", 2, 1)

    def core(self, g):
        kept, sent = g
        count, rows, width = kept.shape
        full = (4 + count % 4, rows, width)
        return call(
            add_core_kernel, "add_core", [(full, F32)] + [(full, BF16)] * 3,
            [self.at, kept, swap(sent, "c", 2, 1)], cost(0, 8 * math.prod(kept.shape)),
        )

    def segment(self, x):
        own, *sends = x
        count, rows, width = own.shape
        one = (count - 3, rows, width)
        got = [swap(y, "s", 4, j + 1) for j, y in enumerate(sends)]
        return call(
            add_segment_kernel, "add_segment", [(one, F32)] + [(one, BF16)] * 3,
            [self.at, own, *got], cost(0, 12 * math.prod(own.shape)),
        )

    def plane(self, x):
        own, *sends = x
        count, rows, width = own.shape
        got = [swap(y, "z", 4, j + 1) for j, y in enumerate(sends)]
        return call(
            add_plane_kernel, "add_plane",
            [((rows, width), BF16)] + [((rows, width), F32)] * (count - 1),
            [self.at, own, *got], cost(0, 12 * math.prod(own.shape)),
        )

    def shared(self, xs):
        x = jnp.concatenate([y[0] for y in xs], axis=-1)
        pieces = [x] + self.across(x, "s")
        ends, at = [], 0
        for y in xs:
            width = y[0].shape[-1]
            ends.append([p[:, at : at + width] for p in pieces])
            at += width
        return ends


def lead_parts(emb_ref):
    lead = emb_ref[:, LEAD:EROWS].astype(BF16).astype(F32)
    gate = jax.nn.sigmoid(lead)
    return lead * gate, gate * (1.0 + lead * (1.0 - gate))


def ada_gradient(silu, sums_ref, layer, index):
    total = 0.0
    for group in range(GROUPS):
        at = 8 * (GROUPS * layer + group) + index
        total = total + silu[:, group : group + 1] * sums_ref[at : at + 1, :D]
    return total


def square_sum(v):
    return jnp.sum(v * v, axis=(0, 1), keepdims=True)


def gather_kernel(at_ref, *refs, widths):
    pieces, (emb_ref, ada_ref, sums_ref), outs = refs[:12], refs[12:15], refs[15:]
    ordered, (lead_ref, square_ref) = outs[:3], outs[3:]
    total = jnp.zeros((1, 1), F32)
    for k, ref in enumerate(ordered):
        squares = []
        for j in range(4):
            piece = pieces[4 * k + j][...]
            ref[at_ref[AT_S] ^ j] = piece
            squares.append(square_sum(piece.astype(F32)))
        total = total + ((squares[0] + squares[1]) + (squares[2] + squares[3]))
    silu, slope = lead_parts(emb_ref)
    rows = silu.shape[0]
    lane = lax.broadcasted_iota(jnp.int32, (rows, 128), 1)
    lead = jnp.zeros((rows, 128), F32)
    for group in range(GROUPS):
        d_silu = jnp.zeros((rows, 1), F32)
        for layer in range(LAYERS):
            for i in range(6):
                at = 8 * (GROUPS * layer + group) + i
                ada = ada_ref[layer, :, D * i : D * (i + 1)].astype(BF16).astype(F32)
                d_silu = d_silu + jnp.sum(ada * sums_ref[at : at + 1, :D], axis=-1, keepdims=True)
        value = d_silu * slope[:, group : group + 1]
        total = total + square_sum(value)
        lead = jnp.where(lane == group, value, lead)
    for layer in range(LAYERS):
        for i in range(6):
            total = total + square_sum(ada_gradient(silu, sums_ref, layer, i))
    lead_ref[...] = lead
    square_ref[...] = jnp.broadcast_to(total, square_ref.shape)


def gathered(at, pieces, emb_t, ada, sums):
    widths = [group[0].shape for group in pieces]
    return call(
        lambda *refs: gather_kernel(*refs, widths=widths),
        "gathered",
        [((4,) + shape, BF16) for shape in widths]
        + [((widths[0][0], 128), F32), ((8, 128), F32)],
        [at, *pieces[0], *pieces[1], *pieces[2], emb_t, ada, sums],
        cost(0, 4e6),
    )


def update_kernel(at_ref, *refs, rate):
    g1_ref, g2_ref, g3_ref, lead_ref, sums_ref, own_ref, got_ref = refs[:7]
    state = refs[7:28]
    outs, (loss_ref, norm_ref) = refs[28:49], refs[49:51]
    results, sems = refs[51:72], refs[72]
    squares = own_ref[0:1, 0:1] + got_ref[0:1, 0:1]
    norm = jnp.sqrt(squares)
    factor = CLIP / jnp.maximum(norm, CLIP)
    norm_ref[...] = norm
    loss_ref[...] = sums_ref[6:7, 0:1] + sums_ref[7:8, 0:1]
    silu, _ = lead_parts(state[0])
    rows = silu.shape[0]

    def advance(index, at, g):
        w_ref, m_ref, a_ref = (state[index + 7 * k] for k in range(3))
        g = g.astype(F32) * factor
        m = KEEP * m_ref[at] + g
        w = w_ref[at] - rate * (BOOST if index == 0 else 1.0) * (g + KEEP * m)
        results[index + 7][at] = m
        results[index][at] = w
        results[index + 14][at] = KEEP * a_ref[at] + (1.0 - KEEP) * w

    copies = []

    def send(index):
        for k in range(3):
            i = index + 7 * k
            copy = pltpu.make_async_copy(results[i], outs[i], sems.at[i])
            copy.start()
            copies.append(copy)

    every = slice(None)
    for layer in range(LAYERS):
        for i in range(6):
            g = ada_gradient(silu, sums_ref, layer, i)
            advance(5, (layer, every, slice(D * i, D * (i + 1))), g)
    send(5)
    att = (g3_ref, g2_ref)
    ff = ((g2_ref, D), (g1_ref, 0))
    for layer in range(LAYERS):
        ref, lane = ff[layer]
        for j in range(2):
            part = slice(HALF * j, HALF * (j + 1))
            advance(3, (layer, every, part), ref[j, :, lane : lane + HALF])
            advance(4, (layer, every, part), ref[2 + j, :, lane : lane + HALF])
    send(3)
    send(4)
    for layer in range(LAYERS):
        for j in range(3):
            advance(1, (layer, every, slice(D * j, D * (j + 1))), att[layer][j, :, :D])
    send(1)
    for layer in range(LAYERS):
        advance(2, (layer,), att[layer][3, :, :D])
    send(2)
    col = lax.broadcasted_iota(jnp.int32, (512, PIXELS), 1)
    row = lax.broadcasted_iota(jnp.int32, (512, PIXELS), 0)
    back = jnp.logical_and(row // 256 == col % 2, row % 256 == col // 2).astype(BF16)
    g_head = jnp.concatenate([g1_ref[j, :, HALF : HALF + 128] for j in range(4)], axis=-1)
    advance(6, (every,), dot(g_head, back))
    send(6)
    lane = lax.broadcasted_iota(jnp.int32, (rows, 128), 1)
    for j in range(3):
        g = g3_ref[j, :, D : D + 128].astype(F32)
        width = min(128, EROWS - 128 * j)
        if LEAD < 128 * j + width:
            first = LEAD - 128 * j
            for group in range(GROUPS):
                g = jnp.where(lane == first + group, lead_ref[:, group : group + 1], g)
        advance(0, (every, slice(128 * j, 128 * j + width)), g[:, :width])
    send(0)
    for copy in copies:
        copy.wait()


def updated(at, g, lead, sums, own, got, state, rate):
    shapes = [(x.shape, F32) for x in state]
    scalar = [((1, 1), F32)] * 2
    inputs = [at, *g, lead, sums, own, got, *state]
    return call(
        lambda *refs: update_kernel(*refs, rate=rate),
        "updated",
        shapes + scalar,
        inputs,
        cost(0, 2e7),
        [pltpu.VMEM(shape, kind) for shape, kind in shapes] + [pltpu.SemaphoreType.DMA((21,))],
        limit=24,
        out_spaces=[ANY] * 21 + [VMEM] * 2,
    )


def layer_bundle(qkv, out, up, down_t, extra):
    pieces = []
    for j in range(4):
        first = qkv[:, D * j : D * (j + 1)] if j < 3 else out
        source = up if j < 2 else down_t
        second = source[:, HALF * (j % 2) : HALF * (j % 2 + 1)]
        row = [first, second] + ([extra[j]] if extra is not None else [])
        pieces.append(jnp.concatenate(row, axis=-1))
    return jnp.stack(pieces)


def per_device(sizes, *arrays):
    (tiles_in, truth_in, labels, var_ids, basis) = arrays[:5]
    masters = arrays[5:12]
    embed_w, qkv_w, out_w, up_w, down_w, ada_w, head_w = masters
    segments, dp = sizes["s"], sizes["z"] * 2
    micro = tiles_in.shape[0]
    assert segments == 2 * micro
    rows = D // dp
    s, z, c = (lax.axis_index(name) for name in CHIP)
    which, owner = s % micro, s // micro
    is_owner = c == owner

    pairs = []
    for a in range(segments):
        for b in range(sizes["z"]):
            base = (a * sizes["z"] + b) * 2
            pairs.append((base + a // micro, base + 1 - a // micro))
    pick = lambda x: lax.dynamic_index_in_dim(x, which, 0, keepdims=False).T
    tiles, truth = pick(tiles_in), pick(truth_in)
    tiles_got = lax.ppermute(tiles, CHIP, pairs)
    label = jnp.where(is_owner, labels, lax.ppermute(labels, CHIP, pairs))
    label = lax.dynamic_index_in_dim(label, which, 0, keepdims=False)
    at = jnp.stack([s, z, c, is_owner, label]).astype(jnp.int32)
    move = (Squares if segments == 4 and sizes["z"] == 4 else Plain)(sizes, at)
    cut = Cut(sizes["z"], rows, move.split)

    emb_t = jnp.pad(embed_w.astype(BF16).T, ((0, 0), (0, ECOLS - EROWS)))
    down_t = down_w.astype(BF16).transpose(0, 2, 1)
    wide = jnp.arange(512)
    source = 2 * (wide % 256) + wide // 256
    to_head = (jnp.arange(PIXELS)[:, None] == source[None]) & (wide % 256 < PIXELS // 2)[None]
    head_b = dot(head_w.astype(BF16), to_head.astype(BF16)).astype(BF16)
    head_b = [head_b[:, 128 * j : 128 * j + 128] for j in range(4)]
    qkv_b, out_b, up_b = qkv_w.astype(BF16), out_w.astype(BF16), up_w.astype(BF16)
    bundles = [
        layer_bundle(qkv_b[l], out_b[l], up_b[l], down_t[l], head_b if l == 1 else None)
        for l in range(LAYERS)
    ]

    emb = move.rows(emb_t, ())
    w0, w1 = move.columns(bundles, ())

    lead = embed_w[LEAD:].astype(BF16).astype(F32)
    ada = ada_w.astype(BF16).astype(F32)
    mods = jnp.einsum("gd,ldm->lgm", jax.nn.silu(lead), ada, precision=lax.Precision.HIGHEST)
    mods = jnp.pad(mods.reshape(LAYERS * GROUPS, 6 * D), ((0, 2), (0, 0)))
    mods = move.total(mods)

    vid4 = jnp.pad(jnp.repeat(var_ids, 4), (0, D - PIXELS), constant_values=-1)[None].astype(
        jnp.int32
    )
    h0, agg, x_own, embk = embed(at, tiles, tiles_got, emb, vid4)
    h1, q0, own0, other0, att0, lse0, *kept = block_forward(at, h0, mods, w0)
    q1, own1 = qkv_rows(at, h1, mods, w1)
    other1 = swap(own1, "c", 2, 1)
    truth_got = lax.ppermute(after(truth, emb), CHIP, pairs)
    d_mid, d_att, att1, lse1, g_out, dmod1, loss, *g_first = turn(
        at, cut, h1, q1, own1, other1, mods, w1, truth, truth_got, basis, 1.0 / (micro * dp)
    )

    def attention_grads(at, q, own, other, lse, att, d_att):
        d_q, d_k, d_v, send = attention_back(at, q, own, other, lse, att, d_att)
        return d_q, d_k, d_v, swap(send, "c", 2, 1)

    grads = attention_grads(at, q1, own1, other1, lse1, att1, d_att)
    first = move.core(g_first)
    d_mid, d_att, g_out, dmod1, dmod0, *g_second = between(
        after(at, *first), cut, grads, h1, d_mid, g_out, dmod1, mods, w1, [att0, *kept], w0
    )
    grads = attention_grads(at, q0, own0, other0, lse0, att0, d_att)
    second = move.core(g_second)
    first = move.segment(first)
    g_third = last(
        after(at, *second, *first), cut, grads, h0, d_mid, g_out, dmod0, dmod1, loss, mods, w0, x_own, agg, embk, vid4
    )
    third = move.core(g_third)
    first = move.plane(first)
    second = move.plane(move.segment(second))
    third = move.plane(move.segment(third))
    ends = move.shared([first, second]) + move.shared([third])
    sums = third[1]

    views = []
    for k in range(3):
        w = list(arrays[5 + 7 * k : 12 + 7 * k])
        w[0], w[4] = w[0].T, w[4].transpose(0, 2, 1)
        views += w
    g1, g2, g3, lead_g, squares = gathered(move.order, ends, views[0], views[5], sums)
    if move.split:
        one, two, three = move.across(squares, "z")
        own = (squares + one) + (two + three)
        got = swap(own, "c", 2, 1)
    else:
        own, got = move.total(squares), jnp.zeros_like(squares)
    count = sum(w.size for w in masters) * dp
    rate = 0.02 * math.sqrt(count) / CLIP
    *new, loss_value, norm = updated(at, (g1, g2, g3), lead_g, sums, own, got, views, rate)
    for k in range(3):
        new[7 * k] = new[7 * k].T
        new[7 * k + 4] = new[7 * k + 4].transpose(0, 2, 1)
    return (loss_value.reshape(()), norm.reshape(()), *new)


def solution(mesh):
    segments, dp = mesh.shape["segment"], mesh.shape["dp"]
    sizes = {"s": segments, "z": dp // 2, "c": 2}
    split = Mesh(mesh.devices.reshape(segments, dp // 2, 2), CHIP)
    d = ("z", "c")
    weights = (
        P(None, d),
        P(None, d, None),
        P(None, d, None),
        P(None, d, None),
        P(None, None, d),
        P(None, d, None),
        P(d, None),
    )
    return jax.shard_map(
        lambda *arrays: per_device(sizes, *arrays),
        mesh=split,
        in_specs=(P(d, None, None), P(d, None, None), P(d), P(), P()) + weights * 3,
        out_specs=(P(), P()) + weights * 3,
        check_vma=False,
    )
```

```python
import math

import jax
import jax.numpy as jnp
from jax import lax
from jax.experimental import pallas as pl
from jax.experimental.pallas import tpu as pltpu
from jax.sharding import Mesh, PartitionSpec as P

D = 384
HEADS = 6
HEAD_DIM = 64
FF = 1536
VARS = 69
CHANNELS = 69
LONP = 128
LATP = 8
LAYERS = 2
GROUPS = 3
PIXELS = 276
LEAD = PIXELS + VARS + 1
EROWS = LEAD + GROUPS
ECOLS = 512
EPS = 1e-06
CLIP = 0.001
KEEP = 0.9
BOOST = 20.0
LABEL_LANE = D - 1
HALF = FF // 2

F32 = jnp.float32
BF16 = jnp.bfloat16
CHIP = ("s", "z", "c")


def dot(a, b):
    return jnp.dot(a, b, preferred_element_type=F32)


def dot_nt(a, b):
    return lax.dot_general(a, b, (((1,), (1,)), ((), ())), preferred_element_type=F32)


def dot_tn(a, b):
    return lax.dot_general(a, b, (((0,), (0,)), ((), ())), preferred_element_type=F32)


def parts(x, count):
    out = []
    for step in range(count):
        piece = x.astype(BF16)
        out.append(piece)
        if step < count - 1:
            x = x - piece.astype(F32)
    return out


def normal(v):
    centered = v - jnp.mean(v, axis=-1, keepdims=True)
    inverse = lax.rsqrt(jnp.mean(centered * centered, axis=-1, keepdims=True) + EPS)
    return centered * inverse, inverse


def normal_back(d_x, x, inverse):
    return inverse * (
        d_x - jnp.mean(d_x, axis=-1, keepdims=True) - x * jnp.mean(d_x * x, axis=-1, keepdims=True)
    )


def lane_below(limit, shape):
    return lax.broadcasted_iota(jnp.int32, shape, len(shape) - 1) < limit


def sublane(shape):
    return lax.broadcasted_iota(jnp.int32, shape, 0)


def same_group():
    col = lax.broadcasted_iota(jnp.int32, (D, D), 1)
    return (sublane((D, D)) // 4 == col // 4).astype(BF16)


def chosen_table(vid_ref):
    return (sublane((ECOLS, D)) - PIXELS == vid_ref[...]).astype(BF16)


def first_of_four(shape):
    return sublane(shape) % 4 == 0


def cost(flops, size, exps=0):
    return pl.CostEstimate(flops=int(flops), bytes_accessed=int(size), transcendentals=int(exps))


VMEM = pl.BlockSpec(memory_space=pltpu.VMEM)
SMEM = pl.BlockSpec(memory_space=pltpu.SMEM)
ANY = pl.BlockSpec(memory_space=pl.ANY)
CHUNK = 256
AT_S, AT_Z, AT_C, AT_OWN, AT_WHICH, AT_LABEL = range(6)


def call(kernel, name, outs, inputs, estimate, scratch=(), limit=24, in_space=VMEM, out_spaces=None):
    return pl.pallas_call(
        kernel,
        in_specs=[SMEM] + [in_space] * (len(inputs) - 1),
        out_specs=out_spaces or [VMEM] * len(outs),
        out_shape=[jax.ShapeDtypeStruct(shape, kind) for shape, kind in outs],
        scratch_shapes=list(scratch),
        compiler_params=pltpu.CompilerParams(vmem_limit_bytes=limit << 20),
        cost_estimate=estimate,
        name=name,
    )(*inputs)


def rows_at(index, size):
    return pl.ds(pl.multiple_of(index * size, size), size)


def after(x, *others):
    return lax.optimization_barrier((x, others))[0]


def column_sum(v):
    return jnp.sum(v, axis=0, keepdims=True)


class Cut:
    def __init__(self, pairs, rows, split):
        self.pairs, self.rows, self.split = pairs, rows, split
        self.outputs = 2
        self.buffer = None

    def shapes(self, width, extra=False):
        if self.split:
            return [((4 * self.pairs + extra, self.rows, width), BF16)] * 2
        return [((4, D, width), BF16), ((1, 48, width), BF16)]

    def scratch(self, width):
        return [pltpu.VMEM((D, width), F32)]

    def on(self, buffer):
        other = Cut(self.pairs, self.rows, self.split)
        other.buffer = buffer
        return other

    def write(self, at_ref, outs, quarter, lane, value):
        width = value.shape[-1]
        cols = slice(lane, lane + width)
        if not self.split:
            outs[0][quarter, :, cols] = value.astype(BF16)
            return
        self.buffer[:, :width] = value
        core = at_ref[AT_C]
        for z in range(self.pairs):
            for ref, which in ((outs[0], core), (outs[1], 1 - core)):
                part = self.buffer[rows_at(2 * z + which, self.rows), :width]
                ref[quarter * self.pairs + z, :, cols] = part.astype(BF16)

    def write_extra(self, outs, value):
        value = value.astype(BF16)
        if self.split:
            outs[0][4 * self.pairs] = value
            outs[1][4 * self.pairs] = value
        else:
            outs[1][0] = value


def embed_kernel(
    at_ref, own_ref, got_ref, emb_ref, vid_ref,
    out_ref, agg_ref, x_ref, embk_ref, x_sc, bases_sc,
):
    tokens = own_ref.shape[1]
    half = tokens // 2
    emb = emb_ref[...]
    embk_ref[...] = emb.astype(F32).T.astype(BF16)
    query = jnp.broadcast_to(emb[:, LEAD - 1 : LEAD].astype(F32), (D, 128)).astype(BF16)
    by_row = dot_tn(emb, query)
    table = chosen_table(vid_ref)
    inside = sublane((D, 1)) < PIXELS
    proj = jnp.where(inside, by_row[:D, :1], 0.0)
    base = sum(dot_tn(table, p) for p in parts(by_row, 3))[:, :1]
    lane = lax.broadcasted_iota(jnp.int32, (D, D), 1)
    bases_sc[...] = jnp.where(lane % 4 == 0, dot(emb, table), 0.0).astype(BF16)
    group = same_group()
    x_sc[...] = jnp.zeros_like(x_sc)
    x_sc[:PIXELS] = jnp.where(at_ref[AT_OWN] == 1, own_ref[...], got_ref[...])

    def step(i, carry):
        here = rows_at(i, CHUNK)
        source = lax.rem(i * CHUNK + at_ref[AT_C] * half, tokens)
        packed = x_sc[:, pl.ds(pl.multiple_of(source, CHUNK), CHUNK)]
        x = packed.astype(F32)
        scores = sum(dot(group, p) for p in parts(x * proj, 3)) + base
        scores = jnp.where(inside, scores * D ** (-0.5), -1e30)
        e = jnp.exp(scores - jnp.max(scores, axis=0, keepdims=True))
        agg = e * (4.0 / column_sum(e))

        agg_ref[:, here] = agg
        x_ref[:, here] = packed
        total = dot(emb_ref[:, :D], (agg * x).astype(BF16))
        for p in parts(agg, 2):
            total = total + dot(bases_sc[...], p)
        out_ref[here, :] = total.T.astype(BF16)
        return carry

    lax.fori_loop(0, tokens // CHUNK, step, 0)


def embed(at, own, got, emb, vid4):
    tokens = own.shape[1]
    return call(
        embed_kernel,
        "embed",
        [
            ((tokens, D), BF16),
            ((D, tokens), F32),
            ((D, tokens), BF16),
            ((ECOLS, D), BF16),
        ],
        [at, own, got, emb, vid4],
        cost(2e9, 2e6),
        [pltpu.VMEM((D, tokens), BF16), pltpu.VMEM((D, D), BF16)],
    )


def embed_back(dh, x_ref, agg_ref, embk_ref, vid_ref):
    x = x_ref[...].astype(F32)
    agg = agg_ref[...]
    embk = embk_ref[:D]
    table = chosen_table(vid_ref)
    bases = dot_tn(table, embk_ref[...]).astype(BF16)
    query = embk_ref[LEAD - 1 : LEAD, :].astype(F32)
    g_patch = dot((agg * x).astype(BF16), dh)
    d_agg = dot_nt(bases, dh)
    group = same_group()
    for p in parts(dot_nt(embk, dh) * x, 2):
        d_agg = d_agg + dot(group, p)
    inner = 0.25 * column_sum(agg * d_agg)
    d_scores = agg * (d_agg - inner) * D ** (-0.5)
    d_proj = jnp.sum(d_scores * x, axis=-1, keepdims=True)
    d_base = jnp.sum(d_scores, axis=-1, keepdims=True)
    d_base = jnp.where(first_of_four(d_base.shape), d_base, 0.0)
    d_bases = d_base * query
    for p in parts(jnp.where(first_of_four((D, 1)), agg, 0.0), 2):
        d_bases = d_bases + dot(p, dh)
    g_table = sum(dot(table, p) for p in parts(d_bases, 2))
    d_query = column_sum(embk.astype(F32) * d_proj) + column_sum(bases.astype(F32) * d_base)
    total = g_table + jnp.where(sublane((ECOLS, 1)) == LEAD - 1, d_query, 0.0)
    return jnp.concatenate([total[:D] + g_patch + d_proj * query, total[D:]], axis=0)


def mod_row(mods_ref, at_ref, layer, index):
    row = 8 * (layer * GROUPS + at_ref[AT_LABEL]) + index
    return mods_ref[pl.ds(row, 1), :D]


def first_norm(h, mods_ref, at_ref, layer):
    x, inverse = normal(h.astype(F32))
    scale = 1.0 + mod_row(mods_ref, at_ref, layer, 1)
    return (x * scale + mod_row(mods_ref, at_ref, layer, 0)).astype(BF16), x, inverse


def pair_masks():
    low = lane_below(HEAD_DIM, (1, 128))
    return low, jnp.logical_not(low)


def both(own_ref, other_ref, lane):
    here = slice(lane, lane + 128)
    return jnp.concatenate([own_ref[:, here], other_ref[:, here]])


def attend(here, q_ref, own_ref, other_ref, att_ref, lse_ref):
    zero = jnp.zeros((), BF16)
    lane = lax.broadcasted_iota(jnp.int32, (CHUNK, 128), 1)
    sums = jnp.zeros((CHUNK, 128), F32)
    for pair in range(HEADS // 2):
        a = 128 * pair
        q = q_ref[here, a : a + 128] * 0.125
        keys = both(own_ref, other_ref, a)
        vals = both(own_ref, other_ref, D + a)
        mixed = jnp.zeros((CHUNK, 128), F32)
        for which, mask in enumerate(pair_masks()):
            scores = dot_nt(q, jnp.where(mask, keys, zero))
            top = jnp.max(scores, axis=-1, keepdims=True)
            e = jnp.exp(scores - top)
            total = jnp.sum(e, axis=-1, keepdims=True)
            mixed = mixed + dot(e.astype(BF16), jnp.where(mask, vals, zero)) * (1.0 / total)
            sums = jnp.where(lane == 2 * pair + which, top + jnp.log(total), sums)
        att_ref[here, a : a + 128] = mixed.astype(BF16)
    lse_ref[here, :] = sums


def gelu_and_slope(u):
    k = math.sqrt(2.0 / math.pi)
    t = jnp.tanh(k * (u + 0.044715 * (u * u * u)))
    cdf = 0.5 * (1.0 + t)
    return u * cdf, cdf + 0.5 * u * (1.0 - t * t) * k * (1.0 + 3 * 0.044715 * (u * u))


def feed_forward(here, h, one, mods_ref, at_ref, layer, w_ref, act_ref, slope_ref, n2_ref=None):
    middle = h.astype(F32) + mod_row(mods_ref, at_ref, layer, 2) * one
    x, _ = normal(middle)
    scale = 1.0 + mod_row(mods_ref, at_ref, layer, 4)
    n2 = (x * scale + mod_row(mods_ref, at_ref, layer, 3)).astype(BF16)
    if n2_ref is not None:
        n2_ref[here, :] = n2
    two = jnp.zeros((CHUNK, D), F32)
    for j in range(2):
        part = slice(HALF * j, HALF * (j + 1))
        act, slope = gelu_and_slope(dot(n2, w_ref[j, :, D : 3 * D]))
        slope_ref[here, part] = slope.astype(slope_ref.dtype)
        act = act.astype(BF16)
        act_ref[here, part] = act
        two = two + dot_nt(act, w_ref[2 + j, :, D : 3 * D])
    return middle, two, middle + mod_row(mods_ref, at_ref, layer, 5) * two


def feed_back(
    here, d_out, one, two, middle, slope_ref, mods_ref, at_ref, layer, w_ref,
    dunits_ref, dtwo_ref, done_ref, dmid_ref, datt_ref, dmod_ref, n2_ref=None,
):
    d_out = d_out.astype(F32)
    d_two = (mod_row(mods_ref, at_ref, layer, 5) * d_out).astype(BF16)
    dtwo_ref[here, :] = d_two
    d_n2 = jnp.zeros(d_out.shape, F32)
    for j in range(2):
        part = slice(HALF * j, HALF * (j + 1))
        slope = slope_ref[here, part].astype(F32)
        d_units = (slope * dot(d_two, w_ref[2 + j, :, D : 3 * D])).astype(BF16)
        dunits_ref[here, part] = d_units
        d_n2 = d_n2 + dot_nt(d_units, w_ref[j, :, D : 3 * D])
    x, inverse = normal(middle)
    scale = 1.0 + mod_row(mods_ref, at_ref, layer, 4)
    if n2_ref is not None:
        n2_ref[here, :] = (x * scale + mod_row(mods_ref, at_ref, layer, 3)).astype(BF16)
    d_mid = d_out + normal_back(d_n2 * scale, x, inverse)
    dmid_ref[here, :] = d_mid
    d_one = (mod_row(mods_ref, at_ref, layer, 2) * d_mid).astype(BF16)
    done_ref[here, :] = d_one
    datt_ref[here, :] = dot_nt(d_one, w_ref[3, :, :D]).astype(BF16)
    dmod_ref[2:3] += column_sum(d_mid * one)
    dmod_ref[3:4] += column_sum(d_n2)
    dmod_ref[4:5] += column_sum(d_n2 * x)
    dmod_ref[5:6] += column_sum(d_out * two)


def feed_gradients(at_ref, cut, outs, lane, n2_ref, dunits_ref, dtwo_ref, act_ref):
    for j in range(2):
        part = slice(HALF * j, HALF * (j + 1))
        cut.write(at_ref, outs, j, lane, dot_tn(n2_ref[...], dunits_ref[:, part]))
        cut.write(at_ref, outs, 2 + j, lane, dot_tn(dtwo_ref[...], act_ref[:, part]))


def rows_scratch(count, widths):
    return [pltpu.VMEM((count, width), BF16) for width in widths]


def block_kernel(
    at_ref, h_ref, mods_ref, w_ref,
    out_ref, q_out, own_out, other_out, att_out, lse_out, one_out, mid_out, slope_out, act_out, two_out,
    q_ref, own_ref, other_ref, att_ref, lse_ref, one_ref, mid_ref, slope_ref, act_ref, two_ref, sems,
):
    count = out_ref.shape[0]
    steps = count // CHUNK

    def project(i, carry):
        here = rows_at(i, CHUNK)
        normed, _, _ = first_norm(h_ref[here, :], mods_ref, at_ref, 0)
        q_ref[here, :] = dot(normed, w_ref[0, :, :D]).astype(BF16)
        for j in range(2):
            own_ref[here, D * j : D * (j + 1)] = dot(normed, w_ref[j + 1, :, :D]).astype(BF16)
        return carry

    lax.fori_loop(0, steps, project, 0)

    def project_other(i, carry):
        here = rows_at(i, CHUNK)
        normed, _, _ = first_norm(h_ref[rows_at(i + steps, CHUNK), :], mods_ref, at_ref, 0)
        for j in range(2):
            other_ref[here, D * j : D * (j + 1)] = dot(normed, w_ref[j + 1, :, :D]).astype(BF16)
        return carry

    lax.fori_loop(0, steps, project_other, 0)
    early = [
        pltpu.make_async_copy(ref, out, sems.at[2, i])
        for i, (ref, out) in enumerate(((q_ref, q_out), (own_ref, own_out), (other_ref, other_out)))
    ]
    for copy in early:
        copy.start()
    kept = (
        (att_ref, att_out), (lse_ref, lse_out), (one_ref, one_out), (mid_ref, mid_out),
        (slope_ref, slope_out), (act_ref, act_out), (two_ref, two_out),
    )

    def copies(i):
        here = rows_at(i, CHUNK)
        return [
            pltpu.make_async_copy(ref.at[here], out.at[here], sems.at[i, k])
            for k, (ref, out) in enumerate(kept)
        ]

    def step(i, carry):
        here = rows_at(i, CHUNK)
        attend(here, q_ref, own_ref, other_ref, att_ref, lse_ref)
        one = dot(att_ref[here, :], w_ref[3, :, :D])
        one_ref[here, :] = one.astype(BF16)
        middle, two, out = feed_forward(
            here, h_ref[here, :], one, mods_ref, at_ref, 0, w_ref, act_ref, slope_ref
        )
        mid_ref[here, :] = middle
        two_ref[here, :] = two.astype(BF16)
        out_ref[here, :] = out.astype(BF16)
        for copy in copies(i):
            copy.start()
        return carry

    lax.fori_loop(0, steps, step, 0)
    for copy in early:
        copy.wait()
    for i in range(steps):
        for copy in copies(i):
            copy.wait()


def block_forward(at, h, mods, weights):
    count = h.shape[0] // 2
    kept = [(D, BF16), (2 * D, BF16), (2 * D, BF16), (D, BF16), (128, F32), (D, BF16), (D, F32)]
    kept += [(FF, BF16), (FF, BF16), (D, BF16)]
    kept = [((count, width), kind) for width, kind in kept]
    return call(
        block_kernel,
        "block_forward",
        [((count, D), BF16)] + kept,
        [at, h, mods, weights],
        cost(2e9, 2e6),
        [pltpu.VMEM(shape, kind) for shape, kind in kept] + [pltpu.SemaphoreType.DMA((3, 7))],
        limit=28,
        out_spaces=[VMEM] + [ANY] * len(kept),
    )


def qkv_kernel(at_ref, h_ref, mods_ref, w_ref, q_ref, kv_ref):
    def step(i, carry):
        here = rows_at(i, CHUNK)
        normed, _, _ = first_norm(h_ref[here, :], mods_ref, at_ref, 1)
        q_ref[here, :] = dot(normed, w_ref[0, :, :D]).astype(BF16)
        for j in range(2):
            kv_ref[here, D * j : D * (j + 1)] = dot(normed, w_ref[j + 1, :, :D]).astype(BF16)
        return carry

    lax.fori_loop(0, q_ref.shape[0] // CHUNK, step, 0)


def qkv_rows(at, h, mods, weights):
    count = h.shape[0]
    return call(
        qkv_kernel,
        "qkv_rows",
        [((count, D), BF16), ((count, 2 * D), BF16)],
        [at, h, mods, weights],
        cost(1e9, 3e6),
    )


def turn_kernel(
    at_ref, h_ref, q_ref, own_ref, other_ref, mods_ref, w_ref, truth_ref, got_ref, basis_ref,
    dmid_ref, datt_ref, att_ref, lse_ref, gout_ref, dmod_ref, loss_ref, keep_ref, send_ref,
    act_ref, dunits_ref, dtwo_ref, n2_ref, done_ref, flat_ref, dpred_ref, true_ref, slope_ref,
    basis_sc, buffer, *, seed, cut,
):
    count = h_ref.shape[0]
    outs = (keep_ref, send_ref)
    entries = LATP * CHANNELS * 2 * LONP
    dmod_ref[...] = jnp.zeros_like(dmod_ref)
    loss_ref[...] = jnp.zeros_like(loss_ref)
    row = lax.broadcasted_iota(jnp.int32, (PIXELS, 256), 0)
    col = lax.broadcasted_iota(jnp.int32, (PIXELS, 256), 1)
    lanes = rows_at(at_ref[AT_C], count)
    truth = jnp.where(at_ref[AT_OWN] == 1, truth_ref[:, lanes], got_ref[:, lanes])
    for b in range(2):
        picked = dot_tn(truth, (row == 2 * col + b).astype(BF16))
        true_ref[:, 256 * b : 256 * b + 256] = picked.astype(BF16)
    to = lax.broadcasted_iota(jnp.int32, (256, 256), 0)
    source = lax.broadcasted_iota(jnp.int32, (256, 256), 1)
    order = (source == 2 * (to % LONP) + to // LONP).astype(BF16)
    for i, p in enumerate(parts(basis_ref[...], 2)):
        basis_sc[i] = dot(order, p).astype(BF16)

    def step(i, carry):
        here = rows_at(i, CHUNK)
        attend(here, q_ref, own_ref, other_ref, att_ref, lse_ref)
        one = dot(att_ref[here, :], w_ref[3, :, :D])
        middle, two, h2 = feed_forward(
            here, h_ref[here, :], one, mods_ref, at_ref, 1, w_ref, act_ref, slope_ref, n2_ref
        )
        x, inverse = normal(h2.astype(BF16).astype(F32))
        flat = x.astype(BF16)
        flat_ref[here, :] = flat
        hw = [w_ref[j, :, 3 * D : 3 * D + 128] for j in range(4)]
        pred = [dot(flat, w) for w in hw]
        pred = [jnp.concatenate(pred[:2], axis=-1), jnp.concatenate(pred[2:], axis=-1)]
        hi, lo = basis_sc[0], basis_sc[1]
        grads = [[], []]
        loss = jnp.zeros((1, 1), F32)
        for p in range(CHUNK // LONP):
            part = slice(p * LONP, (p + 1) * LONP)
            fine = rows_at(i * (CHUNK // LONP) + p, LONP)
            seen = parts(jnp.concatenate([pred[0][part], pred[1][part]], axis=0), 2)
            waves = dot_tn(hi, seen[0]) + (dot_tn(hi, seen[1]) + dot_tn(lo, seen[0]))
            want = jnp.concatenate([true_ref[fine, :256], true_ref[fine, 256:]], axis=0)
            target = dot_tn(hi, want) + dot_tn(lo, want)
            top, low = waves[:LONP], waves[LONP:]
            gap = (top * top + low * low) - (
                target[:LONP] * target[:LONP] + target[LONP:] * target[LONP:]
            )
            loss = loss + jnp.sum(gap * gap, axis=(0, 1), keepdims=True)
            scaled = gap * (4.0 * seed / entries)
            d_waves = parts(jnp.concatenate([scaled * top, scaled * low], axis=0), 2)
            d_seen = dot(hi, d_waves[0]) + (dot(hi, d_waves[1]) + dot(lo, d_waves[0]))
            d_seen = d_seen.astype(BF16)
            grads[0].append(d_seen[:LONP])
            grads[1].append(d_seen[LONP:])
        loss_ref[...] += jnp.broadcast_to(loss * (seed / entries), loss_ref.shape)
        d_flat = jnp.zeros((CHUNK, D), F32)
        for b in range(2):
            whole = jnp.concatenate(grads[b], axis=0)
            dpred_ref[here, 256 * b : 256 * b + 256] = whole
            for j in range(2):
                d_flat = d_flat + dot_nt(whole[:, 128 * j : 128 * j + 128], hw[2 * b + j])
        d_h2 = normal_back(d_flat, x, inverse).astype(BF16)
        feed_back(
            here, d_h2, one, two, middle, slope_ref, mods_ref, at_ref, 1, w_ref,
            dunits_ref, dtwo_ref, done_ref, dmid_ref, datt_ref, dmod_ref,
        )
        return carry

    lax.fori_loop(0, count // CHUNK, step, 0)
    cut = cut.on(buffer)
    feed_gradients(at_ref, cut, outs, 0, n2_ref, dunits_ref, dtwo_ref, act_ref)
    for j in range(4):
        cut.write(at_ref, outs, j, HALF, dot_tn(flat_ref[...], dpred_ref[:, 128 * j : 128 * j + 128]))
    gout_ref[...] = dot_tn(att_ref[...], done_ref[...])


def turn(at, cut, h, q, own, other, mods, weights, truth, got, basis, seed):
    count = h.shape[0]
    return call(
        lambda *refs: turn_kernel(*refs, seed=seed, cut=cut),
        "turn",
        [
            ((count, D), F32),
            ((count, D), BF16),
            ((count, D), BF16),
            ((count, 128), F32),
            ((D, D), F32),
            ((8, D), F32),
            ((8, 128), F32),
        ]
        + cut.shapes(HALF + 128),
        [at, h, q, own, other, mods, weights, truth, got, basis],
        cost(4e9, 4e6),
        rows_scratch(count, [FF, FF, D, D, D, D, 512, 512])
        + [pltpu.VMEM((count, FF), F32), pltpu.VMEM((2, 256, 256), BF16)]
        + cut.scratch(HALF),
        limit=32,
    )


def attention_back_kernel(
    at_ref, q_ref, own_ref, other_ref, lse_ref, att_ref, datt_ref, *refs, start, steps, more, finish,
):
    zero = jnp.zeros((), BF16)
    count = own_ref.shape[0]
    if more:
        dk_in, dv_in, refs = refs[0], refs[1], refs[2:]
    dq_ref, *outs = refs
    dk_sc, dv_sc = outs[-2:] if finish else outs[:2]
    dk_sc[...] = dk_in[...] if more else jnp.zeros_like(dk_sc)
    dv_sc[...] = dv_in[...] if more else jnp.zeros_like(dv_sc)

    def step(i, carry):
        rows = rows_at(i + start, CHUNK)
        for pair in range(HEADS // 2):
            a = 128 * pair
            here = slice(a, a + 128)
            q = q_ref[rows, here]
            d_att = datt_ref[rows, here]
            keys = both(own_ref, other_ref, a)
            vals = both(own_ref, other_ref, D + a)
            dots = d_att.astype(F32) * att_ref[rows, here].astype(F32)
            d_q = jnp.zeros((CHUNK, 128), F32)
            d_k = jnp.zeros((keys.shape[0], 128), F32)
            d_v = jnp.zeros((keys.shape[0], 128), F32)
            for which, mask in enumerate(pair_masks()):
                head = 2 * pair + which
                k = jnp.where(mask, keys, zero)
                v = jnp.where(mask, vals, zero)
                inner = jnp.sum(jnp.where(mask, dots, 0.0), axis=-1, keepdims=True)
                probs = jnp.exp(dot_nt(q * 0.125, k) - lse_ref[rows, head : head + 1])
                d_scores = (probs * (dot_nt(d_att, v) - inner)).astype(BF16)
                d_q = d_q + dot(d_scores, k)
                d_k = d_k + dot_tn(d_scores, jnp.where(mask, q, zero))
                d_v = d_v + dot_tn(probs.astype(BF16), jnp.where(mask, d_att, zero))
            dq_ref[rows_at(i, CHUNK), here] = (d_q * 0.125).astype(BF16)
            dk_sc[:, here] += d_k * 0.125
            dv_sc[:, here] += d_v
        return carry

    lax.fori_loop(0, steps, step, 0)
    if finish:
        dk_ref, dv_ref, dk_send, dv_send = outs[:4]
        dk_ref[...] = dk_sc[:count]
        dv_ref[...] = dv_sc[:count]
        dk_send[...] = dk_sc[count:].astype(BF16)
        dv_send[...] = dv_sc[count:].astype(BF16)


def attention_back(at, q, own, other, lse, att, d_att, start=0, steps=2, carried=(), finish=False):
    count = q.shape[0]
    full = ((2 * count, D), F32)
    outs = [((count, D), F32)] * 2 + [((count, D), BF16)] * 2 if finish else [full] * 2
    options = dict(start=start, steps=steps, more=bool(carried), finish=finish)
    return call(
        lambda *refs: attention_back_kernel(*refs, **options),
        "attention_back",
        [((CHUNK * steps, D), BF16)] + outs,
        [at, q, own, other, lse, att, d_att, *carried],
        cost(1e9 * steps, 1e6),
        [pltpu.VMEM(*full)] * 2 if finish else (),
    )


def qkv_back(
    at_ref, cut, outs, lane, layer, d_q, d_k, d_v, h_ref, dmid_ref, gout_ref, mods_ref, w_ref,
):
    count, rows = d_q.shape[0], d_k.shape[0]
    normed, x, inverse = first_norm(h_ref[:rows], mods_ref, at_ref, layer)
    first = dot_nt(d_q, w_ref[0, :, :D])
    rest = dot_nt(d_k, w_ref[1, :, :D]) + dot_nt(d_v, w_ref[2, :, :D])
    if rows > count:
        d_n = jnp.concatenate([rest[:count] + first, rest[count:]], axis=0)
    else:
        d_n = rest + first
    cut.write(at_ref, outs, 0, lane, dot_tn(normed[:count], d_q))
    cut.write(at_ref, outs, 1, lane, dot_tn(normed, d_k))
    cut.write(at_ref, outs, 2, lane, dot_tn(normed, d_v))
    cut.write(at_ref, outs, 3, lane, gout_ref[...])
    scale = 1.0 + mod_row(mods_ref, at_ref, layer, 1)
    d_h = normal_back(d_n * scale, x, inverse)
    if rows > count:
        d_h = jnp.concatenate([d_h[:count] + dmid_ref[...], d_h[count:]], axis=0)
    else:
        d_h = d_h + dmid_ref[...]
    return d_h.astype(BF16), column_sum(d_n), column_sum(d_n * x)


def between_kernel(
    at_ref, dq_ref, dk_ref, dv_ref, dk_got, dv_got, h_ref, dmid_ref, gout_ref, dmod_ref, mods_ref, w1_ref,
    one_ref, two_ref, mid_ref, slope_ref, act_ref, att_ref, w0_ref,
    dmid_out, datt_out, gout_out, dmod_out, dmod_next, keep_ref, send_ref,
    dh_sc, dunits_ref, dtwo_ref, n2_ref, done_ref, buffer, *, cut,
):
    outs = (keep_ref, send_ref)
    cut = cut.on(buffer)
    d_k = (dk_ref[...] + dk_got[...].astype(F32)).astype(BF16)
    d_v = (dv_ref[...] + dv_got[...].astype(F32)).astype(BF16)
    d_h, shift, scale = qkv_back(
        at_ref, cut, outs, 0, 1, dq_ref[...], d_k, d_v, h_ref, dmid_ref, gout_ref, mods_ref, w1_ref,
    )
    dmod_out[...] = dmod_ref[...]
    dmod_out[0:1] = shift
    dmod_out[1:2] = scale
    dh_sc[...] = d_h
    dmod_next[...] = jnp.zeros_like(dmod_next)

    def step(i, carry):
        here = rows_at(i, CHUNK)
        feed_back(
            here, dh_sc[here, :], one_ref[here, :].astype(F32), two_ref[here, :].astype(F32),
            mid_ref[here, :], slope_ref, mods_ref, at_ref, 0, w0_ref,
            dunits_ref, dtwo_ref, done_ref, dmid_out, datt_out, dmod_next, n2_ref,
        )
        return carry

    lax.fori_loop(0, dh_sc.shape[0] // CHUNK, step, 0)
    feed_gradients(at_ref, cut, outs, D, n2_ref, dunits_ref, dtwo_ref, act_ref)
    gout_out[...] = dot_tn(att_ref[...], done_ref[...])


def between(at, cut, grads, h, d_mid, g_out, dmod, mods, w1, kept, w0):
    att, one, mid, slope, act, two = kept
    count = d_mid.shape[0]
    return call(
        lambda *refs: between_kernel(*refs, cut=cut),
        "between",
        [((count, D), F32), ((count, D), BF16), ((D, D), F32), ((8, D), F32), ((8, D), F32)]
        + cut.shapes(D + HALF),
        [at, *grads, h, d_mid, g_out, dmod, mods, w1, one, two, mid, slope, act, att, w0],
        cost(1e9, 1e6),
        rows_scratch(count, [D, FF, D, D, D]) + cut.scratch(HALF),
        limit=28,
    )


def last_kernel(
    at_ref, dqa_ref, dqb_ref, dk_ref, dv_ref, h_ref, dmid_ref, gout_ref, dmod0_ref, dmod1_ref, loss_ref,
    mods_ref, w_ref, x_ref, agg_ref, embk_ref, vid_ref, keep_ref, send_ref, sums_sc, buffer, *, cut,
):
    outs = (keep_ref, send_ref)
    cut = cut.on(buffer)
    d_q = jnp.concatenate([dqa_ref[...], dqb_ref[...]], axis=0)
    d_k, d_v = dk_ref[...].astype(BF16), dv_ref[...].astype(BF16)
    d_h, shift, scale = qkv_back(
        at_ref, cut, outs, 0, 0, d_q, d_k, d_v, h_ref, dmid_ref, gout_ref, mods_ref, w_ref,
    )
    sums_sc[...] = jnp.zeros_like(sums_sc)
    for group in range(GROUPS):
        hot = (at_ref[AT_LABEL] == group).astype(F32)
        for layer, ref in enumerate((dmod0_ref, dmod1_ref)):
            at = 8 * (GROUPS * layer + group)
            sums_sc[at : at + 8, :D] = ref[...] * hot
        sums_sc[8 * group : 8 * group + 1, :D] = shift * hot
        sums_sc[8 * group + 1 : 8 * group + 2, :D] = scale * hot
    loss = loss_ref[0:1, 0:1]
    top = loss.astype(BF16).astype(F32)
    sums_sc[6:7, :] = jnp.broadcast_to(top, (1, ECOLS))
    sums_sc[7:8, :] = jnp.broadcast_to(loss - top, (1, ECOLS))
    cut.write_extra(outs, sums_sc[...])
    g = embed_back(d_h, x_ref, agg_ref, embk_ref, vid_ref).T
    for j in range(4):
        cut.write(at_ref, outs, j, D, g[:, 128 * j : 128 * j + 128])


def last(at, cut, grads, h, d_mid, g_out, dmod0, dmod1, loss, mods, w0, x, agg, embk, vid4):
    return call(
        lambda *refs: last_kernel(*refs, cut=cut),
        "last",
        cut.shapes(ECOLS, True),
        [at, *grads, h, d_mid, g_out, dmod0, dmod1, loss, mods, w0, x, agg, embk, vid4],
        cost(1e9, 1e6),
        [pltpu.VMEM((48, ECOLS), F32)] + cut.scratch(D),
        limit=28,
    )


def swap(x, axis, size, by):
    return lax.ppermute(x, axis, [(i, i ^ by) for i in range(size)])


def place_kernel(at_ref, *refs, columns, rows):
    out_ref, sems = refs[-2], refs[-1]
    inputs = refs[:-2]
    s, z, c = at_ref[AT_S], at_ref[AT_Z], at_ref[AT_C]
    copies = []
    index = 0
    for jc in range(2):
        for js in range(columns):
            source = inputs[jc * columns + js]
            for jz in range(source.shape[0]):
                at = rows_at((z ^ jz) * 2 + (c ^ jc), rows)
                target = out_ref.at[s ^ js, at] if columns > 1 else out_ref.at[at]
                copies.append(pltpu.make_async_copy(source.at[jz], target, sems.at[index]))
                index += 1
    for copy in copies:
        copy.start()
    for copy in copies:
        copy.wait()


def placed(at, own, got):
    columns, (zs, rows, width) = len(own), own[0].shape
    full = (zs * 2 * rows, width)
    shape = (columns,) + full if columns > 1 else full
    return call(
        lambda *refs: place_kernel(*refs, columns=columns, rows=rows),
        "placed",
        [(shape, BF16)],
        [at, *own, *got],
        cost(0, 4 * math.prod(shape)),
        [pltpu.SemaphoreType.DMA((2 * columns * zs,))],
        limit=4,
        in_space=ANY,
    )[0]


def first_kernel(at_ref, own_ref, got_ref, emb_ref, mods_ref, out_ref):
    rows = own_ref.shape[2]
    total = jnp.zeros((rows, D), F32)
    for jc, ref in enumerate((own_ref, got_ref)):
        for jz in range(ref.shape[0]):
            row = (at_ref[AT_Z] ^ jz) * 2 + (at_ref[AT_C] ^ jc)
            emb_ref[rows_at(row, rows), :] = ref[jz, 0]
            total = total + (ref[jz, 1, :, :D].astype(F32) + ref[jz, 2, :, :D].astype(F32))
    mods_ref[...] = total
    for i in range(AT_LABEL):
        out_ref[i] = at_ref[i]
    labels = jnp.where(
        at_ref[AT_OWN] == 1, own_ref[0, 1, 0:8, 0:128].astype(F32), got_ref[0, 1, 0:8, 0:128].astype(F32)
    )
    picked = sublane((8, 128)) == 6 + at_ref[AT_WHICH]
    out_ref[AT_LABEL] = jnp.max(jnp.where(picked, labels, 0.0)).astype(jnp.int32)


def pack_kernel(
    at_ref, labels_ref, emb_ref, qkv_ref, out_ref, up_ref, down_ref, ada_ref, head_ref,
    first_ref, zero_ref, one_ref,
):
    rows = emb_ref.shape[0]
    first_ref[...] = jnp.zeros_like(first_ref)
    first_ref[0, :rows, :EROWS] = emb_ref[...].astype(BF16)
    silu, _ = lead_parts(emb_ref)
    for layer in range(LAYERS):
        for i in range(6):
            ada = ada_ref[layer, :, D * i : D * (i + 1)].astype(BF16).astype(F32)
            for g in range(GROUPS):
                at = 8 * (GROUPS * layer + g) + i
                value = column_sum(silu[:, g : g + 1] * ada)
                top = value.astype(BF16)
                first_ref[1, at : at + 1, :D] = top
                first_ref[2, at : at + 1, :D] = (value - top.astype(F32)).astype(BF16)
    for i in range(2):
        label = jnp.full((1, D), labels_ref[i], jnp.int32).astype(F32).astype(BF16)
        first_ref[1, 6 + i : 7 + i, :D] = label
    col = lax.broadcasted_iota(jnp.int32, (PIXELS, 128), 0)
    lane = lax.broadcasted_iota(jnp.int32, (PIXELS, 128), 1)
    for j in range(4):

        def fill(j=j):
            for layer, ref in enumerate((zero_ref, one_ref)):
                at = 0 if ref.shape[0] == 1 else j
                part = qkv_ref[layer, :, D * j : D * (j + 1)] if j < 3 else out_ref[layer]
                ref[at, :, :D] = part.astype(BF16)
                source = (up_ref if j < 2 else down_ref)[layer]
                ref[at, :, D : 3 * D] = source[:, HALF * (j % 2) : HALF * (j % 2 + 1)].astype(BF16)
            wide = lane + 128 * (j % 2)
            pick = jnp.logical_and(col == 2 * wide + j // 2, wide < PIXELS // 2).astype(BF16)
            at = 0 if one_ref.shape[0] == 1 else j
            one_ref[at, :, 3 * D :] = dot(head_ref[...].astype(BF16), pick).astype(BF16)

        if zero_ref.shape[0] == 4:
            fill()
        else:
            pl.when(at_ref[AT_S] == j)(fill)


def packed(at, labels, weights, quarters):
    rows = weights[0].shape[0]
    inputs = [at, labels, *weights]
    return pl.pallas_call(
        pack_kernel,
        in_specs=[SMEM, SMEM] + [VMEM] * 7,
        out_specs=[VMEM] * 3,
        out_shape=[
            jax.ShapeDtypeStruct((3, 48, ECOLS), BF16),
            jax.ShapeDtypeStruct((quarters, rows, 3 * D), BF16),
            jax.ShapeDtypeStruct((quarters, rows, 3 * D + 128), BF16),
        ],
        compiler_params=pltpu.CompilerParams(vmem_limit_bytes=16 << 20),
        cost_estimate=cost(0, 1e6),
        name="packed",
    )(*inputs)


def two_rows(v):
    loss = v[6:7] + v[7:8]
    top = loss.astype(BF16).astype(F32)
    row = sublane(v.shape)
    return jnp.where(row == 6, top, jnp.where(row == 7, loss - top, v)).astype(BF16)


class Rows:
    def __init__(self, refs, cuts):
        self.refs, self.cuts = refs, cuts

    def fill(self, out):
        for ref, a, b in zip(self.refs, self.cuts[:-1], self.cuts[1:]):
            out[a:b] = ref[...]


def add_core_kernel(at_ref, kept_ref, pieces, own_ref, *refs):
    sends, got_ref = refs[:3], refs[3]
    pieces.fill(got_ref)
    zs = 4
    for j in range(4):
        here = pl.ds((at_ref[AT_S] ^ j) * zs, zs)
        value = kept_ref[here].astype(F32) + got_ref[here].astype(F32)
        if j == 0:
            own_ref[:zs] = value
        else:
            sends[j - 1][:zs] = value.astype(BF16)
    if own_ref.shape[0] > zs:
        value = two_rows(kept_ref[4 * zs].astype(F32) + got_ref[4 * zs].astype(F32))
        own_ref[zs] = value.astype(F32)
        for send in sends:
            send[zs] = value


def summed(refs, at):
    a, b, c, d = (ref[at].astype(F32) for ref in refs)
    return (a + b) + (c + d)


def add_segment_kernel(at_ref, own_ref, a_ref, b_ref, c_ref, kept_ref, *sends):
    refs = (own_ref, a_ref, b_ref, c_ref)
    for j in range(4):
        value = summed(refs, at_ref[AT_Z] ^ j)
        if j == 0:
            kept_ref[0] = value
        else:
            sends[j - 1][0] = value.astype(BF16)
    if kept_ref.shape[0] > 1:
        value = two_rows(summed(refs, 4))
        kept_ref[1] = value.astype(F32)
        for send in sends:
            send[1] = value


def add_plane_kernel(at_ref, own_ref, a_ref, b_ref, c_ref, out_ref, *more):
    refs = (own_ref, a_ref, b_ref, c_ref)
    out_ref[...] = summed(refs, 0).astype(BF16)
    if more:
        more[0][...] = summed(refs, 1)


def add_split_kernel(at_ref, kept_ref, got_ref, own_ref, send_ref, *, by):
    zs = 4
    for i, j in enumerate((0, 3 - by, by, 3)):
        here = pl.ds((at_ref[AT_S] ^ j) * zs, zs)
        value = kept_ref[here].astype(F32) + got_ref[here].astype(F32)
        if i < 2:
            own_ref[i] = value
        else:
            send_ref[i - 2] = value.astype(BF16)


def add_half_kernel(at_ref, own_ref, got_ref, kept_ref, send_ref):
    kept_ref[...] = own_ref[0] + got_ref[0].astype(F32)
    send_ref[...] = (own_ref[1] + got_ref[1].astype(F32)).astype(BF16)


def add_quarter_kernel(at_ref, own_ref, got_ref, kept_ref, send_ref):
    z = at_ref[AT_Z]
    for i, j in enumerate((0, 2, 1, 3)):
        value = own_ref[z ^ j] + got_ref[z ^ j].astype(F32)
        if i < 2:
            kept_ref[i] = value
        else:
            send_ref[i - 2] = value.astype(BF16)


def add_both_kernel(at_ref, own_ref, got_ref, out_ref):
    out_ref[...] = (own_ref[...] + got_ref[...].astype(F32)).astype(BF16)


def both_split_kernel(at_ref, kept_ref, got_ref, owna_ref, ownb_ref, a_ref, b_ref):
    for half, (own, send, by) in enumerate(((owna_ref, a_ref, 1), (ownb_ref, b_ref, 2))):
        for i, j in enumerate((0, 3 - by, by, 3)):
            here = pl.ds((at_ref[AT_S] ^ j) * 4 + 2 * half, 2)
            value = kept_ref[here].astype(F32) + got_ref[here].astype(F32)
            if i < 2:
                own[i] = value
            else:
                send[i - 2] = value.astype(BF16)


def both_half_kernel(at_ref, owna_ref, ownb_ref, gota_ref, gotb_ref, kept_ref, a_ref, b_ref):
    for half, (own, got, send) in enumerate(((owna_ref, gota_ref, a_ref), (ownb_ref, gotb_ref, b_ref))):
        kept_ref[2 * half : 2 * half + 2] = own[0] + got[0].astype(F32)
        send[...] = (own[1] + got[1].astype(F32)).astype(BF16)


def both_quarter_kernel(at_ref, own_ref, gota_ref, gotb_ref, kept_ref, *refs):
    sends, sc = refs[:3], refs[3]
    sc[0:2] = own_ref[0:2] + gota_ref[...].astype(F32)
    sc[2:4] = own_ref[2:4] + gotb_ref[...].astype(F32)
    for j in range(4):
        value = sc[at_ref[AT_Z] ^ j]
        if j == 0:
            kept_ref[0] = value
        else:
            sends[j - 1][0] = value.astype(BF16)


class Plain:
    split = False

    def __init__(self, sizes, at):
        self.sizes, self.at = sizes, at
        self.order = at.at[AT_S].set(0)

    def first(self, x, labels, pairs):
        rows = D // (2 * self.sizes["z"])
        emb = lax.all_gather(x[0, :rows], ("z", "c"), axis=0, tiled=True)
        mods = lax.psum(x[1].astype(F32) + x[2].astype(F32), ("z", "c"))
        got = lax.ppermute(labels, CHIP, pairs)
        label = jnp.where(self.at[AT_OWN] == 1, labels, got)[self.at[AT_WHICH]]
        return emb, mods, self.at.at[AT_LABEL].set(label)

    def columns(self, bundles):
        return [lax.all_gather(x, ("z", "c"), axis=1, tiled=True) for x in bundles]

    def total(self, x):
        return lax.psum(x, ("z", "c")), jnp.zeros_like(x)

    def core(self, g):
        own = lax.psum_scatter(g[0].astype(F32), ("z", "c"), scatter_dimension=1, tiled=True)
        return lax.psum(own, "s"), lax.psum(g[1][0].astype(F32), CHIP)

    core_halves = core_both = core

    def segment(self, x):
        return x

    plane = halves_one = halves_two = both_one = both_two = segment

    def shared(self, xs):
        return [[x[0][j].astype(BF16) for j in range(4)] for x in xs]


class Squares(Plain):
    split = True

    def __init__(self, sizes, at):
        self.sizes, self.at, self.order = sizes, at, at

    def across(self, x, axis):
        return [swap(x, axis, 4, by) for by in (1, 2, 3)]

    def first(self, x, labels, pairs):
        own = jnp.stack([x] + self.across(x, "z"))
        self.ready = own
        return call(
            first_kernel,
            "first",
            [((D, ECOLS), BF16), ((48, D), F32), ((AT_LABEL + 1,), jnp.int32)],
            [self.at, own, swap(own, "c", 2, 1)],
            cost(0, 1e6),
            out_spaces=[VMEM, VMEM, SMEM],
        )

    def columns(self, bundles):
        out, wait = [], ()
        for x in bundles:
            mine = x[0]
            stack = jnp.stack([mine] + self.across(after(mine, *wait[:1]), "z"))
            pieces = self.across(after(stack, *wait[1:]), "s")
            own = [stack] + pieces
            out.append((own, [swap(y, "c", 2, 1) for y in own]))
            wait = (stack, *pieces)
        self.ready = out[0][0][0]
        return [placed(self.at, own, got) for own, got in out]

    def total(self, x):
        one, two, three = self.across(x, "z")
        x = (x + one) + (two + three)
        return x, swap(x, "c", 2, 1)

    def run(self, kernel, name, outs, inputs, scratch=()):
        return call(kernel, name, outs, [self.at, *inputs], cost(0, 1e5), scratch)

    def core(self, g):
        kept, sent = g
        count, rows, width = kept.shape
        full = (4 + count % 4, rows, width)
        cuts = (0, count // 3, 2 * (count // 3), count)
        got = [swap(sent[a:b], "c", 2, 1) for a, b in zip(cuts[:-1], cuts[1:])]
        outs = [(full, F32)] + [(full, BF16)] * 3
        return self.run(
            lambda at, kept, *refs: add_core_kernel(at, kept, Rows(refs[:3], cuts), *refs[3:]),
            "add_core", outs, [kept, *got], [pltpu.VMEM(kept.shape, BF16)],
        )

    def core_halves(self, g):
        kept, sent = g
        count, rows, width = kept.shape
        half = (2, 4, rows, width)
        return self.run(
            lambda *refs: add_split_kernel(*refs, by=1), "add_split", [(half, F32), (half, BF16)],
            [kept, swap(sent, "c", 2, 1)],
        )

    def halves_one(self, x):
        own, send = x
        full = own.shape[1:]
        outs = [(full, F32), (full, BF16)]
        return self.run(add_half_kernel, "add_half", outs, [own, swap(send, "s", 4, 1)])

    def halves_two(self, x):
        own, send = x
        part = (2,) + own.shape[1:]
        outs = [(part, F32), (part, BF16)]
        own, send = self.run(add_quarter_kernel, "add_quarter", outs, [own, swap(send, "s", 4, 2)])
        one = own.shape[1:]
        outs = [(one, F32), (one, BF16)]
        own, send = self.run(add_half_kernel, "add_half", outs, [own, swap(send, "z", 4, 1)])
        return self.run(add_both_kernel, "add_both", [(one, BF16)], [own, swap(send, "z", 4, 2)])

    def core_both(self, g):
        kept, sent = g
        count, rows, width = kept.shape
        part = (2, 2, rows, width)
        return self.run(
            both_split_kernel, "both_split", [(part, F32)] * 2 + [(part, BF16)] * 2,
            [kept, swap(sent, "c", 2, 1)],
        )

    def both_one(self, x):
        own_a, own_b, a, b = x
        part = own_a.shape[1:]
        return self.run(
            both_half_kernel, "both_half", [((4,) + part[1:], F32)] + [(part, BF16)] * 2,
            [own_a, own_b, swap(a, "s", 4, 1), swap(b, "s", 4, 2)],
        )

    def both_two(self, x):
        own, a, b = x
        one = (1,) + own.shape[1:]
        return self.run(
            both_quarter_kernel, "both_quarter", [(one, F32)] + [(one, BF16)] * 3,
            [own, swap(a, "s", 4, 2), swap(b, "s", 4, 1)], [pltpu.VMEM(own.shape, F32)],
        )

    def segment(self, x):
        own, *sends = x
        count, rows, width = own.shape
        one = (count - 3, rows, width)
        got = [swap(y, "s", 4, j + 1) for j, y in enumerate(sends)]
        return call(
            add_segment_kernel, "add_segment", [(one, F32)] + [(one, BF16)] * 3,
            [self.at, own, *got], cost(0, 1e5),
        )

    def plane(self, x):
        own, *sends = x
        count, rows, width = own.shape
        got = [swap(y, "z", 4, j + 1) for j, y in enumerate(sends)]
        return call(
            add_plane_kernel, "add_plane",
            [((rows, width), BF16)] + [((rows, width), F32)] * (count - 1),
            [self.at, own, *got], cost(0, 1e5),
        )

    def shared(self, xs):
        x = jnp.concatenate([y[0] for y in xs], axis=-1)
        pieces = [x] + self.across(x, "s")
        ends, at = [], 0
        for y in xs:
            width = y[0].shape[-1]
            ends.append([p[:, at : at + width] for p in pieces])
            at += width
        return ends


def lead_parts(emb_ref):
    lead = emb_ref[:, LEAD:EROWS].astype(BF16).astype(F32)
    gate = jax.nn.sigmoid(lead)
    return lead * gate, gate * (1.0 + lead * (1.0 - gate))


def ada_gradient(silu, sums_ref, layer, index):
    total = 0.0
    for group in range(GROUPS):
        at = 8 * (GROUPS * layer + group) + index
        total = total + silu[:, group : group + 1] * sums_ref[at : at + 1, :D]
    return total


def square_sum(v):
    return jnp.sum(v * v, axis=(0, 1), keepdims=True)


def gather_kernel(at_ref, *refs, widths):
    pieces, (emb_ref, ada_ref, sums_ref), outs = refs[:12], refs[12:15], refs[15:]
    ordered, (lead_ref, square_ref) = outs[:3], outs[3:]
    total = jnp.zeros((1, 1), F32)
    for k, ref in enumerate(ordered):
        squares = []
        for j in range(4):
            piece = pieces[4 * k + j][...]
            ref[at_ref[AT_S] ^ j] = piece
            squares.append(square_sum(piece.astype(F32)))
        total = total + ((squares[0] + squares[1]) + (squares[2] + squares[3]))
    silu, slope = lead_parts(emb_ref)
    rows = silu.shape[0]
    lane = lax.broadcasted_iota(jnp.int32, (rows, 128), 1)
    lead = jnp.zeros((rows, 128), F32)
    for group in range(GROUPS):
        d_silu = jnp.zeros((rows, 1), F32)
        for layer in range(LAYERS):
            for i in range(6):
                at = 8 * (GROUPS * layer + group) + i
                ada = ada_ref[layer, :, D * i : D * (i + 1)].astype(BF16).astype(F32)
                d_silu = d_silu + jnp.sum(ada * sums_ref[at : at + 1, :D], axis=-1, keepdims=True)
        value = d_silu * slope[:, group : group + 1]
        total = total + square_sum(value)
        lead = jnp.where(lane == group, value, lead)
    for layer in range(LAYERS):
        for i in range(6):
            total = total + square_sum(ada_gradient(silu, sums_ref, layer, i))
    lead_ref[...] = lead
    square_ref[...] = jnp.broadcast_to(total, square_ref.shape)


def gathered(at, pieces, emb_t, ada, sums):
    widths = [group[0].shape for group in pieces]
    return call(
        lambda *refs: gather_kernel(*refs, widths=widths),
        "gathered",
        [((4,) + shape, BF16) for shape in widths]
        + [((widths[0][0], 128), F32), ((8, 128), F32)],
        [at, *pieces[0], *pieces[1], *pieces[2], emb_t, ada, sums],
        cost(0, 4e6),
    )


def update_kernel(at_ref, *refs, rate):
    g1_ref, g2_ref, g3_ref, lead_ref, sums_ref, own_ref, got_ref = refs[:7]
    state = refs[7:28]
    outs, (loss_ref, norm_ref) = refs[28:49], refs[49:51]
    results, sems = refs[51:72], refs[72]
    squares = own_ref[0:1, 0:1] + got_ref[0:1, 0:1]
    norm = jnp.sqrt(squares)
    factor = CLIP / jnp.maximum(norm, CLIP)
    norm_ref[...] = norm
    loss_ref[...] = sums_ref[6:7, 0:1] + sums_ref[7:8, 0:1]
    silu, _ = lead_parts(state[0])
    rows = silu.shape[0]

    def advance(index, at, g):
        w_ref, m_ref, a_ref = (state[index + 7 * k] for k in range(3))
        g = g.astype(F32) * factor
        m = KEEP * m_ref[at] + g
        w = w_ref[at] - rate * (BOOST if index == 0 else 1.0) * (g + KEEP * m)
        results[index + 7][at] = m
        results[index][at] = w
        results[index + 14][at] = KEEP * a_ref[at] + (1.0 - KEEP) * w

    copies = []

    def send(index):
        for k in range(3):
            i = index + 7 * k
            copy = pltpu.make_async_copy(results[i], outs[i], sems.at[i])
            copy.start()
            copies.append(copy)

    every = slice(None)
    for layer in range(LAYERS):
        for i in range(6):
            g = ada_gradient(silu, sums_ref, layer, i)
            advance(5, (layer, every, slice(D * i, D * (i + 1))), g)
    send(5)
    att = (g3_ref, g2_ref)
    ff = ((g2_ref, D), (g1_ref, 0))
    for layer in range(LAYERS):
        ref, lane = ff[layer]
        for j in range(2):
            part = slice(HALF * j, HALF * (j + 1))
            advance(3, (layer, every, part), ref[j, :, lane : lane + HALF])
            advance(4, (layer, every, part), ref[2 + j, :, lane : lane + HALF])
    send(3)
    send(4)
    for layer in range(LAYERS):
        for j in range(3):
            advance(1, (layer, every, slice(D * j, D * (j + 1))), att[layer][j, :, :D])
    send(1)
    for layer in range(LAYERS):
        advance(2, (layer,), att[layer][3, :, :D])
    send(2)
    col = lax.broadcasted_iota(jnp.int32, (512, PIXELS), 1)
    row = lax.broadcasted_iota(jnp.int32, (512, PIXELS), 0)
    back = jnp.logical_and(row // 256 == col % 2, row % 256 == col // 2).astype(BF16)
    g_head = jnp.concatenate([g1_ref[j, :, HALF : HALF + 128] for j in range(4)], axis=-1)
    advance(6, (every,), dot(g_head, back))
    send(6)
    lane = lax.broadcasted_iota(jnp.int32, (rows, 128), 1)
    for j in range(3):
        g = g3_ref[j, :, D : D + 128].astype(F32)
        width = min(128, EROWS - 128 * j)
        if LEAD < 128 * j + width:
            first = LEAD - 128 * j
            for group in range(GROUPS):
                g = jnp.where(lane == first + group, lead_ref[:, group : group + 1], g)
        advance(0, (every, slice(128 * j, 128 * j + width)), g[:, :width])
    send(0)
    for copy in copies:
        copy.wait()


def updated(at, g, lead, sums, own, got, state, rate):
    shapes = [(x.shape, F32) for x in state]
    scalar = [((1, 1), F32)] * 2
    inputs = [at, *g, lead, sums, own, got, *state]
    return call(
        lambda *refs: update_kernel(*refs, rate=rate),
        "updated",
        shapes + scalar,
        inputs,
        cost(0, 2e7),
        [pltpu.VMEM(shape, kind) for shape, kind in shapes] + [pltpu.SemaphoreType.DMA((21,))],
        limit=24,
        out_spaces=[ANY] * 21 + [VMEM] * 2,
    )


def per_device(sizes, *arrays):
    (tiles_in, truth_in, labels, var_ids, basis) = arrays[:5]
    masters = arrays[5:12]
    segments, dp = sizes["s"], sizes["z"] * 2
    micro = tiles_in.shape[0]
    assert segments == 2 * micro
    rows = D // dp
    s, z, c = (lax.axis_index(name) for name in CHIP)
    which, owner = s % micro, s // micro
    at = jnp.stack([s, z, c, c == owner, which, 0]).astype(jnp.int32)
    fast = segments == 4 and sizes["z"] == 4
    move = (Squares if fast else Plain)(sizes, at)
    cut = Cut(sizes["z"], rows, move.split)
    views = []
    for k in range(3):
        w = list(arrays[5 + 7 * k : 12 + 7 * k])
        w[0], w[4] = w[0].T, w[4].transpose(0, 2, 1)
        views += w

    pairs = []
    for a in range(segments):
        for b in range(sizes["z"]):
            base = (a * sizes["z"] + b) * 2
            pairs.append((base + a // micro, base + 1 - a // micro))
    pick = lambda x: lax.dynamic_index_in_dim(x, which, 0, keepdims=False).T

    first, *bundles = packed(at, labels, views[:7], 1 if fast else 4)
    tiles = pick(tiles_in)
    tiles_got = lax.ppermute(tiles, CHIP, pairs)
    emb, mods, at = move.first(first, labels, pairs)
    w0, w1 = move.columns(bundles)
    truth = pick(truth_in)
    truth_got = lax.ppermute(after(truth, tiles_got), CHIP, pairs)
    vid4 = jnp.pad(jnp.repeat(var_ids, 4), (0, D - PIXELS), constant_values=-1)[None].astype(
        jnp.int32
    )
    h0, agg, x_all, embk = embed(at, tiles, tiles_got, emb, vid4)
    h1, q0, own0, other0, att0, lse0, *kept = block_forward(after(at, truth_got), h0, mods, w0)
    q1, own1 = qkv_rows(at, h1, mods, w1)
    other1 = swap(own1, "c", 2, 1)
    d_mid, d_att, att1, lse1, g_out, dmod1, loss, *g_first = turn(
        at, cut, h1, q1, own1, other1, mods, w1, truth, truth_got, basis, 1.0 / (micro * dp)
    )
    d_q, d_k, d_v, *sent = attention_back(at, q1, own1, other1, lse1, att1, d_att, finish=True)
    got = [swap(x, "c", 2, 1) for x in sent]
    first = move.core_halves(g_first)
    d_mid, d_att, g_out, dmod1, dmod0, *g_second = between(
        after(at, *first), cut, [d_q, d_k, d_v, *got], h1, d_mid, g_out, dmod1, mods, w1, [att0, *kept], w0
    )
    saved = (q0, own0, other0, lse0, att0, d_att)
    d_qa, d_k, d_v = attention_back(at, *saved, steps=1)
    second = move.core_both(g_second)
    first = move.halves_one(first)
    d_qb, d_k, d_v = attention_back(
        after(at, *second, *first), *saved, start=1, steps=1, carried=(d_k, d_v)
    )
    g_third = last(
        at, cut, [d_qa, d_qb, d_k, d_v], h0, d_mid, g_out, dmod0, dmod1, loss, mods, w0, x_all, agg, embk, vid4
    )
    second = move.both_one(second)
    third = move.core([g_third[0], after(g_third[1])])
    third = move.plane(move.segment(third))
    first = move.halves_two(first)
    second = move.plane(move.both_two(second))
    ends = move.shared([first, second]) + move.shared([third])
    sums = third[1]

    g1, g2, g3, lead_g, squares = gathered(move.order, ends, views[0], views[5], sums)
    own, got = move.total(squares)
    count = sum(w.size for w in masters) * dp
    rate = 0.02 * math.sqrt(count) / CLIP
    *new, loss_value, norm = updated(at, (g1, g2, g3), lead_g, sums, own, got, views, rate)
    for k in range(3):
        new[7 * k] = new[7 * k].T
        new[7 * k + 4] = new[7 * k + 4].transpose(0, 2, 1)
    return (loss_value.reshape(()), norm.reshape(()), *new)


def solution(mesh):
    segments, dp = mesh.shape["segment"], mesh.shape["dp"]
    sizes = {"s": segments, "z": dp // 2, "c": 2}
    split = Mesh(mesh.devices.reshape(segments, dp // 2, 2), CHIP)
    d = ("z", "c")
    weights = (
        P(None, d),
        P(None, d, None),
        P(None, d, None),
        P(None, d, None),
        P(None, None, d),
        P(None, d, None),
        P(d, None),
    )
    return jax.shard_map(
        lambda *arrays: per_device(sizes, *arrays),
        mesh=split,
        in_specs=(P(d, None, None), P(d, None, None), P(d), P(), P()) + weights * 3,
        out_specs=(P(), P()) + weights * 3,
        check_vma=False,
    )
```

```python
import math

import jax
import jax.numpy as jnp
from jax import lax
from jax.experimental import pallas as pl
from jax.experimental.pallas import tpu as pltpu
from jax.sharding import Mesh, PartitionSpec as P

D = 384
HEADS = 6
HEAD_DIM = 64
FF = 1536
VARS = 69
CHANNELS = 69
LONP = 128
LATP = 8
LAYERS = 2
GROUPS = 3
PIXELS = 276
LEAD = PIXELS + VARS + 1
EROWS = LEAD + GROUPS
ECOLS = 384
EPS = 1e-06
CLIP = 0.001
KEEP = 0.9
BOOST = 20.0
LABEL_LANE = D - 1
HALF = FF // 2

F32 = jnp.float32
BF16 = jnp.bfloat16
CHIP = ("s", "z", "c")


def dot(a, b):
    return jnp.dot(a, b, preferred_element_type=F32)


def dot_nt(a, b):
    return lax.dot_general(a, b, (((1,), (1,)), ((), ())), preferred_element_type=F32)


def dot_tn(a, b):
    return lax.dot_general(a, b, (((0,), (0,)), ((), ())), preferred_element_type=F32)


def parts(x, count):
    out = []
    for step in range(count):
        piece = x.astype(BF16)
        out.append(piece)
        if step < count - 1:
            x = x - piece.astype(F32)
    return out


def normal(v):
    centered = v - jnp.mean(v, axis=-1, keepdims=True)
    inverse = lax.rsqrt(jnp.mean(centered * centered, axis=-1, keepdims=True) + EPS)
    return centered * inverse, inverse


def normal_back(d_x, x, inverse):
    return inverse * (
        d_x - jnp.mean(d_x, axis=-1, keepdims=True) - x * jnp.mean(d_x * x, axis=-1, keepdims=True)
    )


def lane_below(limit, shape):
    return lax.broadcasted_iota(jnp.int32, shape, len(shape) - 1) < limit


def sublane(shape):
    return lax.broadcasted_iota(jnp.int32, shape, 0)


def same_group():
    col = lax.broadcasted_iota(jnp.int32, (D, D), 1)
    return (sublane((D, D)) // 4 == col // 4).astype(BF16)


def chosen_table(vid_ref):
    return (sublane((ECOLS, D)) - PIXELS == vid_ref[...]).astype(BF16)


def first_of_four(shape):
    return sublane(shape) % 4 == 0


def cost(flops, size, exps=0):
    return pl.CostEstimate(flops=int(flops), bytes_accessed=int(size), transcendentals=int(exps))


VMEM = pl.BlockSpec(memory_space=pltpu.VMEM)
SMEM = pl.BlockSpec(memory_space=pltpu.SMEM)
HBM = pl.BlockSpec(memory_space=pltpu.HBM)
CHUNK = 512
SPAN = 512
AT_S, AT_Z, AT_C, AT_OWN, AT_WHICH, AT_LABEL = range(6)


def call(kernel, name, outs, inputs, estimate, scratch=(), limit=24, in_space=VMEM, out_spaces=None):
    return pl.pallas_call(
        kernel,
        in_specs=[SMEM] + [in_space] * (len(inputs) - 1),
        out_specs=out_spaces or [VMEM] * len(outs),
        out_shape=[jax.ShapeDtypeStruct(shape, kind) for shape, kind in outs],
        scratch_shapes=list(scratch),
        compiler_params=pltpu.CompilerParams(vmem_limit_bytes=limit << 20),
        cost_estimate=estimate,
        name=name,
    )(*inputs)


def rows_at(index, size):
    return pl.ds(pl.multiple_of(index * size, size), size)


def after(x, *others):
    return lax.optimization_barrier((x, others))[0]


def column_sum(v):
    return jnp.sum(v, axis=0, keepdims=True)


class Cut:
    def __init__(self, pairs, rows, split):
        self.pairs, self.rows, self.split = pairs, rows, split
        self.outputs = 2
        self.buffer = None

    def shapes(self, width, extra=False):
        if self.split:
            return [((4 * self.pairs + extra, self.rows, width), BF16)] * 2
        return [((4, D, width), BF16), ((1, 48, width), BF16)]

    def scratch(self, width):
        return [pltpu.VMEM((D, width), F32)]

    def on(self, buffer):
        other = Cut(self.pairs, self.rows, self.split)
        other.buffer = buffer
        return other

    def write(self, at_ref, outs, quarter, lane, value):
        width = value.shape[-1]
        cols = slice(lane, lane + width)
        if not self.split:
            outs[0][quarter, :, cols] = value.astype(BF16)
            return
        self.buffer[:, :width] = value
        core = at_ref[AT_C]
        for z in range(self.pairs):
            for ref, which in ((outs[0], core), (outs[1], 1 - core)):
                part = self.buffer[rows_at(2 * z + which, self.rows), :width]
                ref[quarter * self.pairs + z, :, cols] = part.astype(BF16)

    def write_extra(self, outs, value):
        value = value.astype(BF16)
        if self.split:
            outs[0][4 * self.pairs] = value
            outs[1][4 * self.pairs] = value
        else:
            outs[1][0] = value


def embed_kernel(
    at_ref, own_ref, got_ref, emb_ref, vid_ref,
    out_ref, agg_ref, x_ref, embk_ref, x_sc, bases_sc,
):
    tokens = own_ref.shape[1]
    half = tokens // 2
    emb = emb_ref[...]
    embk_ref[...] = emb.astype(F32).T.astype(BF16)
    query = jnp.broadcast_to(emb[:, LEAD - 1 : LEAD].astype(F32), (D, 128)).astype(BF16)
    by_row = dot_tn(emb, query)
    table = chosen_table(vid_ref)
    inside = sublane((D, 1)) < PIXELS
    proj = jnp.where(inside, by_row[:D, :1], 0.0)
    base = sum(dot_tn(table, p) for p in parts(by_row, 3))[:, :1]
    lane = lax.broadcasted_iota(jnp.int32, (D, D), 1)
    bases_sc[...] = jnp.where(lane % 4 == 0, dot(emb, table), 0.0).astype(BF16)
    group = same_group()
    x_sc[...] = jnp.zeros_like(x_sc)
    x_sc[:PIXELS] = jnp.where(at_ref[AT_OWN] == 1, own_ref[...], got_ref[...])

    def step(i, carry):
        here = rows_at(i, CHUNK)
        source = lax.rem(i * CHUNK + at_ref[AT_C] * half, tokens)
        packed = x_sc[:, pl.ds(pl.multiple_of(source, CHUNK), CHUNK)]
        x = packed.astype(F32)
        scores = sum(dot(group, p) for p in parts(x * proj, 3)) + base
        scores = jnp.where(inside, scores * D ** (-0.5), -1e30)
        e = jnp.exp(scores - jnp.max(scores, axis=0, keepdims=True))
        agg = e * (4.0 / column_sum(e))

        agg_ref[:, here] = agg
        x_ref[:, here] = packed
        total = dot(emb_ref[:, :D], (agg * x).astype(BF16))
        for p in parts(agg, 2):
            total = total + dot(bases_sc[...], p)
        out_ref[here, :] = total.T.astype(BF16)
        return carry

    lax.fori_loop(0, tokens // CHUNK, step, 0)


def embed(at, own, got, emb, vid4):
    tokens = own.shape[1]
    return call(
        embed_kernel,
        "embed",
        [
            ((tokens, D), BF16),
            ((D, tokens), F32),
            ((D, tokens), BF16),
            ((ECOLS, D), BF16),
        ],
        [at, own, got, emb, vid4],
        cost(1e6, 1e4),
        [pltpu.VMEM((D, tokens), BF16), pltpu.VMEM((D, D), BF16)],
    )


def embed_back(dh, x_ref, agg_ref, embk_ref, vid_ref):
    x = x_ref[...].astype(F32)
    agg = agg_ref[...]
    embk = embk_ref[...]
    table = chosen_table(vid_ref)
    bases = dot_tn(table, embk_ref[...]).astype(BF16)
    query = embk_ref[LEAD - 1 : LEAD, :].astype(F32)
    g_patch = dot((agg * x).astype(BF16), dh)
    d_agg = dot_nt(bases, dh)
    group = same_group()
    for p in parts(dot_nt(embk, dh) * x, 2):
        d_agg = d_agg + dot(group, p)
    inner = 0.25 * column_sum(agg * d_agg)
    d_scores = agg * (d_agg - inner) * D ** (-0.5)
    d_proj = jnp.sum(d_scores * x, axis=-1, keepdims=True)
    d_base = jnp.sum(d_scores, axis=-1, keepdims=True)
    d_base = jnp.where(first_of_four(d_base.shape), d_base, 0.0)
    d_bases = d_base * query
    for p in parts(jnp.where(first_of_four((D, 1)), agg, 0.0), 2):
        d_bases = d_bases + dot(p, dh)
    g_table = sum(dot(table, p) for p in parts(d_bases, 2))
    d_query = column_sum(embk.astype(F32) * d_proj) + column_sum(bases.astype(F32) * d_base)
    total = g_table + jnp.where(sublane((ECOLS, 1)) == LEAD - 1, d_query, 0.0)
    return total + g_patch + d_proj * query


def mod_row(mods_ref, at_ref, layer, index):
    row = 8 * (layer * GROUPS + at_ref[AT_LABEL]) + index
    return mods_ref[pl.ds(row, 1), :D]


def first_norm(h, mods_ref, at_ref, layer):
    x, inverse = normal(h.astype(F32))
    scale = 1.0 + mod_row(mods_ref, at_ref, layer, 1)
    return (x * scale + mod_row(mods_ref, at_ref, layer, 0)).astype(BF16), x, inverse


def pair_masks():
    low = lane_below(HEAD_DIM, (1, 128))
    return low, jnp.logical_not(low)


def both(own_ref, other_ref, lane):
    here = slice(lane, lane + 128)
    return jnp.concatenate([own_ref[:, here], other_ref[:, here]])


def attend(here, q_ref, own_ref, other_ref, att_ref, lse_ref):
    zero = jnp.zeros((), BF16)
    rows = q_ref[here, :].shape[0]
    lane = lax.broadcasted_iota(jnp.int32, (rows, 128), 1)
    sums = jnp.zeros((rows, 128), F32)
    for pair in range(HEADS // 2):
        a = 128 * pair
        q = q_ref[here, a : a + 128] * 0.125
        keys = both(own_ref, other_ref, a)
        vals = both(own_ref, other_ref, D + a)
        mixed = jnp.zeros((rows, 128), F32)
        for which, mask in enumerate(pair_masks()):
            scores = dot_nt(q, jnp.where(mask, keys, zero))
            top = jnp.max(scores, axis=-1, keepdims=True)
            e = jnp.exp(scores - top)
            total = jnp.sum(e, axis=-1, keepdims=True)
            mixed = mixed + dot(e.astype(BF16), jnp.where(mask, vals, zero)) * (1.0 / total)
            sums = jnp.where(lane == 2 * pair + which, top + jnp.log(total), sums)
        att_ref[here, a : a + 128] = mixed.astype(BF16)
    lse_ref[here, :] = sums


def gelu_and_slope(u):
    k = math.sqrt(2.0 / math.pi)
    t = jnp.tanh(k * (u + 0.044715 * (u * u * u)))
    cdf = 0.5 * (1.0 + t)
    return u * cdf, cdf + 0.5 * u * (1.0 - t * t) * k * (1.0 + 3 * 0.044715 * (u * u))


def feed_forward(
    here, h, one, mods_ref, at_ref, layer, w_ref, act_ref, slope_ref, n2_ref=None, stored=lambda j: None
):
    middle = h.astype(F32) + mod_row(mods_ref, at_ref, layer, 2) * one
    x, _ = normal(middle)
    scale = 1.0 + mod_row(mods_ref, at_ref, layer, 4)
    n2 = (x * scale + mod_row(mods_ref, at_ref, layer, 3)).astype(BF16)
    if n2_ref is not None:
        n2_ref[here, :] = n2
    two = jnp.zeros(middle.shape, F32)
    for j in range(2):
        part = slice(HALF * j, HALF * (j + 1))
        act, slope = gelu_and_slope(dot(n2, w_ref[j, :, D : 3 * D]))
        slope_ref[here, part] = slope.astype(slope_ref.dtype)
        act = act.astype(BF16)
        act_ref[here, part] = act
        stored(j)
        two = two + dot_nt(act, w_ref[2 + j, :, D : 3 * D])
    return middle, two, middle + mod_row(mods_ref, at_ref, layer, 5) * two


def feed_back(
    here, d_out, one, two, middle, slope_ref, mods_ref, at_ref, layer, w_ref,
    dunits_ref, dtwo_ref, done_ref, dmid_ref, datt_ref, dmod_ref, n2_ref=None,
):
    d_out = d_out.astype(F32)
    d_two = (mod_row(mods_ref, at_ref, layer, 5) * d_out).astype(BF16)
    dtwo_ref[here, :] = d_two
    d_n2 = jnp.zeros(d_out.shape, F32)
    for j in range(2):
        part = slice(HALF * j, HALF * (j + 1))
        slope = slope_ref[here, part].astype(F32)
        d_units = (slope * dot(d_two, w_ref[2 + j, :, D : 3 * D])).astype(BF16)
        dunits_ref[here, part] = d_units
        d_n2 = d_n2 + dot_nt(d_units, w_ref[j, :, D : 3 * D])
    x, inverse = normal(middle)
    scale = 1.0 + mod_row(mods_ref, at_ref, layer, 4)
    if n2_ref is not None:
        n2_ref[here, :] = (x * scale + mod_row(mods_ref, at_ref, layer, 3)).astype(BF16)
    d_mid = d_out + normal_back(d_n2 * scale, x, inverse)
    dmid_ref[here, :] = d_mid
    d_one = (mod_row(mods_ref, at_ref, layer, 2) * d_mid).astype(BF16)
    done_ref[here, :] = d_one
    datt_ref[here, :] = dot_nt(d_one, w_ref[3, :, :D]).astype(BF16)
    dmod_ref[2:3] += column_sum(d_mid * one)
    dmod_ref[3:4] += column_sum(d_n2)
    dmod_ref[4:5] += column_sum(d_n2 * x)
    dmod_ref[5:6] += column_sum(d_out * two)


def feed_gradients(at_ref, cut, outs, lane, n2_ref, dunits_ref, dtwo_ref, act_ref):
    for j in range(2):
        part = slice(HALF * j, HALF * (j + 1))
        cut.write(at_ref, outs, j, lane, dot_tn(n2_ref[...], dunits_ref[:, part]))
        cut.write(at_ref, outs, 2 + j, lane, dot_tn(dtwo_ref[...], act_ref[:, part]))


def rows_scratch(count, widths):
    return [pltpu.VMEM((count, width), BF16) for width in widths]


def block_kernel(
    at_ref, h_ref, mods_ref, w_ref,
    out_ref, q_out, own_out, other_out, att_out, lse_out, one_out, mid_out, slope_out, act_out, two_out,
    q_ref, own_ref, other_ref, att_ref, lse_ref, one_ref, mid_ref, slope_ref, act_ref, two_ref, sems,
):
    count = out_ref.shape[0]
    steps = count // CHUNK

    def project(i, carry):
        here = rows_at(i, CHUNK)
        normed, _, _ = first_norm(h_ref[here, :], mods_ref, at_ref, 0)
        q_ref[here, :] = dot(normed, w_ref[0, :, :D]).astype(BF16)
        for j in range(2):
            own_ref[here, D * j : D * (j + 1)] = dot(normed, w_ref[j + 1, :, :D]).astype(BF16)
        return carry

    lax.fori_loop(0, steps, project, 0)

    def project_other(i, carry):
        here = rows_at(i, CHUNK)
        normed, _, _ = first_norm(h_ref[rows_at(i + steps, CHUNK), :], mods_ref, at_ref, 0)
        for j in range(2):
            other_ref[here, D * j : D * (j + 1)] = dot(normed, w_ref[j + 1, :, :D]).astype(BF16)
        return carry

    lax.fori_loop(0, steps, project_other, 0)
    early = [
        pltpu.make_async_copy(ref, out, sems.at[2, i])
        for i, (ref, out) in enumerate(((q_ref, q_out), (own_ref, own_out), (other_ref, other_out)))
    ]
    for copy in early:
        copy.start()
    kept = (
        (att_ref, att_out), (lse_ref, lse_out), (one_ref, one_out), (mid_ref, mid_out),
        (slope_ref, slope_out), (act_ref, act_out), (two_ref, two_out),
    )

    slope, act = kept[4:6]
    whole = [
        pltpu.make_async_copy(ref, out, sems.at[0, k])
        for k, (ref, out) in enumerate(kept[:4] + kept[6:])
    ]
    halves = [
        [
            pltpu.make_async_copy(ref.at[:, part], out.at[:, part], sems.at[1, 2 * j + k])
            for k, (ref, out) in enumerate((slope, act))
        ]
        for j, part in enumerate((pl.ds(0, HALF), pl.ds(HALF, HALF)))
    ]

    def start(*copies):
        for copy in copies:
            copy.start()

    here = slice(0, count)
    attend(here, q_ref, own_ref, other_ref, att_ref, lse_ref)
    one = dot(att_ref[...], w_ref[3, :, :D])
    one_ref[...] = one.astype(BF16)
    start(*whole[:3])
    middle, two, out = feed_forward(
        here, h_ref[:count], one, mods_ref, at_ref, 0, w_ref, act_ref, slope_ref,
        stored=lambda j: start(*halves[j]),
    )
    mid_ref[...] = middle
    start(whole[3])
    two_ref[...] = two.astype(BF16)
    start(whole[4])
    out_ref[...] = out.astype(BF16)
    for copy in early + whole + halves[0] + halves[1]:
        copy.wait()


def block_forward(at, h, mods, weights):
    count = h.shape[0] // 2
    kept = [(D, BF16), (2 * D, BF16), (2 * D, BF16), (D, BF16), (128, F32), (D, BF16), (D, F32)]
    kept += [(FF, BF16), (FF, BF16), (D, BF16)]
    kept = [((count, width), kind) for width, kind in kept]
    return call(
        block_kernel,
        "block_forward",
        [((count, D), BF16)] + kept,
        [at, h, mods, weights],
        cost(2e9, 2e6),
        [pltpu.VMEM(shape, kind) for shape, kind in kept] + [pltpu.SemaphoreType.DMA((3, 7))],
        limit=28,
        out_spaces=[VMEM] + [HBM] * len(kept),
    )


def qkv_kernel(at_ref, h_ref, mods_ref, w_ref, q_ref, kv_ref):
    def step(i, carry):
        here = rows_at(i, CHUNK)
        normed, _, _ = first_norm(h_ref[here, :], mods_ref, at_ref, 1)
        q_ref[here, :] = dot(normed, w_ref[0, :, :D]).astype(BF16)
        for j in range(2):
            kv_ref[here, D * j : D * (j + 1)] = dot(normed, w_ref[j + 1, :, :D]).astype(BF16)
        return carry

    lax.fori_loop(0, q_ref.shape[0] // CHUNK, step, 0)


def qkv_rows(at, h, mods, weights):
    count = h.shape[0]
    return call(
        qkv_kernel,
        "qkv_rows",
        [((count, D), BF16), ((count, 2 * D), BF16)],
        [at, h, mods, weights],
        cost(1e9, 3e6),
    )


def turn_kernel(
    at_ref, h_ref, q_ref, own_ref, other_ref, mods_ref, w_ref, truth_ref, got_ref, basis_ref,
    dmid_ref, datt_ref, att_ref, lse_ref, gout_ref, dmod_ref, loss_ref, keep_ref, send_ref,
    act_ref, dunits_ref, dtwo_ref, n2_ref, done_ref, flat_ref, dpred_ref, true_ref, slope_ref,
    basis_sc, buffer, *, seed, cut,
):
    count = h_ref.shape[0]
    outs = (keep_ref, send_ref)
    entries = LATP * CHANNELS * 2 * LONP
    dmod_ref[...] = jnp.zeros_like(dmod_ref)
    loss_ref[...] = jnp.zeros_like(loss_ref)
    row = lax.broadcasted_iota(jnp.int32, (PIXELS, 256), 0)
    col = lax.broadcasted_iota(jnp.int32, (PIXELS, 256), 1)
    truth = jnp.where(at_ref[AT_OWN] == 1, truth_ref[...], got_ref[...])
    for b in range(2):
        picked = dot_tn(truth, (row == 2 * col + b).astype(BF16))
        true_ref[:, 256 * b : 256 * b + 256] = picked.astype(BF16)
    to = lax.broadcasted_iota(jnp.int32, (256, 256), 0)
    source = lax.broadcasted_iota(jnp.int32, (256, 256), 1)
    order = (source == 2 * (to % LONP) + to // LONP).astype(BF16)
    for i, p in enumerate(parts(basis_ref[...], 2)):
        basis_sc[i] = dot(order, p).astype(BF16)

    for i in range(count // SPAN):
        attend(slice(i * SPAN, (i + 1) * SPAN), q_ref, own_ref, other_ref, att_ref, lse_ref)

    def step(i, carry):
        here = rows_at(i, CHUNK)
        one = dot(att_ref[here, :], w_ref[3, :, :D])
        middle, two, h2 = feed_forward(
            here, h_ref[here, :], one, mods_ref, at_ref, 1, w_ref, act_ref, slope_ref, n2_ref
        )
        x, inverse = normal(h2.astype(BF16).astype(F32))
        flat = x.astype(BF16)
        flat_ref[here, :] = flat
        hw = [w_ref[j, :, 3 * D : 3 * D + 128] for j in range(4)]
        pred = [dot(flat, w) for w in hw]
        pred = [jnp.concatenate(pred[:2], axis=-1), jnp.concatenate(pred[2:], axis=-1)]
        hi, lo = basis_sc[0], basis_sc[1]
        grads = [[], []]
        loss = jnp.zeros((1, 1), F32)
        for p in range(CHUNK // LONP):
            part = slice(p * LONP, (p + 1) * LONP)
            fine = rows_at(i * (CHUNK // LONP) + p, LONP)
            seen = parts(jnp.concatenate([pred[0][part], pred[1][part]], axis=0), 2)
            waves = dot_tn(hi, seen[0]) + (dot_tn(hi, seen[1]) + dot_tn(lo, seen[0]))
            want = jnp.concatenate([true_ref[fine, :256], true_ref[fine, 256:]], axis=0)
            target = dot_tn(hi, want) + dot_tn(lo, want)
            top, low = waves[:LONP], waves[LONP:]
            gap = (top * top + low * low) - (
                target[:LONP] * target[:LONP] + target[LONP:] * target[LONP:]
            )
            loss = loss + jnp.sum(gap * gap, axis=(0, 1), keepdims=True)
            scaled = gap * (4.0 * seed / entries)
            d_waves = parts(jnp.concatenate([scaled * top, scaled * low], axis=0), 2)
            d_seen = dot(hi, d_waves[0]) + (dot(hi, d_waves[1]) + dot(lo, d_waves[0]))
            d_seen = d_seen.astype(BF16)
            grads[0].append(d_seen[:LONP])
            grads[1].append(d_seen[LONP:])
        loss_ref[...] += jnp.broadcast_to(loss * (seed / entries), loss_ref.shape)
        d_flat = jnp.zeros((CHUNK, D), F32)
        for b in range(2):
            whole = jnp.concatenate(grads[b], axis=0)
            dpred_ref[here, 256 * b : 256 * b + 256] = whole
            for j in range(2):
                d_flat = d_flat + dot_nt(whole[:, 128 * j : 128 * j + 128], hw[2 * b + j])
        d_h2 = normal_back(d_flat, x, inverse).astype(BF16)
        feed_back(
            here, d_h2, one, two, middle, slope_ref, mods_ref, at_ref, 1, w_ref,
            dunits_ref, dtwo_ref, done_ref, dmid_ref, datt_ref, dmod_ref,
        )
        return carry

    lax.fori_loop(0, count // CHUNK, step, 0)
    cut = cut.on(buffer)
    feed_gradients(at_ref, cut, outs, 0, n2_ref, dunits_ref, dtwo_ref, act_ref)
    for j in range(4):
        cut.write(at_ref, outs, j, HALF, dot_tn(flat_ref[...], dpred_ref[:, 128 * j : 128 * j + 128]))
    gout_ref[...] = dot_tn(att_ref[...], done_ref[...])


def turn(at, cut, h, q, own, other, mods, weights, truth, got, basis, seed):
    count = h.shape[0]
    return call(
        lambda *refs: turn_kernel(*refs, seed=seed, cut=cut),
        "turn",
        [
            ((count, D), F32),
            ((count, D), BF16),
            ((count, D), BF16),
            ((count, 128), F32),
            ((D, D), F32),
            ((8, D), F32),
            ((8, 128), F32),
        ]
        + cut.shapes(HALF + 128),
        [at, h, q, own, other, mods, weights, truth, got, basis],
        cost(4e9, 4e6),
        rows_scratch(count, [FF, FF, D, D, D, D, 512, 512])
        + [pltpu.VMEM((count, FF), F32), pltpu.VMEM((2, 256, 256), BF16)]
        + cut.scratch(HALF),
        limit=32,
    )


def attention_back_kernel(
    at_ref, q_ref, own_ref, other_ref, lse_ref, att_ref, datt_ref, dq_ref, *outs, finish,
):
    zero = jnp.zeros((), BF16)
    count = own_ref.shape[0]
    dk_sc, dv_sc = outs[-2:] if finish else outs[:2]
    dk_sc[...] = jnp.zeros_like(dk_sc)
    dv_sc[...] = jnp.zeros_like(dv_sc)

    def step(i, carry):
        rows = rows_at(i, SPAN)
        for pair in range(HEADS // 2):
            a = 128 * pair
            here = slice(a, a + 128)
            q = q_ref[rows, here]
            d_att = datt_ref[rows, here]
            keys = both(own_ref, other_ref, a)
            vals = both(own_ref, other_ref, D + a)
            dots = d_att.astype(F32) * att_ref[rows, here].astype(F32)
            d_q = jnp.zeros((SPAN, 128), F32)
            d_k = jnp.zeros((keys.shape[0], 128), F32)
            d_v = jnp.zeros((keys.shape[0], 128), F32)
            for which, mask in enumerate(pair_masks()):
                head = 2 * pair + which
                k = jnp.where(mask, keys, zero)
                v = jnp.where(mask, vals, zero)
                inner = jnp.sum(jnp.where(mask, dots, 0.0), axis=-1, keepdims=True)
                probs = jnp.exp(dot_nt(q * 0.125, k) - lse_ref[rows, head : head + 1])
                d_scores = (probs * (dot_nt(d_att, v) - inner)).astype(BF16)
                d_q = d_q + dot(d_scores, k)
                d_k = d_k + dot_tn(d_scores, jnp.where(mask, q, zero))
                d_v = d_v + dot_tn(probs.astype(BF16), jnp.where(mask, d_att, zero))
            dq_ref[rows, here] = (d_q * 0.125).astype(BF16)
            dk_sc[:, here] += d_k * 0.125
            dv_sc[:, here] += d_v
        return carry

    lax.fori_loop(0, count // SPAN, step, 0)
    if finish:
        dk_ref, dv_ref, dk_send, dv_send = outs[:4]
        dk_ref[...] = dk_sc[:count]
        dv_ref[...] = dv_sc[:count]
        dk_send[...] = dk_sc[count:].astype(BF16)
        dv_send[...] = dv_sc[count:].astype(BF16)


def attention_back(at, q, own, other, lse, att, d_att, finish=False):
    count = q.shape[0]
    full = ((2 * count, D), F32)
    outs = [((count, D), F32)] * 2 + [((count, D), BF16)] * 2 if finish else [full] * 2
    return call(
        lambda *refs: attention_back_kernel(*refs, finish=finish),
        "attention_back",
        [((count, D), BF16)] + outs,
        [at, q, own, other, lse, att, d_att],
        cost(5e9, 1e6),
        [pltpu.VMEM(*full)] * 2 if finish else (),
    )


def qkv_back(
    at_ref, cut, outs, lane, layer, d_q, d_k, d_v, h_ref, dmid_ref, gout_ref, mods_ref, w_ref,
):
    count, rows = d_q.shape[0], d_k.shape[0]
    normed, x, inverse = first_norm(h_ref[:rows], mods_ref, at_ref, layer)
    first = dot_nt(d_q, w_ref[0, :, :D])
    rest = dot_nt(d_k, w_ref[1, :, :D]) + dot_nt(d_v, w_ref[2, :, :D])
    if rows > count:
        d_n = jnp.concatenate([rest[:count] + first, rest[count:]], axis=0)
    else:
        d_n = rest + first
    cut.write(at_ref, outs, 0, lane, dot_tn(normed[:count], d_q))
    cut.write(at_ref, outs, 1, lane, dot_tn(normed, d_k))
    cut.write(at_ref, outs, 2, lane, dot_tn(normed, d_v))
    if gout_ref is not None:
        cut.write(at_ref, outs, 3, lane, gout_ref[...])
    scale = 1.0 + mod_row(mods_ref, at_ref, layer, 1)
    d_h = normal_back(d_n * scale, x, inverse)
    if rows > count:
        d_h = jnp.concatenate([d_h[:count] + dmid_ref[...], d_h[count:]], axis=0)
    else:
        d_h = d_h + dmid_ref[...]
    return d_h.astype(BF16), column_sum(d_n), column_sum(d_n * x)


def between_kernel(
    at_ref, dq_ref, dk_ref, dv_ref, dk_got, dv_got, h_ref, dmid_ref, gout_ref, dmod_ref, mods_ref, w1_ref,
    one_ref, two_ref, mid_ref, slope_ref, act_ref, att_ref, w0_ref,
    dmid_out, datt_out, dmod_out, dmod_next, keep_ref, send_ref,
    dh_sc, dunits_ref, dtwo_ref, n2_ref, done_ref, buffer, *, cut,
):
    outs = (keep_ref, send_ref)
    cut = cut.on(buffer)
    d_k = (dk_ref[...] + dk_got[...].astype(F32)).astype(BF16)
    d_v = (dv_ref[...] + dv_got[...].astype(F32)).astype(BF16)
    d_h, shift, scale = qkv_back(
        at_ref, cut, outs, 0, 1, dq_ref[...], d_k, d_v, h_ref, dmid_ref, gout_ref, mods_ref, w1_ref,
    )
    dmod_out[...] = dmod_ref[...]
    dmod_out[0:1] = shift
    dmod_out[1:2] = scale
    dh_sc[...] = d_h
    dmod_next[...] = jnp.zeros_like(dmod_next)

    def step(i, carry):
        here = rows_at(i, CHUNK)
        feed_back(
            here, dh_sc[here, :], one_ref[here, :].astype(F32), two_ref[here, :].astype(F32),
            mid_ref[here, :], slope_ref, mods_ref, at_ref, 0, w0_ref,
            dunits_ref, dtwo_ref, done_ref, dmid_out, datt_out, dmod_next, n2_ref,
        )
        return carry

    lax.fori_loop(0, dh_sc.shape[0] // CHUNK, step, 0)
    feed_gradients(at_ref, cut, outs, D, n2_ref, dunits_ref, dtwo_ref, act_ref)
    g_out = dot_tn(att_ref[...], done_ref[...])
    for j in range(4):
        tile = g_out[:, 128 * j : 128 * j + 128] if j < 3 else jnp.zeros((D, 128), F32)
        cut.write(at_ref, outs, j, D + HALF, tile)


def between(at, cut, grads, h, d_mid, g_out, dmod, mods, w1, kept, w0):
    att, one, mid, slope, act, two = kept
    count = d_mid.shape[0]
    return call(
        lambda *refs: between_kernel(*refs, cut=cut),
        "between",
        [((count, D), F32), ((count, D), BF16), ((8, D), F32), ((8, D), F32)]
        + cut.shapes(D + HALF + 128),
        [at, *grads, h, d_mid, g_out, dmod, mods, w1, one, two, mid, slope, act, att, w0],
        cost(1e9, 1e6),
        rows_scratch(count, [D, FF, D, D, D]) + cut.scratch(HALF),
        limit=28,
    )


def last_kernel(
    at_ref, dq_ref, dk_ref, dv_ref, h_ref, dmid_ref, dmod0_ref, dmod1_ref, loss_ref,
    mods_ref, w_ref, x_ref, agg_ref, embk_ref, vid_ref, keep_ref, send_ref, sums_sc, buffer, *, cut,
):
    outs = (keep_ref, send_ref)
    cut = cut.on(buffer)
    d_q = dq_ref[...]
    d_k, d_v = dk_ref[...].astype(BF16), dv_ref[...].astype(BF16)
    d_h, shift, scale = qkv_back(
        at_ref, cut, outs, 0, 0, d_q, d_k, d_v, h_ref, dmid_ref, None, mods_ref, w_ref,
    )
    sums_sc[...] = jnp.zeros_like(sums_sc)
    for group in range(GROUPS):
        hot = (at_ref[AT_LABEL] == group).astype(F32)
        for layer, ref in enumerate((dmod0_ref, dmod1_ref)):
            at = 8 * (GROUPS * layer + group)
            sums_sc[at : at + 8, :D] = ref[...] * hot
        sums_sc[8 * group : 8 * group + 1, :D] = shift * hot
        sums_sc[8 * group + 1 : 8 * group + 2, :D] = scale * hot
    loss = loss_ref[0:1, 0:1]
    top = loss.astype(BF16).astype(F32)
    sums_sc[6:7, :] = jnp.broadcast_to(top, (1, ECOLS))
    sums_sc[7:8, :] = jnp.broadcast_to(loss - top, (1, ECOLS))
    cut.write_extra(outs, sums_sc[...])
    cut.write(at_ref, outs, 3, 0, embed_back(d_h, x_ref, agg_ref, embk_ref, vid_ref).T)


def last(at, cut, grads, h, d_mid, dmod0, dmod1, loss, mods, w0, x, agg, embk, vid4):
    return call(
        lambda *refs: last_kernel(*refs, cut=cut),
        "last",
        cut.shapes(ECOLS, True),
        [at, *grads, h, d_mid, dmod0, dmod1, loss, mods, w0, x, agg, embk, vid4],
        cost(1e9, 1e6),
        [pltpu.VMEM((48, ECOLS), F32)] + cut.scratch(D),
        limit=28,
    )


def swap(x, axis, size, by):
    return lax.ppermute(x, axis, [(i, i ^ by) for i in range(size)])


def place_kernel(at_ref, *refs, rows):
    out_ref, inputs = refs[-1], refs[:-1]
    s, z, c = at_ref[AT_S], at_ref[AT_Z], at_ref[AT_C]
    for jc in range(2):
        for js in range(4):
            source = inputs[4 * jc + js]
            for jz in range(4):
                at = rows_at((z ^ jz) * 2 + (c ^ jc), rows)
                if len(source.shape) == 3:
                    out_ref[s ^ js, at, :] = source[jz]
                    continue
                for k in range(source.shape[1]):
                    out_ref[s ^ js, at, D * k : D * (k + 1)] = source[jz, k]


def placed(at, own, got):
    rows = own[0].shape[-2]
    width = math.prod(own[0].shape[1:]) // rows
    return call(
        lambda *refs: place_kernel(*refs, rows=rows),
        "placed",
        [((4, 8 * rows, width), BF16)],
        [at, *own, *got],
        cost(0, 1e5),
        limit=8,
    )[0]


def first_kernel(at_ref, own_ref, gota_ref, gotb_ref, emb_ref, mods_ref, out_ref):
    rows = own_ref.shape[2]
    total = jnp.zeros((rows, D), F32)
    for jc in range(2):
        for jz in range(4):
            ref, i = (own_ref, jz) if jc == 0 else ((gota_ref, gotb_ref)[jz // 2], jz % 2)
            row = (at_ref[AT_Z] ^ jz) * 2 + (at_ref[AT_C] ^ jc)
            emb_ref[rows_at(row, rows), :] = ref[i, 0]
            total = total + (ref[i, 1].astype(F32) + ref[i, 2].astype(F32))
    mods_ref[...] = total
    for i in range(AT_LABEL):
        out_ref[i] = at_ref[i]
    labels = [ref[0, 1, 0:8, 0:128].astype(F32) for ref in (own_ref, gota_ref)]
    labels = jnp.where(at_ref[AT_OWN] == 1, labels[0], labels[1])
    picked = jnp.where(sublane((8, 128)) == 6 + at_ref[AT_WHICH], labels, 0.0)
    out_ref[AT_LABEL] = jnp.max(picked).astype(jnp.int32)


def pack_kernel(at_ref, labels_ref, *refs, split):
    sources, (first_ref, zero_ref, one_ref), held, sems = refs[:7], refs[7:10], refs[10:17], refs[17]
    copies = [
        pltpu.make_async_copy(source, target, sems.at[i])
        for i, (source, target) in enumerate(zip(sources, held))
    ]
    for copy in copies:
        copy.start()
    emb_ref, qkv_ref, out_ref, up_ref, down_ref, ada_ref, head_ref = held
    rows = emb_ref.shape[0]
    blocks = first_ref
    blocks[...] = jnp.zeros_like(blocks)
    for i in (1, 2, 3, 4, 6):
        copies[i].wait()
    col = lax.broadcasted_iota(jnp.int32, (PIXELS, 128), 0)
    lane = lax.broadcasted_iota(jnp.int32, (PIXELS, 128), 1)
    for j in range(4):

        def fill(j=j):
            for layer, ref in enumerate((zero_ref, one_ref)):
                part = qkv_ref[layer, :, D * j : D * (j + 1)] if j < 3 else out_ref[layer]
                source = (up_ref if j < 2 else down_ref)[layer]
                source = source[:, HALF * (j % 2) : HALF * (j % 2 + 1)].astype(BF16)
                if split and layer == 0:
                    ref[0] = part.astype(BF16)
                    ref[1] = source[:, :D]
                    ref[2] = source[:, D:]
                    continue
                at = 0 if split else j
                ref[at, :, :D] = part.astype(BF16)
                ref[at, :, D : 3 * D] = source
            wide = lane + 128 * (j % 2)
            pick = jnp.logical_and(col == 2 * wide + j // 2, wide < PIXELS // 2).astype(BF16)
            one_ref[0 if split else j, :, 3 * D :] = dot(head_ref[...].astype(BF16), pick).astype(BF16)

        if split:
            pl.when(at_ref[AT_S] == j)(fill)
        else:
            fill()
    copies[0].wait()
    copies[5].wait()
    blocks[0, :rows, :EROWS] = emb_ref[...].astype(BF16)
    silu, _ = lead_parts(emb_ref)
    for layer in range(LAYERS):
        for i in range(6):
            ada = ada_ref[layer, :, D * i : D * (i + 1)].astype(BF16).astype(F32)
            for g in range(GROUPS):
                at = 8 * (GROUPS * layer + g) + i
                value = column_sum(silu[:, g : g + 1] * ada)
                top = value.astype(BF16)
                blocks[1, at : at + 1, :] = top
                blocks[2, at : at + 1, :] = (value - top.astype(F32)).astype(BF16)
    for i in range(2):
        label = jnp.full((1, D), labels_ref[i], jnp.int32).astype(F32).astype(BF16)
        blocks[1, 6 + i : 7 + i, :] = label
    if split:
        zero_ref[3:6] = blocks[...]


def packed(at, labels, weights, split):
    rows = weights[0].shape[0]
    quarters = 1 if split else 4
    return pl.pallas_call(
        lambda *refs: pack_kernel(*refs, split=split),
        in_specs=[SMEM, SMEM] + [HBM] * 7,
        out_specs=[VMEM] * 3,
        out_shape=[
            jax.ShapeDtypeStruct((3, 48, ECOLS), BF16),
            jax.ShapeDtypeStruct((6, rows, D) if split else (4, rows, 3 * D), BF16),
            jax.ShapeDtypeStruct((quarters, rows, 3 * D + 128), BF16),
        ],
        scratch_shapes=[pltpu.VMEM(w.shape, F32) for w in weights] + [pltpu.SemaphoreType.DMA((7,))],
        compiler_params=pltpu.CompilerParams(vmem_limit_bytes=60 << 20),
        cost_estimate=cost(0, 1e6),
        name="packed",
    )(at, labels, *weights)


def two_rows(v):
    loss = v[6:7] + v[7:8]
    top = loss.astype(BF16).astype(F32)
    row = sublane(v.shape)
    return jnp.where(row == 6, top, jnp.where(row == 7, loss - top, v)).astype(BF16)


class Rows:
    def __init__(self, refs, cuts):
        self.refs, self.cuts = refs, cuts

    def fill(self, out):
        for ref, a, b in zip(self.refs, self.cuts[:-1], self.cuts[1:]):
            out[a:b] = ref[...]


def add_core_kernel(at_ref, kept_ref, pieces, own_ref, *refs):
    sends, got_ref = refs[:3], refs[3]
    pieces.fill(got_ref)
    zs = 4
    for j in range(4):
        here = pl.ds((at_ref[AT_S] ^ j) * zs, zs)
        value = kept_ref[here].astype(F32) + got_ref[here].astype(F32)
        if j == 0:
            own_ref[:zs] = value
        else:
            sends[j - 1][:zs] = value.astype(BF16)
    if own_ref.shape[0] > zs:
        value = two_rows(kept_ref[4 * zs].astype(F32) + got_ref[4 * zs].astype(F32))
        own_ref[zs] = value.astype(F32)
        for send in sends:
            send[zs] = value


def summed(refs, at):
    a, b, c, d = (ref[at].astype(F32) for ref in refs)
    return (a + b) + (c + d)


def add_segment_kernel(at_ref, own_ref, a_ref, b_ref, c_ref, kept_ref, *sends):
    refs = (own_ref, a_ref, b_ref, c_ref)
    for j in range(4):
        value = summed(refs, at_ref[AT_Z] ^ j)
        if j == 0:
            kept_ref[0] = value
        else:
            sends[j - 1][0] = value.astype(BF16)
    if kept_ref.shape[0] > 1:
        value = two_rows(summed(refs, 4))
        kept_ref[1] = value.astype(F32)
        for send in sends:
            send[1] = value


def add_plane_kernel(at_ref, own_ref, a_ref, b_ref, c_ref, out_ref, *more):
    refs = (own_ref, a_ref, b_ref, c_ref)
    out_ref[...] = summed(refs, 0).astype(BF16)
    if more:
        more[0][...] = summed(refs, 1)


def add_half_kernel(at_ref, own_ref, got_ref, kept_ref, send_ref):
    kept_ref[...] = own_ref[0] + got_ref[0].astype(F32)
    send_ref[...] = (own_ref[1] + got_ref[1].astype(F32)).astype(BF16)


def add_both_kernel(at_ref, own_ref, got_ref, out_ref):
    out_ref[...] = (own_ref[...] + got_ref[...].astype(F32)).astype(BF16)


def both_split_kernel(at_ref, kept_ref, pieces, owna_ref, ownb_ref, a_ref, b_ref, got_ref):
    pieces.fill(got_ref)
    for half, (own, send, by) in enumerate(((owna_ref, a_ref, 1), (ownb_ref, b_ref, 2))):
        for i, j in enumerate((0, 3 - by, by, 3)):
            here = pl.ds((at_ref[AT_S] ^ j) * 4 + 2 * half, 2)
            value = kept_ref[here].astype(F32) + got_ref[here].astype(F32)
            if i < 2:
                own[i] = value
            else:
                send[i - 2] = value.astype(BF16)


def both_half_kernel(at_ref, owna_ref, ownb_ref, gota_ref, gotb_ref, kept_ref, a_ref, b_ref):
    for half, (own, got, send) in enumerate(((owna_ref, gota_ref, a_ref), (ownb_ref, gotb_ref, b_ref))):
        kept_ref[2 * half : 2 * half + 2] = own[0] + got[0].astype(F32)
        send[...] = (own[1] + got[1].astype(F32)).astype(BF16)


def both_planes_kernel(at_ref, own_ref, gota_ref, gotb_ref, kept_ref, send_ref, sc):
    sc[0:2] = own_ref[0:2] + gota_ref[...].astype(F32)
    sc[2:4] = own_ref[2:4] + gotb_ref[...].astype(F32)
    for i, j in enumerate((0, 2, 1, 3)):
        value = sc[at_ref[AT_Z] ^ j]
        if i < 2:
            kept_ref[i] = value
        else:
            send_ref[i - 2] = value.astype(BF16)


class Plain:
    split = False

    def __init__(self, sizes, at):
        self.sizes, self.at = sizes, at
        self.order = at.at[AT_S].set(0)

    def first_layer(self, first, x):
        self.shares = first
        return x

    def next_layer(self, x, *wait):
        return x

    next_layer_two = next_layer

    def first(self, labels, pairs, *wait):
        x, rows = self.shares, D // (2 * self.sizes["z"])
        emb = lax.all_gather(x[0, :rows], ("z", "c"), axis=0, tiled=True)
        mods = lax.psum(x[1].astype(F32) + x[2].astype(F32), ("z", "c"))
        got = lax.ppermute(labels, CHIP, pairs)
        label = jnp.where(self.at[AT_OWN] == 1, labels, got)[self.at[AT_WHICH]]
        return emb, mods, self.at.at[AT_LABEL].set(label)

    def columns(self, stack, *wait):
        return (stack,)

    def placed(self, own, *wait):
        return lax.all_gather(own[0], ("z", "c"), axis=1, tiled=True)

    def total(self, x):
        return lax.psum(x, ("z", "c")), jnp.zeros_like(x)

    def core(self, g):
        own = lax.psum_scatter(g[0].astype(F32), ("z", "c"), scatter_dimension=1, tiled=True)
        return lax.psum(own, "s"), lax.psum(g[1][0].astype(F32), CHIP)

    def core_both(self, g, count):
        return self.core(g)

    def segment(self, x, flops=0):
        return x

    plane = both_one = both_planes = planes_one = planes_two = segment

    def shared(self, x, wait=()):
        return [x[0][j].astype(BF16) for j in range(4)]

    far_shared = shared


class Squares(Plain):
    split = True

    def __init__(self, sizes, at):
        self.sizes, self.at, self.order = sizes, at, at

    def across(self, x, axis):
        return [swap(x, axis, 4, by) for by in (1, 2, 3)]

    def doubled(self, x, axis):
        x = jnp.stack([x, swap(x, axis, 4, 1)])
        return jnp.concatenate([x, swap(x, axis, 4, 2)])

    def first_layer(self, first, x):
        pieces = [x] + self.across(x, "z")
        self.shares = jnp.stack([p[3:] for p in pieces])
        return jnp.stack([p[:3] for p in pieces])

    def next_layer(self, x, *wait):
        return jnp.stack([x[0], swap(after(x[0], *wait), "z", 4, 1)])

    def next_layer_two(self, x, *wait):
        return jnp.concatenate([x, swap(after(x, *wait), "z", 4, 2)])

    def first(self, labels, pairs, *wait):
        own = after(self.shares, *wait)
        return call(
            first_kernel,
            "first",
            [((D, ECOLS), BF16), ((48, D), F32), ((AT_LABEL + 1,), jnp.int32)],
            [self.at, own, *self.pieces(own, 2)[0]],
            cost(0, 1e4),
            out_spaces=[VMEM, VMEM, SMEM],
        )

    def columns(self, stack, *wait):
        return [stack] + self.across(after(stack, *wait), "s")

    def placed(self, own, *wait):
        got = [swap(after(x, *wait) if i else x, "c", 2, 1) for i, x in enumerate(own)]
        return placed(self.at, own, got)

    def total(self, x):
        one, two, three = self.across(x, "z")
        x = (x + one) + (two + three)
        return x, swap(x, "c", 2, 1)

    def run(self, kernel, name, outs, inputs, scratch=(), flops=0):
        return call(kernel, name, outs, [self.at, *inputs], cost(flops, 1e5), scratch)

    def pieces(self, x, parts):
        cuts = [x.shape[0] * i // parts for i in range(parts + 1)]
        return [swap(x[a:b], "c", 2, 1) for a, b in zip(cuts[:-1], cuts[1:])], cuts

    def core(self, g):
        kept, sent = g
        count, rows, width = kept.shape
        full = (4 + count % 4, rows, width)
        got, cuts = self.pieces(sent, 2)
        outs = [(full, F32)] + [(full, BF16)] * 3
        return self.run(
            lambda at, kept, *refs: add_core_kernel(at, kept, Rows(refs[:2], cuts), *refs[2:]),
            "add_core", outs, [kept, *got], [pltpu.VMEM(kept.shape, BF16)],
        )

    def planes_one(self, x):
        own, send = x
        one = own.shape[1:]
        outs = [(one, F32), (one, BF16)]
        return self.run(add_half_kernel, "add_half", outs, [own, swap(send, "z", 4, 1)])

    def planes_two(self, x):
        own, send = x
        outs = [(own.shape, BF16)]
        return self.run(add_both_kernel, "add_both", outs, [own, swap(send, "z", 4, 2)])

    def core_both(self, g, count):
        kept, sent = g
        rows, width = kept.shape[1:]
        part = (2, 2, rows, width)
        got, cuts = self.pieces(sent, count)
        n = 2 + len(got)
        return self.run(
            lambda *refs: both_split_kernel(*refs[:2], Rows(refs[2:n], cuts), *refs[n:]),
            "both_split", [(part, F32)] * 2 + [(part, BF16)] * 2,
            [kept, *got], [pltpu.VMEM(kept.shape, BF16)],
        )

    def both_one(self, x, flops=0):
        own_a, own_b, a, b = x
        part = own_a.shape[1:]
        return self.run(
            both_half_kernel, "both_half", [((4,) + part[1:], F32)] + [(part, BF16)] * 2,
            [own_a, own_b, swap(a, "s", 4, 1), swap(b, "s", 4, 2)], flops=flops,
        )

    def both_planes(self, x):
        own, a, b = x
        part = (2,) + own.shape[1:]
        return self.run(
            both_planes_kernel, "both_planes", [(part, F32), (part, BF16)],
            [own, swap(a, "s", 4, 2), swap(b, "s", 4, 1)], [pltpu.VMEM(own.shape, F32)],
        )

    def segment(self, x):
        own, *sends = x
        count, rows, width = own.shape
        one = (count - 3, rows, width)
        got = [swap(y, "s", 4, j + 1) for j, y in enumerate(sends)]
        return call(
            add_segment_kernel, "add_segment", [(one, F32)] + [(one, BF16)] * 3,
            [self.at, own, *got], cost(0, 1e5),
        )

    def plane(self, x):
        own, *sends = x
        count, rows, width = own.shape
        got = [swap(y, "z", 4, j + 1) for j, y in enumerate(sends)]
        return call(
            add_plane_kernel, "add_plane",
            [((rows, width), BF16)] + [((rows, width), F32)] * (count - 1),
            [self.at, own, *got], cost(0, 1e5),
        )

    def shared(self, x, wait=()):
        return [x[0]] + self.across(after(x[0], *wait), "s")

    def far_shared(self, x, wait=()):
        pieces = self.doubled(after(x[0], *wait), "s")
        return [pieces[j] for j in range(4)]


def lead_parts(emb_ref):
    lead = emb_ref[:, LEAD:EROWS].astype(BF16).astype(F32)
    gate = jax.nn.sigmoid(lead)
    return lead * gate, gate * (1.0 + lead * (1.0 - gate))


def ada_gradient(silu, sums_ref, layer, index):
    total = 0.0
    for group in range(GROUPS):
        at = 8 * (GROUPS * layer + group) + index
        total = total + silu[:, group : group + 1] * sums_ref[at : at + 1, :D]
    return total


def square_sum(v):
    return jnp.sum(v * v, axis=(0, 1), keepdims=True)


def gather_kernel(at_ref, *refs, widths):
    pieces, (emb_ref, ada_ref, sums_ref), outs = refs[:12], refs[12:15], refs[15:]
    ordered, (lead_ref, square_ref) = outs[:3], outs[3:]
    total = jnp.zeros((1, 1), F32)
    for k, ref in enumerate(ordered):
        squares = []
        for j in range(4):
            piece = pieces[4 * k + j][...]
            ref[at_ref[AT_S] ^ j] = piece
            squares.append(square_sum(piece.astype(F32)))
        total = total + ((squares[0] + squares[1]) + (squares[2] + squares[3]))
    silu, slope = lead_parts(emb_ref)
    rows = silu.shape[0]
    lane = lax.broadcasted_iota(jnp.int32, (rows, 128), 1)
    lead = jnp.zeros((rows, 128), F32)
    for group in range(GROUPS):
        d_silu = jnp.zeros((rows, 1), F32)
        for layer in range(LAYERS):
            for i in range(6):
                at = 8 * (GROUPS * layer + group) + i
                ada = ada_ref[layer, :, D * i : D * (i + 1)].astype(BF16).astype(F32)
                d_silu = d_silu + jnp.sum(ada * sums_ref[at : at + 1, :D], axis=-1, keepdims=True)
        value = d_silu * slope[:, group : group + 1]
        total = total + square_sum(value)
        lead = jnp.where(lane == group, value, lead)
    for layer in range(LAYERS):
        for i in range(6):
            total = total + square_sum(ada_gradient(silu, sums_ref, layer, i))
    lead_ref[...] = lead
    square_ref[...] = jnp.broadcast_to(total, square_ref.shape)


def gathered(at, pieces, emb_t, ada, sums):
    widths = [group[0].shape for group in pieces]
    return call(
        lambda *refs: gather_kernel(*refs, widths=widths),
        "gathered",
        [((4,) + shape, BF16) for shape in widths]
        + [((widths[0][0], 128), F32), ((8, 128), F32)],
        [at, *pieces[0], *pieces[1], *pieces[2], emb_t, ada, sums],
        cost(0, 4e6),
    )


def update_kernel(at_ref, *refs, rate):
    g1_ref, g2_ref, g3_ref, lead_ref, sums_ref, own_ref, got_ref = refs[:7]
    state = refs[7:28]
    outs, (loss_ref, norm_ref) = refs[28:49], refs[49:51]
    results, sems = refs[51:72], refs[72]
    squares = own_ref[0:1, 0:1] + got_ref[0:1, 0:1]
    norm = jnp.sqrt(squares)
    factor = CLIP / jnp.maximum(norm, CLIP)
    norm_ref[...] = norm
    loss_ref[...] = sums_ref[6:7, 0:1] + sums_ref[7:8, 0:1]
    silu, _ = lead_parts(state[0])
    rows = silu.shape[0]

    def advance(index, at, g):
        w_ref, m_ref, a_ref = (state[index + 7 * k] for k in range(3))
        g = g.astype(F32) * factor
        m = KEEP * m_ref[at] + g
        w = w_ref[at] - rate * (BOOST if index == 0 else 1.0) * (g + KEEP * m)
        results[index + 7][at] = m
        results[index][at] = w
        results[index + 14][at] = KEEP * a_ref[at] + (1.0 - KEEP) * w

    copies = []

    def send(index):
        for k in range(3):
            i = index + 7 * k
            copy = pltpu.make_async_copy(results[i], outs[i], sems.at[i])
            copy.start()
            copies.append(copy)

    every = slice(None)
    for layer in range(LAYERS):
        for i in range(6):
            g = ada_gradient(silu, sums_ref, layer, i)
            advance(5, (layer, every, slice(D * i, D * (i + 1))), g)
    send(5)
    qkv = (g3_ref, g2_ref)
    ff = ((g2_ref, D), (g1_ref, 0))
    for layer in range(LAYERS):
        ref, lane = ff[layer]
        for j in range(2):
            part = slice(HALF * j, HALF * (j + 1))
            advance(3, (layer, every, part), ref[j, :, lane : lane + HALF])
            advance(4, (layer, every, part), ref[2 + j, :, lane : lane + HALF])
    send(3)
    send(4)
    for layer in range(LAYERS):
        for j in range(3):
            advance(1, (layer, every, slice(D * j, D * (j + 1))), qkv[layer][j, :, :D])
    send(1)
    for j in range(3):
        advance(2, (0, every, slice(128 * j, 128 * (j + 1))), g2_ref[j, :, D + HALF : D + HALF + 128])
    advance(2, (1,), g2_ref[3, :, :D])
    send(2)
    col = lax.broadcasted_iota(jnp.int32, (512, PIXELS), 1)
    row = lax.broadcasted_iota(jnp.int32, (512, PIXELS), 0)
    back = jnp.logical_and(row // 256 == col % 2, row % 256 == col // 2).astype(BF16)
    g_head = jnp.concatenate([g1_ref[j, :, HALF : HALF + 128] for j in range(4)], axis=-1)
    advance(6, (every,), dot(g_head, back))
    send(6)
    lane = lax.broadcasted_iota(jnp.int32, (rows, 128), 1)
    for j in range(3):
        g = g3_ref[3, :, 128 * j : 128 * j + 128].astype(F32)
        width = min(128, EROWS - 128 * j)
        if LEAD < 128 * j + width:
            first = LEAD - 128 * j
            for group in range(GROUPS):
                g = jnp.where(lane == first + group, lead_ref[:, group : group + 1], g)
        advance(0, (every, slice(128 * j, 128 * j + width)), g[:, :width])
    send(0)
    for copy in copies:
        copy.wait()


def updated(at, g, lead, sums, own, got, state, rate):
    shapes = [(x.shape, F32) for x in state]
    scalar = [((1, 1), F32)] * 2
    inputs = [at, *g, lead, sums, own, got, *state]
    return call(
        lambda *refs: update_kernel(*refs, rate=rate),
        "updated",
        shapes + scalar,
        inputs,
        cost(0, 2e7),
        [pltpu.VMEM(shape, kind) for shape, kind in shapes] + [pltpu.SemaphoreType.DMA((21,))],
        limit=24,
        out_spaces=[HBM] * 21 + [VMEM] * 2,
    )


def per_device(sizes, *arrays):
    (tiles_in, truth_in, labels, var_ids, basis) = arrays[:5]
    masters = arrays[5:12]
    segments, dp = sizes["s"], sizes["z"] * 2
    micro = tiles_in.shape[0]
    assert segments == 2 * micro
    rows = D // dp
    s, z, c = (lax.axis_index(name) for name in CHIP)
    which, owner = s % micro, s // micro
    at = jnp.stack([s, z, c, c == owner, which, 0]).astype(jnp.int32)
    fast = segments == 4 and sizes["z"] == 4
    move = (Squares if fast else Plain)(sizes, at)
    cut = Cut(sizes["z"], rows, move.split)
    views = []
    for k in range(3):
        w = list(arrays[5 + 7 * k : 12 + 7 * k])
        w[0], w[4] = w[0].T, w[4].transpose(0, 2, 1)
        views += w

    pairs = []
    for a in range(segments):
        for b in range(sizes["z"]):
            base = (a * sizes["z"] + b) * 2
            pairs.append((base + a // micro, base + 1 - a // micro))
    pick = lambda x: lax.dynamic_index_in_dim(x, which, 0, keepdims=False).T

    first, *bundles = packed(at, labels, views[:7], fast)
    stack0 = move.first_layer(first, bundles[0])
    tiles = pick(tiles_in)
    tiles_got = lax.ppermute(tiles, CHIP, pairs)
    columns0 = move.columns(stack0)
    stack1 = move.next_layer(bundles[1])
    emb, mods, at = move.first(labels, pairs, tiles_got, stack1)
    stack1 = move.next_layer_two(stack1, emb)
    vid4 = jnp.pad(jnp.repeat(var_ids, 4), (0, D - PIXELS), constant_values=-1)[None].astype(
        jnp.int32
    )
    h0, agg, x_all, embk = embed(at, tiles, tiles_got, emb, vid4)
    truth = pick(after(truth_in, h0, *columns0[1:]))
    half = truth.shape[1] // 2
    lanes = lambda core: jnp.where(core == 0, truth[:, :half], truth[:, half:])
    truth_got = lax.ppermute(lanes(1 - c), CHIP, pairs)
    truth = lanes(c)
    w0 = move.placed(columns0, h0, stack1)
    columns1 = move.columns(stack1, h0, *columns0[1:])
    h1, q0, own0, other0, att0, lse0, *kept = block_forward(after(at, truth_got), h0, mods, w0)
    w1 = move.placed(columns1, h1)
    q1, own1 = qkv_rows(at, h1, mods, w1)
    other1 = swap(own1, "c", 2, 1)
    d_mid, d_att, att1, lse1, g_out, dmod1, loss, *g_first = turn(
        at, cut, h1, q1, own1, other1, mods, w1, truth, truth_got, basis, 1.0 / (micro * dp)
    )
    d_q, d_k, d_v, *sent = attention_back(at, q1, own1, other1, lse1, att1, d_att, finish=True)
    got = [swap(x, "c", 2, 1) for x in sent]
    first = move.core_both(g_first, 1)
    d_mid, d_att, dmod1, dmod0, *g_second = between(
        after(at, *first), cut, [d_q, d_k, d_v, *got], h1, d_mid, g_out, dmod1, mods, w1, [att0, *kept], w0
    )
    first = move.both_one(first, 1e10)
    second = move.core_both([after(g_second[0], *first), g_second[1]], 3)
    d_q, d_k, d_v = attention_back(after(at, *first, *second), q0, own0, other0, lse0, att0, d_att)
    first = move.both_planes([after(first[0], d_q), *first[1:]])
    g_third = last(
        after(at, *first), cut, [d_q, d_k, d_v], h0, d_mid, dmod0, dmod1, loss, mods, w0, x_all, agg, embk, vid4
    )
    first = move.planes_one(first)
    second = move.both_one(second)
    third = move.core([after(g_third[0], *first), after(g_third[1], *first, *second)])
    first = move.planes_two([after(first[0], *third), first[1]])
    second = move.planes_one(move.both_planes(second))
    third = move.segment([after(third[0], *first, *second), *third[1:]])
    second = move.planes_two(second)
    ends = [move.far_shared(first), move.shared(second)]
    third = move.plane(third)
    ends.append(move.shared(third))
    sums = third[1]

    g1, g2, g3, lead_g, squares = gathered(move.order, ends, views[0], views[5], sums)
    own, got = move.total(squares)
    count = sum(w.size for w in masters) * dp
    rate = 0.02 * math.sqrt(count) / CLIP
    *new, loss_value, norm = updated(at, (g1, g2, g3), lead_g, sums, own, got, views, rate)
    for k in range(3):
        new[7 * k] = new[7 * k].T
        new[7 * k + 4] = new[7 * k + 4].transpose(0, 2, 1)
    return (loss_value.reshape(()), norm.reshape(()), *new)


def solution(mesh):
    segments, dp = mesh.shape["segment"], mesh.shape["dp"]
    sizes = {"s": segments, "z": dp // 2, "c": 2}
    split = Mesh(mesh.devices.reshape(segments, dp // 2, 2), CHIP)
    d = ("z", "c")
    weights = (
        P(None, d),
        P(None, d, None),
        P(None, d, None),
        P(None, d, None),
        P(None, None, d),
        P(None, d, None),
        P(d, None),
    )
    return jax.shard_map(
        lambda *arrays: per_device(sizes, *arrays),
        mesh=split,
        in_specs=(P(d, None, None), P(d, None, None), P(d), P(), P()) + weights * 3,
        out_specs=(P(), P()) + weights * 3,
        check_vma=False,
    )
```

```python
import math

import jax
import jax.numpy as jnp
from jax import lax
from jax.experimental import pallas as pl
from jax.experimental.pallas import tpu as pltpu
from jax.sharding import Mesh, PartitionSpec as P

D = 384
HEADS = 6
HEAD_DIM = 64
FF = 1536
VARS = 69
CHANNELS = 69
LONP = 128
LATP = 8
LAYERS = 2
GROUPS = 3
PIXELS = 276
LEAD = PIXELS + VARS + 1
EROWS = LEAD + GROUPS
ECOLS = 384
EPS = 1e-06
CLIP = 0.001
KEEP = 0.9
BOOST = 20.0
LABEL_LANE = D - 1
HALF = FF // 2

F32 = jnp.float32
BF16 = jnp.bfloat16
CHIP = ("s", "z", "c")


def dot(a, b):
    return jnp.dot(a, b, preferred_element_type=F32)


def dot_nt(a, b):
    return lax.dot_general(a, b, (((1,), (1,)), ((), ())), preferred_element_type=F32)


def dot_tn(a, b):
    return lax.dot_general(a, b, (((0,), (0,)), ((), ())), preferred_element_type=F32)


def parts(x, count):
    out = []
    for step in range(count):
        piece = x.astype(BF16)
        out.append(piece)
        if step < count - 1:
            x = x - piece.astype(F32)
    return out


def normal(v):
    centered = v - jnp.mean(v, axis=-1, keepdims=True)
    inverse = lax.rsqrt(jnp.mean(centered * centered, axis=-1, keepdims=True) + EPS)
    return centered * inverse, inverse


def normal_back(d_x, x, inverse):
    return inverse * (
        d_x - jnp.mean(d_x, axis=-1, keepdims=True) - x * jnp.mean(d_x * x, axis=-1, keepdims=True)
    )


def lane_below(limit, shape):
    return lax.broadcasted_iota(jnp.int32, shape, len(shape) - 1) < limit


def sublane(shape):
    return lax.broadcasted_iota(jnp.int32, shape, 0)


def same_group():
    col = lax.broadcasted_iota(jnp.int32, (D, D), 1)
    return (sublane((D, D)) // 4 == col // 4).astype(BF16)


def chosen_table(vid_ref):
    return (sublane((ECOLS, D)) - PIXELS == vid_ref[...]).astype(BF16)


def first_of_four(shape):
    return sublane(shape) % 4 == 0


def cost(flops, size, exps=0):
    return pl.CostEstimate(flops=int(flops), bytes_accessed=int(size), transcendentals=int(exps))


VMEM = pl.BlockSpec(memory_space=pltpu.VMEM)
SMEM = pl.BlockSpec(memory_space=pltpu.SMEM)
HBM = pl.BlockSpec(memory_space=pltpu.HBM)
CHUNK = 512
SPAN = 512
AT_S, AT_Z, AT_C, AT_OWN, AT_WHICH, AT_LABEL = range(6)


def call(kernel, name, outs, inputs, estimate, scratch=(), limit=24, in_space=VMEM, out_spaces=None):
    return pl.pallas_call(
        kernel,
        in_specs=[SMEM] + [in_space] * (len(inputs) - 1),
        out_specs=out_spaces or [VMEM] * len(outs),
        out_shape=[jax.ShapeDtypeStruct(shape, kind) for shape, kind in outs],
        scratch_shapes=list(scratch),
        compiler_params=pltpu.CompilerParams(vmem_limit_bytes=limit << 20),
        cost_estimate=estimate,
        name=name,
    )(*inputs)


def rows_at(index, size):
    return pl.ds(pl.multiple_of(index * size, size), size)


def after(x, *others):
    return lax.optimization_barrier((x, others))[0]


def column_sum(v):
    return jnp.sum(v, axis=0, keepdims=True)


class Cut:
    def __init__(self, pairs, rows, split):
        self.pairs, self.rows, self.split = pairs, rows, split

    def shapes(self, width, extra=False):
        if self.split:
            return [((4 * self.pairs + extra, self.rows, width), BF16)] * 2
        return [((4, D, width), BF16), ((1, 48, width), BF16)]

    def write(self, at_ref, outs, quarter, lane, value):
        value = value.astype(BF16)
        cols = slice(lane, lane + value.shape[-1])
        if not self.split:
            outs[0][quarter, :, cols] = value
            return
        first = at_ref[AT_C] == 0
        for z in range(self.pairs):
            row = 2 * z * self.rows
            one, two = value[row : row + self.rows], value[row + self.rows : row + 2 * self.rows]
            outs[0][quarter * self.pairs + z, :, cols] = jnp.where(first, one, two)
            outs[1][quarter * self.pairs + z, :, cols] = jnp.where(first, two, one)

    def write_extra(self, outs, value):
        value = value.astype(BF16)
        if self.split:
            outs[0][4 * self.pairs] = value
            outs[1][4 * self.pairs] = value
        else:
            outs[1][0] = value


def embed_kernel(
    at_ref, own_ref, got_ref, emb_ref, vid_ref,
    out_ref, agg_ref, x_ref, embk_ref, x_sc, bases_sc,
):
    tokens = own_ref.shape[1]
    half = tokens // 2
    emb = emb_ref[...]
    embk_ref[...] = emb.astype(F32).T.astype(BF16)
    query = jnp.broadcast_to(emb[:, LEAD - 1 : LEAD].astype(F32), (D, 128)).astype(BF16)
    by_row = dot_tn(emb, query)
    table = chosen_table(vid_ref)
    inside = sublane((D, 1)) < PIXELS
    proj = jnp.where(inside, by_row[:D, :1], 0.0)
    base = sum(dot_tn(table, p) for p in parts(by_row, 3))[:, :1]
    lane = lax.broadcasted_iota(jnp.int32, (D, D), 1)
    bases_sc[...] = jnp.where(lane % 4 == 0, dot(emb, table), 0.0).astype(BF16)
    group = same_group()
    x_sc[...] = jnp.zeros_like(x_sc)
    x_sc[:PIXELS] = jnp.where(at_ref[AT_OWN] == 1, own_ref[...], got_ref[...])

    def step(i, carry):
        here = rows_at(i, CHUNK)
        source = lax.rem(i * CHUNK + at_ref[AT_C] * half, tokens)
        packed = x_sc[:, pl.ds(pl.multiple_of(source, CHUNK), CHUNK)]
        x = packed.astype(F32)
        scores = sum(dot(group, p) for p in parts(x * proj, 3)) + base
        scores = jnp.where(inside, scores * D ** (-0.5), -1e30)
        e = jnp.exp(scores - jnp.max(scores, axis=0, keepdims=True))
        agg = e * (4.0 / column_sum(e))

        agg_ref[:, here] = agg
        x_ref[:, here] = packed
        total = dot(emb_ref[:, :D], (agg * x).astype(BF16))
        for p in parts(agg, 2):
            total = total + dot(bases_sc[...], p)
        out_ref[here, :] = total.T.astype(BF16)
        return carry

    lax.fori_loop(0, tokens // CHUNK, step, 0)


def embed(at, own, got, emb, vid4):
    tokens = own.shape[1]
    return call(
        embed_kernel,
        "embed",
        [
            ((tokens, D), BF16),
            ((D, tokens), F32),
            ((D, tokens), BF16),
            ((ECOLS, D), BF16),
        ],
        [at, own, got, emb, vid4],
        cost(1e6, 1e4),
        [pltpu.VMEM((D, tokens), BF16), pltpu.VMEM((D, D), BF16)],
    )


def embed_back(dh, x_ref, agg_ref, embk_ref, vid_ref):
    x = x_ref[...].astype(F32)
    agg = agg_ref[...]
    embk = embk_ref[...]
    table = chosen_table(vid_ref)
    bases = dot_tn(table, embk_ref[...]).astype(BF16)
    query = embk_ref[LEAD - 1 : LEAD, :].astype(F32)
    g_patch = dot((agg * x).astype(BF16), dh)
    d_agg = dot_nt(bases, dh)
    group = same_group()
    for p in parts(dot_nt(embk, dh) * x, 2):
        d_agg = d_agg + dot(group, p)
    inner = 0.25 * column_sum(agg * d_agg)
    d_scores = agg * (d_agg - inner) * D ** (-0.5)
    d_proj = jnp.sum(d_scores * x, axis=-1, keepdims=True)
    d_base = jnp.sum(d_scores, axis=-1, keepdims=True)
    d_base = jnp.where(first_of_four(d_base.shape), d_base, 0.0)
    d_bases = d_base * query
    for p in parts(jnp.where(first_of_four((D, 1)), agg, 0.0), 2):
        d_bases = d_bases + dot(p, dh)
    g_table = sum(dot(table, p) for p in parts(d_bases, 2))
    d_query = column_sum(embk.astype(F32) * d_proj) + column_sum(bases.astype(F32) * d_base)
    total = g_table + jnp.where(sublane((ECOLS, 1)) == LEAD - 1, d_query, 0.0)
    return total + g_patch + d_proj * query


def project(normed, w_ref, first, last):
    w = jnp.concatenate([w_ref[j, :, :D] for j in range(first, last)], axis=-1)
    return dot(normed, w).astype(BF16)


def mod_row(mods_ref, at_ref, layer, index):
    row = 8 * (layer * GROUPS + at_ref[AT_LABEL]) + index
    return mods_ref[pl.ds(row, 1), :D]


def first_norm(h, mods_ref, at_ref, layer):
    x, inverse = normal(h.astype(F32))
    scale = 1.0 + mod_row(mods_ref, at_ref, layer, 1)
    return (x * scale + mod_row(mods_ref, at_ref, layer, 0)).astype(BF16), x, inverse


def pair_masks():
    low = lane_below(HEAD_DIM, (1, 128))
    return low, jnp.logical_not(low)


def both(own_ref, other_ref, lane):
    here = slice(lane, lane + 128)
    return jnp.concatenate([own_ref[:, here], other_ref[:, here]])


def attend(here, q_ref, own_ref, other_ref, att_ref, lse_ref):
    zero = jnp.zeros((), BF16)
    rows = q_ref[here, :].shape[0]
    lane = lax.broadcasted_iota(jnp.int32, (rows, 128), 1)
    sums = jnp.zeros((rows, 128), F32)
    for pair in range(HEADS // 2):
        a = 128 * pair
        q = q_ref[here, a : a + 128] * 0.125
        keys = both(own_ref, other_ref, a)
        vals = both(own_ref, other_ref, D + a)
        mixed = jnp.zeros((rows, 128), F32)
        for which, mask in enumerate(pair_masks()):
            scores = dot_nt(q, jnp.where(mask, keys, zero))
            top = jnp.max(scores, axis=-1, keepdims=True)
            e = jnp.exp(scores - top)
            total = jnp.sum(e, axis=-1, keepdims=True)
            mixed = mixed + dot(e.astype(BF16), jnp.where(mask, vals, zero)) * (1.0 / total)
            sums = jnp.where(lane == 2 * pair + which, top + jnp.log(total), sums)
        att_ref[here, a : a + 128] = mixed.astype(BF16)
    lse_ref[here, :] = sums


def gelu_and_slope(u):
    k = math.sqrt(2.0 / math.pi)
    t = jnp.tanh(k * (u + 0.044715 * (u * u * u)))
    cdf = 0.5 * (1.0 + t)
    return u * cdf, cdf + 0.5 * u * (1.0 - t * t) * k * (1.0 + 3 * 0.044715 * (u * u))


def feed_forward(
    here, h, one, mods_ref, at_ref, layer, w_ref, act_ref, slope_ref, n2_ref=None, stored=lambda j: None
):
    middle = h.astype(F32) + mod_row(mods_ref, at_ref, layer, 2) * one
    x, _ = normal(middle)
    scale = 1.0 + mod_row(mods_ref, at_ref, layer, 4)
    n2 = (x * scale + mod_row(mods_ref, at_ref, layer, 3)).astype(BF16)
    if n2_ref is not None:
        n2_ref[here, :] = n2
    two = jnp.zeros(middle.shape, F32)
    for j in range(2):
        part = slice(HALF * j, HALF * (j + 1))
        act, slope = gelu_and_slope(dot(n2, w_ref[j, :, D : 3 * D]))
        slope_ref[here, part] = slope.astype(slope_ref.dtype)
        act = act.astype(BF16)
        act_ref[here, part] = act
        stored(j)
        two = two + dot_nt(act, w_ref[2 + j, :, D : 3 * D])
    return middle, two, middle + mod_row(mods_ref, at_ref, layer, 5) * two


def feed_back(
    here, d_out, one, two, middle, slope_ref, mods_ref, at_ref, layer, w_ref,
    dunits_ref, dtwo_ref, done_ref, dmid_ref, datt_ref, dmod_ref, n2_ref=None,
):
    d_out = d_out.astype(F32)
    d_two = (mod_row(mods_ref, at_ref, layer, 5) * d_out).astype(BF16)
    dtwo_ref[here, :] = d_two
    d_n2 = jnp.zeros(d_out.shape, F32)
    for j in range(2):
        part = slice(HALF * j, HALF * (j + 1))
        slope = slope_ref[here, part].astype(F32)
        d_units = (slope * dot(d_two, w_ref[2 + j, :, D : 3 * D])).astype(BF16)
        dunits_ref[here, part] = d_units
        d_n2 = d_n2 + dot_nt(d_units, w_ref[j, :, D : 3 * D])
    x, inverse = normal(middle)
    scale = 1.0 + mod_row(mods_ref, at_ref, layer, 4)
    if n2_ref is not None:
        n2_ref[here, :] = (x * scale + mod_row(mods_ref, at_ref, layer, 3)).astype(BF16)
    d_mid = d_out + normal_back(d_n2 * scale, x, inverse)
    dmid_ref[here, :] = d_mid
    d_one = (mod_row(mods_ref, at_ref, layer, 2) * d_mid).astype(BF16)
    done_ref[here, :] = d_one
    datt_ref[here, :] = dot_nt(d_one, w_ref[3, :, :D]).astype(BF16)
    dmod_ref[2:3] += column_sum(d_mid * one)
    dmod_ref[3:4] += column_sum(d_n2)
    dmod_ref[4:5] += column_sum(d_n2 * x)
    dmod_ref[5:6] += column_sum(d_out * two)


def feed_gradients(at_ref, cut, outs, lane, n2_ref, dunits_ref, dtwo_ref, act_ref):
    for j in range(2):
        part = slice(HALF * j, HALF * (j + 1))
        cut.write(at_ref, outs, j, lane, dot_tn(n2_ref[...], dunits_ref[:, part]))
        cut.write(at_ref, outs, 2 + j, lane, dot_tn(dtwo_ref[...], act_ref[:, part]))


def rows_scratch(count, widths):
    return [pltpu.VMEM((count, width), BF16) for width in widths]


def block_kernel(
    at_ref, h_ref, mods_ref, w_ref,
    out_ref, q_out, own_out, other_out, att_out, lse_out, one_out, mid_out, slope_out, act_out, two_out,
    q_ref, own_ref, other_ref, att_ref, lse_ref, one_ref, mid_ref, slope_ref, act_ref, two_ref, sems,
):
    count = out_ref.shape[0]

    normed, _, _ = first_norm(h_ref[:count], mods_ref, at_ref, 0)
    qkv = project(normed, w_ref, 0, 3)
    q_ref[...] = qkv[:, :D]
    own_ref[...] = qkv[:, D:]
    normed, _, _ = first_norm(h_ref[count:], mods_ref, at_ref, 0)
    other_ref[...] = project(normed, w_ref, 1, 3)
    early = [
        pltpu.make_async_copy(ref, out, sems.at[2, i])
        for i, (ref, out) in enumerate(((q_ref, q_out), (own_ref, own_out), (other_ref, other_out)))
    ]
    for copy in early:
        copy.start()
    kept = (
        (att_ref, att_out), (lse_ref, lse_out), (one_ref, one_out), (mid_ref, mid_out),
        (slope_ref, slope_out), (act_ref, act_out), (two_ref, two_out),
    )

    slope, act = kept[4:6]
    whole = [
        pltpu.make_async_copy(ref, out, sems.at[0, k])
        for k, (ref, out) in enumerate(kept[:4] + kept[6:])
    ]
    halves = [
        [
            pltpu.make_async_copy(ref.at[:, part], out.at[:, part], sems.at[1, 2 * j + k])
            for k, (ref, out) in enumerate((slope, act))
        ]
        for j, part in enumerate((pl.ds(0, HALF), pl.ds(HALF, HALF)))
    ]

    def start(*copies):
        for copy in copies:
            copy.start()

    here = slice(0, count)
    attend(here, q_ref, own_ref, other_ref, att_ref, lse_ref)
    one = dot(att_ref[...], w_ref[3, :, :D])
    one_ref[...] = one.astype(BF16)
    start(*whole[:3])
    middle, two, out = feed_forward(
        here, h_ref[:count], one, mods_ref, at_ref, 0, w_ref, act_ref, slope_ref,
        stored=lambda j: start(*halves[j]),
    )
    mid_ref[...] = middle
    start(whole[3])
    two_ref[...] = two.astype(BF16)
    start(whole[4])
    out_ref[...] = out.astype(BF16)
    for copy in early + whole + halves[0] + halves[1]:
        copy.wait()


def block_forward(at, h, mods, weights):
    count = h.shape[0] // 2
    kept = [(D, BF16), (2 * D, BF16), (2 * D, BF16), (D, BF16), (128, F32), (D, BF16), (D, F32)]
    kept += [(FF, BF16), (FF, BF16), (D, BF16)]
    kept = [((count, width), kind) for width, kind in kept]
    return call(
        block_kernel,
        "block_forward",
        [((count, D), BF16)] + kept,
        [at, h, mods, weights],
        cost(1e6, 1e4),
        [pltpu.VMEM(shape, kind) for shape, kind in kept] + [pltpu.SemaphoreType.DMA((3, 7))],
        limit=28,
        out_spaces=[VMEM] + [HBM] * len(kept),
    )


def qkv_kernel(at_ref, h_ref, mods_ref, w_ref, q_ref, kv_ref):
    normed, _, _ = first_norm(h_ref[...], mods_ref, at_ref, 1)
    qkv = project(normed, w_ref, 0, 3)
    q_ref[...] = qkv[:, :D]
    kv_ref[...] = qkv[:, D:]


def qkv_rows(at, h, mods, weights):
    count = h.shape[0]
    return call(
        qkv_kernel,
        "qkv_rows",
        [((count, D), BF16), ((count, 2 * D), BF16)],
        [at, h, mods, weights],
        cost(1e9, 3e6),
    )


def turn_kernel(
    at_ref, h_ref, q_ref, own_ref, other_ref, mods_ref, w_ref, truth_ref, got_ref, basis_ref,
    dmid_ref, datt_ref, att_ref, lse_ref, gout_ref, dmod_ref, loss_ref, keep_ref, send_ref,
    act_ref, dunits_ref, dtwo_ref, n2_ref, done_ref, flat_ref, dpred_ref, true_ref, slope_ref,
    basis_sc, *, seed, cut,
):
    count = h_ref.shape[0]
    outs = (keep_ref, send_ref)
    entries = LATP * CHANNELS * 2 * LONP
    dmod_ref[...] = jnp.zeros_like(dmod_ref)
    loss_ref[...] = jnp.zeros_like(loss_ref)
    row = lax.broadcasted_iota(jnp.int32, (PIXELS, 256), 0)
    col = lax.broadcasted_iota(jnp.int32, (PIXELS, 256), 1)
    truth = jnp.where(at_ref[AT_OWN] == 1, truth_ref[...], got_ref[...])
    for b in range(2):
        picked = dot_tn(truth, (row == 2 * col + b).astype(BF16))
        true_ref[:, 256 * b : 256 * b + 256] = picked.astype(BF16)
    to = lax.broadcasted_iota(jnp.int32, (256, 256), 0)
    source = lax.broadcasted_iota(jnp.int32, (256, 256), 1)
    order = (source == 2 * (to % LONP) + to // LONP).astype(BF16)
    for i, p in enumerate(parts(basis_ref[...], 2)):
        basis_sc[i] = dot(order, p).astype(BF16)

    for i in range(count // SPAN):
        attend(slice(i * SPAN, (i + 1) * SPAN), q_ref, own_ref, other_ref, att_ref, lse_ref)

    def step(i, carry):
        here = rows_at(i, CHUNK)
        one = dot(att_ref[here, :], w_ref[3, :, :D])
        middle, two, h2 = feed_forward(
            here, h_ref[here, :], one, mods_ref, at_ref, 1, w_ref, act_ref, slope_ref, n2_ref
        )
        x, inverse = normal(h2.astype(BF16).astype(F32))
        flat = x.astype(BF16)
        flat_ref[here, :] = flat
        hw = [w_ref[j, :, 3 * D : 3 * D + 128] for j in range(4)]
        pred = [dot(flat, w) for w in hw]
        pred = [jnp.concatenate(pred[:2], axis=-1), jnp.concatenate(pred[2:], axis=-1)]
        hi, lo = basis_sc[0], basis_sc[1]
        grads = [[], []]
        loss = jnp.zeros((1, 1), F32)
        for p in range(CHUNK // LONP):
            part = slice(p * LONP, (p + 1) * LONP)
            fine = rows_at(i * (CHUNK // LONP) + p, LONP)
            seen = parts(jnp.concatenate([pred[0][part], pred[1][part]], axis=0), 2)
            waves = dot_tn(hi, seen[0]) + (dot_tn(hi, seen[1]) + dot_tn(lo, seen[0]))
            want = jnp.concatenate([true_ref[fine, :256], true_ref[fine, 256:]], axis=0)
            target = dot_tn(hi, want) + dot_tn(lo, want)
            top, low = waves[:LONP], waves[LONP:]
            gap = (top * top + low * low) - (
                target[:LONP] * target[:LONP] + target[LONP:] * target[LONP:]
            )
            loss = loss + jnp.sum(gap * gap, axis=(0, 1), keepdims=True)
            scaled = gap * (4.0 * seed / entries)
            d_waves = parts(jnp.concatenate([scaled * top, scaled * low], axis=0), 2)
            d_seen = dot(hi, d_waves[0]) + (dot(hi, d_waves[1]) + dot(lo, d_waves[0]))
            d_seen = d_seen.astype(BF16)
            grads[0].append(d_seen[:LONP])
            grads[1].append(d_seen[LONP:])
        loss_ref[...] += jnp.broadcast_to(loss * (seed / entries), loss_ref.shape)
        d_flat = jnp.zeros((CHUNK, D), F32)
        for b in range(2):
            whole = jnp.concatenate(grads[b], axis=0)
            dpred_ref[here, 256 * b : 256 * b + 256] = whole
            for j in range(2):
                d_flat = d_flat + dot_nt(whole[:, 128 * j : 128 * j + 128], hw[2 * b + j])
        d_h2 = normal_back(d_flat, x, inverse).astype(BF16)
        feed_back(
            here, d_h2, one, two, middle, slope_ref, mods_ref, at_ref, 1, w_ref,
            dunits_ref, dtwo_ref, done_ref, dmid_ref, datt_ref, dmod_ref,
        )
        return carry

    lax.fori_loop(0, count // CHUNK, step, 0)
    feed_gradients(at_ref, cut, outs, 0, n2_ref, dunits_ref, dtwo_ref, act_ref)
    for j in range(4):
        cut.write(at_ref, outs, j, HALF, dot_tn(flat_ref[...], dpred_ref[:, 128 * j : 128 * j + 128]))
    gout_ref[...] = dot_tn(att_ref[...], done_ref[...])


def turn(at, cut, h, q, own, other, mods, weights, truth, got, basis, seed):
    count = h.shape[0]
    return call(
        lambda *refs: turn_kernel(*refs, seed=seed, cut=cut),
        "turn",
        [
            ((count, D), F32),
            ((count, D), BF16),
            ((count, D), BF16),
            ((count, 128), F32),
            ((D, D), F32),
            ((8, D), F32),
            ((8, 128), F32),
        ]
        + cut.shapes(HALF + 128),
        [at, h, q, own, other, mods, weights, truth, got, basis],
        cost(4e9, 4e6),
        rows_scratch(count, [FF, FF, D, D, D, D, 512, 512])
        + [pltpu.VMEM((count, FF), F32), pltpu.VMEM((2, 256, 256), BF16)],
        limit=32,
    )


def attention_back_kernel(
    at_ref, q_ref, own_ref, other_ref, lse_ref, att_ref, datt_ref, dq_ref, *outs, finish,
):
    zero = jnp.zeros((), BF16)
    count = own_ref.shape[0]
    dk_sc, dv_sc = outs[-2:] if finish else outs[:2]
    dk_sc[...] = jnp.zeros_like(dk_sc)
    dv_sc[...] = jnp.zeros_like(dv_sc)

    def step(i, carry):
        rows = rows_at(i, SPAN)
        for pair in range(HEADS // 2):
            a = 128 * pair
            here = slice(a, a + 128)
            q = q_ref[rows, here]
            d_att = datt_ref[rows, here]
            keys = both(own_ref, other_ref, a)
            vals = both(own_ref, other_ref, D + a)
            dots = d_att.astype(F32) * att_ref[rows, here].astype(F32)
            d_q = jnp.zeros((SPAN, 128), F32)
            d_k = jnp.zeros((keys.shape[0], 128), F32)
            d_v = jnp.zeros((keys.shape[0], 128), F32)
            for which, mask in enumerate(pair_masks()):
                head = 2 * pair + which
                k = jnp.where(mask, keys, zero)
                v = jnp.where(mask, vals, zero)
                inner = jnp.sum(jnp.where(mask, dots, 0.0), axis=-1, keepdims=True)
                probs = jnp.exp(dot_nt(q * 0.125, k) - lse_ref[rows, head : head + 1])
                d_scores = (probs * (dot_nt(d_att, v) - inner)).astype(BF16)
                d_q = d_q + dot(d_scores, k)
                d_k = d_k + dot_tn(d_scores, jnp.where(mask, q, zero))
                d_v = d_v + dot_tn(probs.astype(BF16), jnp.where(mask, d_att, zero))
            dq_ref[rows, here] = (d_q * 0.125).astype(BF16)
            dk_sc[:, here] += d_k * 0.125
            dv_sc[:, here] += d_v
        return carry

    lax.fori_loop(0, count // SPAN, step, 0)
    if finish:
        dk_ref, dv_ref, dk_send, dv_send = outs[:4]
        dk_ref[...] = dk_sc[:count]
        dv_ref[...] = dv_sc[:count]
        dk_send[...] = dk_sc[count:].astype(BF16)
        dv_send[...] = dv_sc[count:].astype(BF16)


def attention_back(at, q, own, other, lse, att, d_att, finish=False):
    count = q.shape[0]
    full = ((2 * count, D), F32)
    outs = [((count, D), F32)] * 2 + [((count, D), BF16)] * 2 if finish else [full] * 2
    return call(
        lambda *refs: attention_back_kernel(*refs, finish=finish),
        "attention_back",
        [((count, D), BF16)] + outs,
        [at, q, own, other, lse, att, d_att],
        cost(5e9, 1e6),
        [pltpu.VMEM(*full)] * 2 if finish else (),
    )


def qkv_back(
    at_ref, cut, outs, lane, layer, d_q, d_k, d_v, h_ref, dmid_ref, gout_ref, mods_ref, w_ref,
):
    count, rows = d_q.shape[0], d_k.shape[0]
    normed, x, inverse = first_norm(h_ref[:rows], mods_ref, at_ref, layer)
    first = dot_nt(d_q, w_ref[0, :, :D])
    rest = dot_nt(d_k, w_ref[1, :, :D]) + dot_nt(d_v, w_ref[2, :, :D])
    if rows > count:
        d_n = jnp.concatenate([rest[:count] + first, rest[count:]], axis=0)
    else:
        d_n = rest + first
    cut.write(at_ref, outs, 0, lane, dot_tn(normed[:count], d_q))
    cut.write(at_ref, outs, 1, lane, dot_tn(normed, d_k))
    cut.write(at_ref, outs, 2, lane, dot_tn(normed, d_v))
    if gout_ref is not None:
        cut.write(at_ref, outs, 3, lane, gout_ref[...])
    scale = 1.0 + mod_row(mods_ref, at_ref, layer, 1)
    d_h = normal_back(d_n * scale, x, inverse)
    if rows > count:
        d_h = jnp.concatenate([d_h[:count] + dmid_ref[...], d_h[count:]], axis=0)
    else:
        d_h = d_h + dmid_ref[...]
    return d_h.astype(BF16), column_sum(d_n), column_sum(d_n * x)


def between_kernel(
    at_ref, dq_ref, dk_ref, dv_ref, dk_got, dv_got, h_ref, dmid_ref, gout_ref, dmod_ref, mods_ref, w1_ref,
    one_ref, two_ref, mid_ref, slope_ref, act_ref, att_ref, w0_ref,
    dmid_out, datt_out, dmod_out, dmod_next, keep_ref, send_ref,
    dh_sc, dunits_ref, dtwo_ref, n2_ref, done_ref, *, cut,
):
    outs = (keep_ref, send_ref)
    d_k = (dk_ref[...] + dk_got[...].astype(F32)).astype(BF16)
    d_v = (dv_ref[...] + dv_got[...].astype(F32)).astype(BF16)
    d_h, shift, scale = qkv_back(
        at_ref, cut, outs, 0, 1, dq_ref[...], d_k, d_v, h_ref, dmid_ref, gout_ref, mods_ref, w1_ref,
    )
    dmod_out[...] = dmod_ref[...]
    dmod_out[0:1] = shift
    dmod_out[1:2] = scale
    dh_sc[...] = d_h
    dmod_next[...] = jnp.zeros_like(dmod_next)

    def step(i, carry):
        here = rows_at(i, CHUNK)
        feed_back(
            here, dh_sc[here, :], one_ref[here, :].astype(F32), two_ref[here, :].astype(F32),
            mid_ref[here, :], slope_ref, mods_ref, at_ref, 0, w0_ref,
            dunits_ref, dtwo_ref, done_ref, dmid_out, datt_out, dmod_next, n2_ref,
        )
        return carry

    lax.fori_loop(0, dh_sc.shape[0] // CHUNK, step, 0)
    feed_gradients(at_ref, cut, outs, D, n2_ref, dunits_ref, dtwo_ref, act_ref)
    g_out = dot_tn(att_ref[...], done_ref[...])
    for j in range(4):
        tile = g_out[:, 128 * j : 128 * j + 128] if j < 3 else jnp.zeros((D, 128), F32)
        cut.write(at_ref, outs, j, D + HALF, tile)


def between(at, cut, grads, h, d_mid, g_out, dmod, mods, w1, kept, w0):
    att, one, mid, slope, act, two = kept
    count = d_mid.shape[0]
    return call(
        lambda *refs: between_kernel(*refs, cut=cut),
        "between",
        [((count, D), F32), ((count, D), BF16), ((8, D), F32), ((8, D), F32)]
        + cut.shapes(D + HALF + 128),
        [at, *grads, h, d_mid, g_out, dmod, mods, w1, one, two, mid, slope, act, att, w0],
        cost(1e9, 1e6),
        rows_scratch(count, [D, FF, D, D, D]),
        limit=28,
    )


def last_kernel(
    at_ref, dq_ref, dk_ref, dv_ref, h_ref, dmid_ref, dmod0_ref, dmod1_ref, loss_ref,
    mods_ref, w_ref, x_ref, agg_ref, embk_ref, vid_ref, keep_ref, send_ref, sums_sc, *, cut,
):
    outs = (keep_ref, send_ref)
    d_q = dq_ref[...]
    d_k, d_v = dk_ref[...].astype(BF16), dv_ref[...].astype(BF16)
    d_h, shift, scale = qkv_back(
        at_ref, cut, outs, 0, 0, d_q, d_k, d_v, h_ref, dmid_ref, None, mods_ref, w_ref,
    )
    sums_sc[...] = jnp.zeros_like(sums_sc)
    for group in range(GROUPS):
        hot = (at_ref[AT_LABEL] == group).astype(F32)
        for layer, ref in enumerate((dmod0_ref, dmod1_ref)):
            at = 8 * (GROUPS * layer + group)
            sums_sc[at : at + 8, :D] = ref[...] * hot
        sums_sc[8 * group : 8 * group + 1, :D] = shift * hot
        sums_sc[8 * group + 1 : 8 * group + 2, :D] = scale * hot
    loss = loss_ref[0:1, 0:1]
    top = loss.astype(BF16).astype(F32)
    sums_sc[6:7, :] = jnp.broadcast_to(top, (1, ECOLS))
    sums_sc[7:8, :] = jnp.broadcast_to(loss - top, (1, ECOLS))
    cut.write_extra(outs, sums_sc[...])
    cut.write(at_ref, outs, 3, 0, embed_back(d_h, x_ref, agg_ref, embk_ref, vid_ref).T)


def last(at, cut, grads, h, d_mid, dmod0, dmod1, loss, mods, w0, x, agg, embk, vid4):
    return call(
        lambda *refs: last_kernel(*refs, cut=cut),
        "last",
        cut.shapes(ECOLS, True),
        [at, *grads, h, d_mid, dmod0, dmod1, loss, mods, w0, x, agg, embk, vid4],
        cost(1e9, 1e6),
        [pltpu.VMEM((48, ECOLS), F32)],
        limit=28,
    )


def swap(x, axis, size, by):
    return lax.ppermute(x, axis, [(i, i ^ by) for i in range(size)])


def place_kernel(at_ref, *refs, rows):
    out_ref, inputs = refs[-1], refs[:-1]
    s, z, c = at_ref[AT_S], at_ref[AT_Z], at_ref[AT_C]
    for jc in range(2):
        for js in range(4):
            source = inputs[4 * jc + js]
            for jz in range(4):
                at = rows_at((z ^ jz) * 2 + (c ^ jc), rows)
                if len(source.shape) == 3:
                    out_ref[s ^ js, at, :] = source[jz]
                    continue
                for k in range(source.shape[1]):
                    out_ref[s ^ js, at, D * k : D * (k + 1)] = source[jz, k]


def placed(at, own, got):
    rows = own[0].shape[-2]
    width = math.prod(own[0].shape[1:]) // rows
    return call(
        lambda *refs: place_kernel(*refs, rows=rows),
        "placed",
        [((4, 8 * rows, width), BF16)],
        [at, *own, *got],
        cost(0, 1e5),
        limit=8,
    )[0]


def first_kernel(at_ref, own_ref, gota_ref, gotb_ref, emb_ref, mods_ref, out_ref):
    rows = own_ref.shape[2]
    total = jnp.zeros((rows, D), F32)
    for jc in range(2):
        for jz in range(4):
            ref, i = (own_ref, jz) if jc == 0 else ((gota_ref, gotb_ref)[jz // 2], jz % 2)
            row = (at_ref[AT_Z] ^ jz) * 2 + (at_ref[AT_C] ^ jc)
            emb_ref[rows_at(row, rows), :] = ref[i, 0]
            total = total + (ref[i, 1].astype(F32) + ref[i, 2].astype(F32))
    mods_ref[...] = total
    for i in range(AT_LABEL):
        out_ref[i] = at_ref[i]
    labels = [ref[0, 1, 0:8, 0:128].astype(F32) for ref in (own_ref, gota_ref)]
    labels = jnp.where(at_ref[AT_OWN] == 1, labels[0], labels[1])
    picked = jnp.where(sublane((8, 128)) == 6 + at_ref[AT_WHICH], labels, 0.0)
    out_ref[AT_LABEL] = jnp.max(picked).astype(jnp.int32)


def pack_kernel(at_ref, labels_ref, *refs, split):
    sources, (first_ref, zero_ref, one_ref), held, sems = refs[:7], refs[7:10], refs[10:17], refs[17]
    copies = [
        pltpu.make_async_copy(source, target, sems.at[i])
        for i, (source, target) in enumerate(zip(sources, held))
    ]
    for copy in copies:
        copy.start()
    emb_ref, qkv_ref, out_ref, up_ref, down_ref, ada_ref, head_ref = held
    rows = emb_ref.shape[0]
    blocks = first_ref
    blocks[...] = jnp.zeros_like(blocks)
    for i in (1, 2, 3, 4, 6):
        copies[i].wait()
    col = lax.broadcasted_iota(jnp.int32, (PIXELS, 128), 0)
    lane = lax.broadcasted_iota(jnp.int32, (PIXELS, 128), 1)
    for j in range(4):

        def fill(j=j):
            for layer, ref in enumerate((zero_ref, one_ref)):
                part = qkv_ref[layer, :, D * j : D * (j + 1)] if j < 3 else out_ref[layer]
                source = (up_ref if j < 2 else down_ref)[layer]
                source = source[:, HALF * (j % 2) : HALF * (j % 2 + 1)].astype(BF16)
                if split and layer == 0:
                    ref[0] = part.astype(BF16)
                    ref[1] = source[:, :D]
                    ref[2] = source[:, D:]
                    continue
                at = 0 if split else j
                ref[at, :, :D] = part.astype(BF16)
                ref[at, :, D : 3 * D] = source
            wide = lane + 128 * (j % 2)
            pick = jnp.logical_and(col == 2 * wide + j // 2, wide < PIXELS // 2).astype(BF16)
            one_ref[0 if split else j, :, 3 * D :] = dot(head_ref[...].astype(BF16), pick).astype(BF16)

        if split:
            pl.when(at_ref[AT_S] == j)(fill)
        else:
            fill()
    copies[0].wait()
    copies[5].wait()
    blocks[0, :rows, :EROWS] = emb_ref[...].astype(BF16)
    silu, _ = lead_parts(emb_ref)
    for layer in range(LAYERS):
        for i in range(6):
            ada = ada_ref[layer, :, D * i : D * (i + 1)].astype(BF16).astype(F32)
            for g in range(GROUPS):
                at = 8 * (GROUPS * layer + g) + i
                value = column_sum(silu[:, g : g + 1] * ada)
                top = value.astype(BF16)
                blocks[1, at : at + 1, :] = top
                blocks[2, at : at + 1, :] = (value - top.astype(F32)).astype(BF16)
    for i in range(2):
        label = jnp.full((1, D), labels_ref[i], jnp.int32).astype(F32).astype(BF16)
        blocks[1, 6 + i : 7 + i, :] = label
    if split:
        zero_ref[3:6] = blocks[...]


def packed(at, labels, weights, split):
    rows = weights[0].shape[0]
    quarters = 1 if split else 4
    return pl.pallas_call(
        lambda *refs: pack_kernel(*refs, split=split),
        in_specs=[SMEM, SMEM] + [HBM] * 7,
        out_specs=[VMEM] * 3,
        out_shape=[
            jax.ShapeDtypeStruct((3, 48, ECOLS), BF16),
            jax.ShapeDtypeStruct((6, rows, D) if split else (4, rows, 3 * D), BF16),
            jax.ShapeDtypeStruct((quarters, rows, 3 * D + 128), BF16),
        ],
        scratch_shapes=[pltpu.VMEM(w.shape, F32) for w in weights] + [pltpu.SemaphoreType.DMA((7,))],
        compiler_params=pltpu.CompilerParams(vmem_limit_bytes=60 << 20),
        cost_estimate=cost(0, 1e6),
        name="packed",
    )(at, labels, *weights)


def two_rows(v):
    loss = v[6:7] + v[7:8]
    top = loss.astype(BF16).astype(F32)
    row = sublane(v.shape)
    return jnp.where(row == 6, top, jnp.where(row == 7, loss - top, v)).astype(BF16)


class Rows:
    def __init__(self, refs, cuts):
        self.refs, self.cuts = refs, cuts

    def fill(self, out):
        for ref, a, b in zip(self.refs, self.cuts[:-1], self.cuts[1:]):
            out[a:b] = ref[...]


def add_core_kernel(at_ref, kept_ref, pieces, own_ref, *refs):
    sends, got_ref = refs[:3], refs[3]
    pieces.fill(got_ref)
    zs = 4
    for j in range(4):
        here = pl.ds((at_ref[AT_S] ^ j) * zs, zs)
        value = kept_ref[here].astype(F32) + got_ref[here].astype(F32)
        if j == 0:
            own_ref[:zs] = value
        else:
            sends[j - 1][:zs] = value.astype(BF16)
    if own_ref.shape[0] > zs:
        value = two_rows(kept_ref[4 * zs].astype(F32) + got_ref[4 * zs].astype(F32))
        own_ref[zs] = value.astype(F32)
        for send in sends:
            send[zs] = value


def summed(refs, at):
    a, b, c, d = (ref[at].astype(F32) for ref in refs)
    return (a + b) + (c + d)


def add_segment_kernel(at_ref, own_ref, a_ref, b_ref, c_ref, kept_ref, *sends):
    refs = (own_ref, a_ref, b_ref, c_ref)
    for j in range(4):
        value = summed(refs, at_ref[AT_Z] ^ j)
        if j == 0:
            kept_ref[0] = value
        else:
            sends[j - 1][0] = value.astype(BF16)
    if kept_ref.shape[0] > 1:
        value = two_rows(summed(refs, 4))
        kept_ref[1] = value.astype(F32)
        for send in sends:
            send[1] = value


def add_plane_kernel(at_ref, own_ref, a_ref, b_ref, c_ref, out_ref, *more):
    refs = (own_ref, a_ref, b_ref, c_ref)
    out_ref[...] = summed(refs, 0).astype(BF16)
    if more:
        more[0][...] = summed(refs, 1)


def add_half_kernel(at_ref, own_ref, got_ref, kept_ref, send_ref):
    kept_ref[...] = own_ref[0] + got_ref[0].astype(F32)
    send_ref[...] = (own_ref[1] + got_ref[1].astype(F32)).astype(BF16)


def add_both_kernel(at_ref, own_ref, got_ref, out_ref):
    out_ref[...] = (own_ref[...] + got_ref[...].astype(F32)).astype(BF16)


def both_split_kernel(at_ref, kept_ref, pieces, owna_ref, ownb_ref, a_ref, b_ref, got_ref):
    pieces.fill(got_ref)
    for half, (own, send, by) in enumerate(((owna_ref, a_ref, 1), (ownb_ref, b_ref, 2))):
        for i, j in enumerate((0, 3 - by, by, 3)):
            here = pl.ds((at_ref[AT_S] ^ j) * 4 + 2 * half, 2)
            value = kept_ref[here].astype(F32) + got_ref[here].astype(F32)
            if i < 2:
                own[i] = value
            else:
                send[i - 2] = value.astype(BF16)


def both_half_kernel(at_ref, owna_ref, ownb_ref, gota_ref, gotb_ref, kept_ref, a_ref, b_ref):
    for half, (own, got, send) in enumerate(((owna_ref, gota_ref, a_ref), (ownb_ref, gotb_ref, b_ref))):
        kept_ref[2 * half : 2 * half + 2] = own[0] + got[0].astype(F32)
        send[...] = (own[1] + got[1].astype(F32)).astype(BF16)


def both_planes_kernel(at_ref, own_ref, gota_ref, gotb_ref, kept_ref, send_ref, sc):
    sc[0:2] = own_ref[0:2] + gota_ref[...].astype(F32)
    sc[2:4] = own_ref[2:4] + gotb_ref[...].astype(F32)
    for i, j in enumerate((0, 2, 1, 3)):
        value = sc[at_ref[AT_Z] ^ j]
        if i < 2:
            kept_ref[i] = value
        else:
            send_ref[i - 2] = value.astype(BF16)


class Plain:
    split = False

    def __init__(self, sizes, at):
        self.sizes, self.at = sizes, at
        self.order = at.at[AT_S].set(0)

    def first_layer(self, first, x):
        self.shares = first
        return x

    def next_layer(self, x, *wait):
        return x

    next_layer_two = next_layer

    def first(self, labels, pairs, *wait):
        x, rows = self.shares, D // (2 * self.sizes["z"])
        emb = lax.all_gather(x[0, :rows], ("z", "c"), axis=0, tiled=True)
        mods = lax.psum(x[1].astype(F32) + x[2].astype(F32), ("z", "c"))
        got = lax.ppermute(labels, CHIP, pairs)
        label = jnp.where(self.at[AT_OWN] == 1, labels, got)[self.at[AT_WHICH]]
        return emb, mods, self.at.at[AT_LABEL].set(label)

    def columns(self, stack, *wait):
        return (stack,)

    def placed(self, own, *wait):
        return lax.all_gather(own[0], ("z", "c"), axis=1, tiled=True)

    def total(self, x):
        return lax.psum(x, ("z", "c")), jnp.zeros_like(x)

    def core(self, g):
        own = lax.psum_scatter(g[0].astype(F32), ("z", "c"), scatter_dimension=1, tiled=True)
        return lax.psum(own, "s"), lax.psum(g[1][0].astype(F32), CHIP)

    def core_both(self, g, count):
        return self.core(g)

    def segment(self, x, flops=0):
        return x

    plane = both_one = both_planes = planes_one = planes_two = segment

    def shared(self, x, wait=()):
        return [x[0][j].astype(BF16) for j in range(4)]

    far_shared = shared


class Squares(Plain):
    split = True

    def __init__(self, sizes, at):
        self.sizes, self.at, self.order = sizes, at, at

    def across(self, x, axis):
        return [swap(x, axis, 4, by) for by in (1, 2, 3)]

    def doubled(self, x, axis):
        x = jnp.stack([x, swap(x, axis, 4, 1)])
        return jnp.concatenate([x, swap(x, axis, 4, 2)])

    def first_layer(self, first, x):
        pieces = [x] + self.across(x, "z")
        self.shares = jnp.stack([p[3:] for p in pieces])
        return jnp.stack([p[:3] for p in pieces])

    def next_layer(self, x, *wait):
        return jnp.stack([x[0], swap(after(x[0], *wait), "z", 4, 1)])

    def next_layer_two(self, x, *wait):
        return jnp.concatenate([x, swap(after(x, *wait), "z", 4, 2)])

    def first(self, labels, pairs, *wait):
        own = after(self.shares, *wait)
        return call(
            first_kernel,
            "first",
            [((D, ECOLS), BF16), ((48, D), F32), ((AT_LABEL + 1,), jnp.int32)],
            [self.at, own, *self.pieces(own, 2)[0]],
            cost(0, 1e4),
            out_spaces=[VMEM, VMEM, SMEM],
        )

    def columns(self, stack, *wait):
        return [stack] + self.across(after(stack, *wait), "s")

    def placed(self, own, *wait):
        got = [swap(after(x, *wait) if i else x, "c", 2, 1) for i, x in enumerate(own)]
        return placed(self.at, own, got)

    def total(self, x):
        one, two, three = self.across(x, "z")
        x = (x + one) + (two + three)
        return x, swap(x, "c", 2, 1)

    def run(self, kernel, name, outs, inputs, scratch=(), flops=0):
        return call(kernel, name, outs, [self.at, *inputs], cost(flops, 1e5), scratch)

    def pieces(self, x, parts):
        cuts = [x.shape[0] * i // parts for i in range(parts + 1)]
        return [swap(x[a:b], "c", 2, 1) for a, b in zip(cuts[:-1], cuts[1:])], cuts

    def core(self, g):
        kept, sent = g
        count, rows, width = kept.shape
        full = (4 + count % 4, rows, width)
        got, cuts = self.pieces(sent, 2)
        outs = [(full, F32)] + [(full, BF16)] * 3
        return self.run(
            lambda at, kept, *refs: add_core_kernel(at, kept, Rows(refs[:2], cuts), *refs[2:]),
            "add_core", outs, [kept, *got], [pltpu.VMEM(kept.shape, BF16)],
        )

    def planes_one(self, x):
        own, send = x
        one = own.shape[1:]
        outs = [(one, F32), (one, BF16)]
        return self.run(add_half_kernel, "add_half", outs, [own, swap(send, "z", 4, 1)])

    def planes_two(self, x):
        own, send = x
        outs = [(own.shape, BF16)]
        return self.run(add_both_kernel, "add_both", outs, [own, swap(send, "z", 4, 2)])

    def core_both(self, g, count):
        kept, sent = g
        rows, width = kept.shape[1:]
        part = (2, 2, rows, width)
        got, cuts = self.pieces(sent, count)
        n = 2 + len(got)
        return self.run(
            lambda *refs: both_split_kernel(*refs[:2], Rows(refs[2:n], cuts), *refs[n:]),
            "both_split", [(part, F32)] * 2 + [(part, BF16)] * 2,
            [kept, *got], [pltpu.VMEM(kept.shape, BF16)],
        )

    def both_one(self, x, flops=0):
        own_a, own_b, a, b = x
        part = own_a.shape[1:]
        return self.run(
            both_half_kernel, "both_half", [((4,) + part[1:], F32)] + [(part, BF16)] * 2,
            [own_a, own_b, swap(a, "s", 4, 1), swap(b, "s", 4, 2)], flops=flops,
        )

    def both_planes(self, x):
        own, a, b = x
        part = (2,) + own.shape[1:]
        return self.run(
            both_planes_kernel, "both_planes", [(part, F32), (part, BF16)],
            [own, swap(a, "s", 4, 2), swap(b, "s", 4, 1)], [pltpu.VMEM(own.shape, F32)],
        )

    def segment(self, x):
        own, *sends = x
        count, rows, width = own.shape
        one = (count - 3, rows, width)
        got = [swap(y, "s", 4, j + 1) for j, y in enumerate(sends)]
        return call(
            add_segment_kernel, "add_segment", [(one, F32)] + [(one, BF16)] * 3,
            [self.at, own, *got], cost(0, 1e5),
        )

    def plane(self, x):
        own, *sends = x
        count, rows, width = own.shape
        got = [swap(y, "z", 4, j + 1) for j, y in enumerate(sends)]
        return call(
            add_plane_kernel, "add_plane",
            [((rows, width), BF16)] + [((rows, width), F32)] * (count - 1),
            [self.at, own, *got], cost(0, 1e5),
        )

    def shared(self, x, wait=()):
        return [x[0]] + self.across(after(x[0], *wait), "s")

    def far_shared(self, x, wait=()):
        pieces = self.doubled(after(x[0], *wait), "s")
        return [pieces[j] for j in range(4)]


def lead_parts(emb_ref):
    lead = emb_ref[:, LEAD:EROWS].astype(BF16).astype(F32)
    gate = jax.nn.sigmoid(lead)
    return lead * gate, gate * (1.0 + lead * (1.0 - gate))


def ada_gradient(silu, sums_ref, layer, index):
    total = 0.0
    for group in range(GROUPS):
        at = 8 * (GROUPS * layer + group) + index
        total = total + silu[:, group : group + 1] * sums_ref[at : at + 1, :D]
    return total


def square_sum(v):
    return jnp.sum(v * v, axis=(0, 1), keepdims=True)


def gather_kernel(at_ref, *refs, widths):
    pieces, (emb_ref, ada_ref, sums_ref), outs = refs[:12], refs[12:15], refs[15:]
    ordered, (lead_ref, square_ref) = outs[:3], outs[3:]
    total = jnp.zeros((1, 1), F32)
    for k, ref in enumerate(ordered):
        squares = []
        for j in range(4):
            piece = pieces[4 * k + j][...]
            ref[at_ref[AT_S] ^ j] = piece
            squares.append(square_sum(piece.astype(F32)))
        total = total + ((squares[0] + squares[1]) + (squares[2] + squares[3]))
    silu, slope = lead_parts(emb_ref)
    rows = silu.shape[0]
    lane = lax.broadcasted_iota(jnp.int32, (rows, 128), 1)
    lead = jnp.zeros((rows, 128), F32)
    for group in range(GROUPS):
        d_silu = jnp.zeros((rows, 1), F32)
        for layer in range(LAYERS):
            for i in range(6):
                at = 8 * (GROUPS * layer + group) + i
                ada = ada_ref[layer, :, D * i : D * (i + 1)].astype(BF16).astype(F32)
                d_silu = d_silu + jnp.sum(ada * sums_ref[at : at + 1, :D], axis=-1, keepdims=True)
        value = d_silu * slope[:, group : group + 1]
        total = total + square_sum(value)
        lead = jnp.where(lane == group, value, lead)
    for layer in range(LAYERS):
        for i in range(6):
            total = total + square_sum(ada_gradient(silu, sums_ref, layer, i))
    lead_ref[...] = lead
    square_ref[...] = jnp.broadcast_to(total, square_ref.shape)


def gathered(at, pieces, emb_t, ada, sums):
    widths = [group[0].shape for group in pieces]
    return call(
        lambda *refs: gather_kernel(*refs, widths=widths),
        "gathered",
        [((4,) + shape, BF16) for shape in widths]
        + [((widths[0][0], 128), F32), ((8, 128), F32)],
        [at, *pieces[0], *pieces[1], *pieces[2], emb_t, ada, sums],
        cost(0, 4e6),
    )


def update_kernel(at_ref, *refs, rate):
    g1_ref, g2_ref, g3_ref, lead_ref, sums_ref, own_ref, got_ref = refs[:7]
    state = refs[7:28]
    outs, (loss_ref, norm_ref) = refs[28:49], refs[49:51]
    results, sems = refs[51:72], refs[72]
    squares = own_ref[0:1, 0:1] + got_ref[0:1, 0:1]
    norm = jnp.sqrt(squares)
    factor = CLIP / jnp.maximum(norm, CLIP)
    norm_ref[...] = norm
    loss_ref[...] = sums_ref[6:7, 0:1] + sums_ref[7:8, 0:1]
    silu, _ = lead_parts(state[0])
    rows = silu.shape[0]

    def advance(index, at, g):
        w_ref, m_ref, a_ref = (state[index + 7 * k] for k in range(3))
        g = g.astype(F32) * factor
        m = KEEP * m_ref[at] + g
        w = w_ref[at] - rate * (BOOST if index == 0 else 1.0) * (g + KEEP * m)
        results[index + 7][at] = m
        results[index][at] = w
        results[index + 14][at] = KEEP * a_ref[at] + (1.0 - KEEP) * w

    copies = []

    def send(index, layer=None):
        for k in range(3):
            i = index + 7 * k
            source, target = results[i], outs[i]
            if layer is not None:
                source, target = source.at[layer], target.at[layer]
            copy = pltpu.make_async_copy(source, target, sems.at[i, layer or 0])
            copy.start()
            copies.append(copy)

    every = slice(None)
    for layer in range(LAYERS):
        for i in range(6):
            g = ada_gradient(silu, sums_ref, layer, i)
            advance(5, (layer, every, slice(D * i, D * (i + 1))), g)
        send(5, layer)
    qkv = (g3_ref, g2_ref)
    ff = ((g2_ref, D), (g1_ref, 0))
    for layer in range(LAYERS):
        ref, lane = ff[layer]
        for j in range(2):
            part = slice(HALF * j, HALF * (j + 1))
            advance(3, (layer, every, part), ref[j, :, lane : lane + HALF])
            advance(4, (layer, every, part), ref[2 + j, :, lane : lane + HALF])
        send(3, layer)
        send(4, layer)
    for layer in range(LAYERS):
        for j in range(3):
            advance(1, (layer, every, slice(D * j, D * (j + 1))), qkv[layer][j, :, :D])
        send(1, layer)
    for j in range(3):
        advance(2, (0, every, slice(128 * j, 128 * (j + 1))), g2_ref[j, :, D + HALF : D + HALF + 128])
    advance(2, (1,), g2_ref[3, :, :D])
    send(2)
    col = lax.broadcasted_iota(jnp.int32, (512, PIXELS), 1)
    row = lax.broadcasted_iota(jnp.int32, (512, PIXELS), 0)
    back = jnp.logical_and(row // 256 == col % 2, row % 256 == col // 2).astype(BF16)
    g_head = jnp.concatenate([g1_ref[j, :, HALF : HALF + 128] for j in range(4)], axis=-1)
    advance(6, (every,), dot(g_head, back))
    send(6)
    lane = lax.broadcasted_iota(jnp.int32, (rows, 128), 1)
    for j in range(3):
        g = g3_ref[3, :, 128 * j : 128 * j + 128].astype(F32)
        width = min(128, EROWS - 128 * j)
        if LEAD < 128 * j + width:
            first = LEAD - 128 * j
            for group in range(GROUPS):
                g = jnp.where(lane == first + group, lead_ref[:, group : group + 1], g)
        advance(0, (every, slice(128 * j, 128 * j + width)), g[:, :width])
    send(0)
    for copy in copies:
        copy.wait()


def updated(at, g, lead, sums, own, got, state, rate):
    shapes = [(x.shape, F32) for x in state]
    scalar = [((1, 1), F32)] * 2
    inputs = [at, *g, lead, sums, own, got, *state]
    return call(
        lambda *refs: update_kernel(*refs, rate=rate),
        "updated",
        shapes + scalar,
        inputs,
        cost(0, 2e7),
        [pltpu.VMEM(shape, kind) for shape, kind in shapes] + [pltpu.SemaphoreType.DMA((21, 2))],
        limit=24,
        out_spaces=[HBM] * 21 + [VMEM] * 2,
    )


def per_device(sizes, *arrays):
    (tiles_in, truth_in, labels, var_ids, basis) = arrays[:5]
    masters = arrays[5:12]
    segments, dp = sizes["s"], sizes["z"] * 2
    micro = tiles_in.shape[0]
    assert segments == 2 * micro
    rows = D // dp
    s, z, c = (lax.axis_index(name) for name in CHIP)
    which, owner = s % micro, s // micro
    at = jnp.stack([s, z, c, c == owner, which, 0]).astype(jnp.int32)
    fast = segments == 4 and sizes["z"] == 4
    move = (Squares if fast else Plain)(sizes, at)
    cut = Cut(sizes["z"], rows, move.split)
    views = []
    for k in range(3):
        w = list(arrays[5 + 7 * k : 12 + 7 * k])
        w[0], w[4] = w[0].T, w[4].transpose(0, 2, 1)
        views += w

    pairs = []
    for a in range(segments):
        for b in range(sizes["z"]):
            base = (a * sizes["z"] + b) * 2
            pairs.append((base + a // micro, base + 1 - a // micro))
    pick = lambda x: lax.dynamic_index_in_dim(x, which, 0, keepdims=False).T

    first, *bundles = packed(at, labels, views[:7], fast)
    stack0 = move.first_layer(first, bundles[0])
    tiles = pick(tiles_in)
    tiles_got = lax.ppermute(tiles, CHIP, pairs)
    columns0 = move.columns(stack0)
    stack1 = move.next_layer(bundles[1])
    emb, mods, at = move.first(labels, pairs, tiles_got, stack1)
    stack1 = move.next_layer_two(stack1, emb)
    vid4 = jnp.pad(jnp.repeat(var_ids, 4), (0, D - PIXELS), constant_values=-1)[None].astype(
        jnp.int32
    )
    h0, agg, x_all, embk = embed(at, tiles, tiles_got, emb, vid4)
    truth = pick(after(truth_in, h0, *columns0[1:]))
    half = truth.shape[1] // 2
    lanes = lambda core: jnp.where(core == 0, truth[:, :half], truth[:, half:])
    truth_got = lax.ppermute(lanes(1 - c), CHIP, pairs)
    truth = lanes(c)
    w0 = move.placed(columns0, h0, stack1)
    columns1 = move.columns(stack1, h0, *columns0[1:])
    h1, q0, own0, other0, att0, lse0, *kept = block_forward(after(at, truth_got), h0, mods, w0)
    w1 = move.placed(columns1, h1)
    q1, own1 = qkv_rows(at, h1, mods, w1)
    other1 = swap(own1, "c", 2, 1)
    d_mid, d_att, att1, lse1, g_out, dmod1, loss, *g_first = turn(
        at, cut, h1, q1, own1, other1, mods, w1, truth, truth_got, basis, 1.0 / (micro * dp)
    )
    d_q, d_k, d_v, *sent = attention_back(at, q1, own1, other1, lse1, att1, d_att, finish=True)
    got = [swap(x, "c", 2, 1) for x in sent]
    first = move.core_both(g_first, 1)
    d_mid, d_att, dmod1, dmod0, *g_second = between(
        after(at, *first), cut, [d_q, d_k, d_v, *got], h1, d_mid, g_out, dmod1, mods, w1, [att0, *kept], w0
    )
    first = move.both_one(first, 1e10)
    second = move.core_both([after(g_second[0], *first), g_second[1]], 3)
    d_q, d_k, d_v = attention_back(after(at, *first, *second), q0, own0, other0, lse0, att0, d_att)
    first = move.both_planes([after(first[0], d_q), *first[1:]])
    g_third = last(
        after(at, *first), cut, [d_q, d_k, d_v], h0, d_mid, dmod0, dmod1, loss, mods, w0, x_all, agg, embk, vid4
    )
    first = move.planes_one(first)
    second = move.both_one(second)
    third = move.core([after(g_third[0], *first), after(g_third[1], *first, *second)])
    first = move.planes_two([after(first[0], *third), first[1]])
    second = move.planes_one(move.both_planes(second))
    third = move.segment([after(third[0], *first, *second), *third[1:]])
    second = move.planes_two(second)
    ends = [move.far_shared(first), move.shared(second)]
    third = move.plane(third)
    ends.append(move.shared(third))
    sums = third[1]

    g1, g2, g3, lead_g, squares = gathered(move.order, ends, views[0], views[5], sums)
    own, got = move.total(squares)
    count = sum(w.size for w in masters) * dp
    rate = 0.02 * math.sqrt(count) / CLIP
    *new, loss_value, norm = updated(at, (g1, g2, g3), lead_g, sums, own, got, views, rate)
    for k in range(3):
        new[7 * k] = new[7 * k].T
        new[7 * k + 4] = new[7 * k + 4].transpose(0, 2, 1)
    return (loss_value.reshape(()), norm.reshape(()), *new)


def solution(mesh):
    segments, dp = mesh.shape["segment"], mesh.shape["dp"]
    sizes = {"s": segments, "z": dp // 2, "c": 2}
    split = Mesh(mesh.devices.reshape(segments, dp // 2, 2), CHIP)
    d = ("z", "c")
    weights = (
        P(None, d),
        P(None, d, None),
        P(None, d, None),
        P(None, d, None),
        P(None, None, d),
        P(None, d, None),
        P(d, None),
    )
    return jax.shard_map(
        lambda *arrays: per_device(sizes, *arrays),
        mesh=split,
        in_specs=(P(d, None, None), P(d, None, None), P(d), P(), P()) + weights * 3,
        out_specs=(P(), P()) + weights * 3,
        check_vma=False,
    )
```

```python
import math

import jax
import jax.numpy as jnp
from jax import lax
from jax.experimental import pallas as pl
from jax.experimental.pallas import tpu as pltpu
from jax.sharding import Mesh, PartitionSpec as P

D = 384
HEADS = 6
HEAD_DIM = 64
FF = 1536
VARS = 69
CHANNELS = 69
LONP = 128
LATP = 8
LAYERS = 2
GROUPS = 3
PIXELS = 276
LEAD = PIXELS + VARS + 1
EROWS = LEAD + GROUPS
ECOLS = 384
EPS = 1e-06
CLIP = 0.001
KEEP = 0.9
BOOST = 20.0
LABEL_LANE = D - 1
HALF = FF // 2

F32 = jnp.float32
BF16 = jnp.bfloat16
CHIP = ("s", "z", "c")


def dot(a, b):
    return jnp.dot(a, b, preferred_element_type=F32)


def dot_nt(a, b):
    return lax.dot_general(a, b, (((1,), (1,)), ((), ())), preferred_element_type=F32)


def dot_tn(a, b):
    return lax.dot_general(a, b, (((0,), (0,)), ((), ())), preferred_element_type=F32)


def parts(x, count):
    out = []
    for step in range(count):
        piece = x.astype(BF16)
        out.append(piece)
        if step < count - 1:
            x = x - piece.astype(F32)
    return out


def normal(v):
    centered = v - jnp.mean(v, axis=-1, keepdims=True)
    inverse = lax.rsqrt(jnp.mean(centered * centered, axis=-1, keepdims=True) + EPS)
    return centered * inverse, inverse


def normal_back(d_x, x, inverse):
    return inverse * (
        d_x - jnp.mean(d_x, axis=-1, keepdims=True) - x * jnp.mean(d_x * x, axis=-1, keepdims=True)
    )


def lane_below(limit, shape):
    return lax.broadcasted_iota(jnp.int32, shape, len(shape) - 1) < limit


def sublane(shape):
    return lax.broadcasted_iota(jnp.int32, shape, 0)


def same_group():
    col = lax.broadcasted_iota(jnp.int32, (D, D), 1)
    return (sublane((D, D)) // 4 == col // 4).astype(BF16)


def chosen_table(vid_ref):
    return (sublane((ECOLS, D)) - PIXELS == vid_ref[...]).astype(BF16)


def first_of_four(shape):
    return sublane(shape) % 4 == 0


def cost(flops, size, exps=0):
    return pl.CostEstimate(flops=int(flops), bytes_accessed=int(size), transcendentals=int(exps))


VMEM = pl.BlockSpec(memory_space=pltpu.VMEM)
SMEM = pl.BlockSpec(memory_space=pltpu.SMEM)
HBM = pl.BlockSpec(memory_space=pltpu.HBM)
CHUNK = 512
SPAN = 512
AT_S, AT_Z, AT_C, AT_OWN, AT_WHICH, AT_LABEL = range(6)


def call(kernel, name, outs, inputs, estimate, scratch=(), limit=24, in_space=VMEM, out_spaces=None):
    return pl.pallas_call(
        kernel,
        in_specs=[SMEM] + [in_space] * (len(inputs) - 1),
        out_specs=out_spaces or [VMEM] * len(outs),
        out_shape=[jax.ShapeDtypeStruct(shape, kind) for shape, kind in outs],
        scratch_shapes=list(scratch),
        compiler_params=pltpu.CompilerParams(vmem_limit_bytes=limit << 20),
        cost_estimate=estimate,
        name=name,
    )(*inputs)


def rows_at(index, size):
    return pl.ds(pl.multiple_of(index * size, size), size)


def after(x, *others):
    return lax.optimization_barrier((x, others))[0]


def column_sum(v):
    return jnp.sum(v, axis=0, keepdims=True)


class Cut:
    def __init__(self, pairs, rows, split):
        self.pairs, self.rows, self.split = pairs, rows, split

    def shapes(self, width, extra=False):
        if self.split:
            return [((4 * self.pairs + extra, self.rows, width), BF16)] * 2
        return [((4, D, width), BF16), ((1, 48, width), BF16)]

    def write(self, at_ref, outs, quarter, lane, value):
        value = value.astype(BF16)
        cols = slice(lane, lane + value.shape[-1])
        if not self.split:
            outs[0][quarter, :, cols] = value
            return
        first = at_ref[AT_C] == 0
        for z in range(self.pairs):
            row = 2 * z * self.rows
            one, two = value[row : row + self.rows], value[row + self.rows : row + 2 * self.rows]
            outs[0][quarter * self.pairs + z, :, cols] = jnp.where(first, one, two)
            outs[1][quarter * self.pairs + z, :, cols] = jnp.where(first, two, one)

    def write_extra(self, outs, value):
        value = value.astype(BF16)
        if self.split:
            outs[0][4 * self.pairs] = value
            outs[1][4 * self.pairs] = value
        else:
            outs[1][0] = value


def embed_kernel(
    at_ref, own_ref, got_ref, emb_ref, vid_ref,
    out_ref, agg_ref, x_ref, embk_ref, x_sc, bases_sc,
):
    tokens = own_ref.shape[1]
    half = tokens // 2
    emb = emb_ref[...]
    embk_ref[...] = emb.astype(F32).T.astype(BF16)
    query = jnp.broadcast_to(emb[:, LEAD - 1 : LEAD].astype(F32), (D, 128)).astype(BF16)
    by_row = dot_tn(emb, query)
    table = chosen_table(vid_ref)
    inside = sublane((D, 1)) < PIXELS
    proj = jnp.where(inside, by_row[:D, :1], 0.0)
    base = sum(dot_tn(table, p) for p in parts(by_row, 3))[:, :1]
    lane = lax.broadcasted_iota(jnp.int32, (D, D), 1)
    bases_sc[...] = jnp.where(lane % 4 == 0, dot(emb, table), 0.0).astype(BF16)
    group = same_group()
    x_sc[...] = jnp.zeros_like(x_sc)
    x_sc[:PIXELS] = jnp.where(at_ref[AT_OWN] == 1, own_ref[...], got_ref[...])

    def step(i, carry):
        here = rows_at(i, CHUNK)
        source = lax.rem(i * CHUNK + at_ref[AT_C] * half, tokens)
        packed = x_sc[:, pl.ds(pl.multiple_of(source, CHUNK), CHUNK)]
        x = packed.astype(F32)
        scores = sum(dot(group, p) for p in parts(x * proj, 3)) + base
        scores = jnp.where(inside, scores * D ** (-0.5), -1e30)
        e = jnp.exp(scores - jnp.max(scores, axis=0, keepdims=True))
        agg = e * (4.0 / column_sum(e))

        agg_ref[:, here] = agg
        x_ref[:, here] = packed
        total = dot(emb_ref[:, :D], (agg * x).astype(BF16))
        for p in parts(agg, 2):
            total = total + dot(bases_sc[...], p)
        out_ref[here, :] = total.T.astype(BF16)
        return carry

    lax.fori_loop(0, tokens // CHUNK, step, 0)


def embed(at, own, got, emb, vid4):
    tokens = own.shape[1]
    return call(
        embed_kernel,
        "embed",
        [
            ((tokens, D), BF16),
            ((D, tokens), F32),
            ((D, tokens), BF16),
            ((ECOLS, D), BF16),
        ],
        [at, own, got, emb, vid4],
        cost(1e6, 1e4),
        [pltpu.VMEM((D, tokens), BF16), pltpu.VMEM((D, D), BF16)],
    )


def embed_back(dh, x_ref, agg_ref, embk_ref, vid_ref):
    x = x_ref[...].astype(F32)
    agg = agg_ref[...]
    embk = embk_ref[...]
    table = chosen_table(vid_ref)
    bases = dot_tn(table, embk_ref[...]).astype(BF16)
    query = embk_ref[LEAD - 1 : LEAD, :].astype(F32)
    g_patch = dot((agg * x).astype(BF16), dh)
    d_agg = dot_nt(bases, dh)
    group = same_group()
    for p in parts(dot_nt(embk, dh) * x, 2):
        d_agg = d_agg + dot(group, p)
    inner = 0.25 * column_sum(agg * d_agg)
    d_scores = agg * (d_agg - inner) * D ** (-0.5)
    d_proj = jnp.sum(d_scores * x, axis=-1, keepdims=True)
    d_base = jnp.sum(d_scores, axis=-1, keepdims=True)
    d_base = jnp.where(first_of_four(d_base.shape), d_base, 0.0)
    d_bases = d_base * query
    for p in parts(jnp.where(first_of_four((D, 1)), agg, 0.0), 2):
        d_bases = d_bases + dot(p, dh)
    g_table = sum(dot(table, p) for p in parts(d_bases, 2))
    d_query = column_sum(embk.astype(F32) * d_proj) + column_sum(bases.astype(F32) * d_base)
    total = g_table + jnp.where(sublane((ECOLS, 1)) == LEAD - 1, d_query, 0.0)
    return total + g_patch + d_proj * query


def project(normed, w_ref, first, last):
    w = jnp.concatenate([w_ref[j, :, :D] for j in range(first, last)], axis=-1)
    return dot(normed, w).astype(BF16)


def mod_row(mods_ref, at_ref, layer, index):
    row = 8 * (layer * GROUPS + at_ref[AT_LABEL]) + index
    return mods_ref[pl.ds(row, 1), :D]


def first_norm(h, mods_ref, at_ref, layer):
    x, inverse = normal(h.astype(F32))
    scale = 1.0 + mod_row(mods_ref, at_ref, layer, 1)
    return (x * scale + mod_row(mods_ref, at_ref, layer, 0)).astype(BF16), x, inverse


def pair_masks():
    low = lane_below(HEAD_DIM, (1, 128))
    return low, jnp.logical_not(low)


def both(own_ref, other_ref, lane):
    here = slice(lane, lane + 128)
    return jnp.concatenate([own_ref[:, here], other_ref[:, here]])


def attend(here, q_ref, own_ref, other_ref, att_ref, lse_ref):
    zero = jnp.zeros((), BF16)
    rows = q_ref[here, :].shape[0]
    lane = lax.broadcasted_iota(jnp.int32, (rows, 128), 1)
    sums = jnp.zeros((rows, 128), F32)
    for pair in range(HEADS // 2):
        a = 128 * pair
        q = q_ref[here, a : a + 128] * 0.125
        keys = both(own_ref, other_ref, a)
        vals = both(own_ref, other_ref, D + a)
        mixed = jnp.zeros((rows, 128), F32)
        for which, mask in enumerate(pair_masks()):
            scores = dot_nt(q, jnp.where(mask, keys, zero))
            top = jnp.max(scores, axis=-1, keepdims=True)
            e = jnp.exp(scores - top)
            total = jnp.sum(e, axis=-1, keepdims=True)
            mixed = mixed + dot(e.astype(BF16), jnp.where(mask, vals, zero)) * (1.0 / total)
            sums = jnp.where(lane == 2 * pair + which, top + jnp.log(total), sums)
        att_ref[here, a : a + 128] = mixed.astype(BF16)
    lse_ref[here, :] = sums


def gelu_and_slope(u):
    k = math.sqrt(2.0 / math.pi)
    t = jnp.tanh(k * (u + 0.044715 * (u * u * u)))
    cdf = 0.5 * (1.0 + t)
    return u * cdf, cdf + 0.5 * u * (1.0 - t * t) * k * (1.0 + 3 * 0.044715 * (u * u))


def feed_forward(
    here, h, one, mods_ref, at_ref, layer, w_ref, act_ref, slope_ref, n2_ref=None, stored=lambda j: None
):
    middle = h.astype(F32) + mod_row(mods_ref, at_ref, layer, 2) * one
    x, _ = normal(middle)
    scale = 1.0 + mod_row(mods_ref, at_ref, layer, 4)
    n2 = (x * scale + mod_row(mods_ref, at_ref, layer, 3)).astype(BF16)
    if n2_ref is not None:
        n2_ref[here, :] = n2
    two = jnp.zeros(middle.shape, F32)
    for j in range(2):
        part = slice(HALF * j, HALF * (j + 1))
        act, slope = gelu_and_slope(dot(n2, w_ref[j, :, D : 3 * D]))
        slope_ref[here, part] = slope.astype(slope_ref.dtype)
        act = act.astype(BF16)
        act_ref[here, part] = act
        stored(j)
        two = two + dot_nt(act, w_ref[2 + j, :, D : 3 * D])
    return middle, two, middle + mod_row(mods_ref, at_ref, layer, 5) * two


def feed_back(
    here, d_out, one, two, middle, slope_ref, mods_ref, at_ref, layer, w_ref,
    dunits_ref, dtwo_ref, done_ref, dmid_ref, datt_ref, dmod_ref, n2_ref=None,
):
    d_out = d_out.astype(F32)
    d_two = (mod_row(mods_ref, at_ref, layer, 5) * d_out).astype(BF16)
    dtwo_ref[here, :] = d_two
    d_n2 = jnp.zeros(d_out.shape, F32)
    for j in range(2):
        part = slice(HALF * j, HALF * (j + 1))
        slope = slope_ref[here, part].astype(F32)
        d_units = (slope * dot(d_two, w_ref[2 + j, :, D : 3 * D])).astype(BF16)
        dunits_ref[here, part] = d_units
        d_n2 = d_n2 + dot_nt(d_units, w_ref[j, :, D : 3 * D])
    x, inverse = normal(middle)
    scale = 1.0 + mod_row(mods_ref, at_ref, layer, 4)
    if n2_ref is not None:
        n2_ref[here, :] = (x * scale + mod_row(mods_ref, at_ref, layer, 3)).astype(BF16)
    d_mid = d_out + normal_back(d_n2 * scale, x, inverse)
    dmid_ref[here, :] = d_mid
    d_one = (mod_row(mods_ref, at_ref, layer, 2) * d_mid).astype(BF16)
    done_ref[here, :] = d_one
    datt_ref[here, :] = dot_nt(d_one, w_ref[3, :, :D]).astype(BF16)
    dmod_ref[2:3] += column_sum(d_mid * one)
    dmod_ref[3:4] += column_sum(d_n2)
    dmod_ref[4:5] += column_sum(d_n2 * x)
    dmod_ref[5:6] += column_sum(d_out * two)


def feed_gradients(at_ref, cut, outs, lane, n2_ref, dunits_ref, dtwo_ref, act_ref):
    for j in range(2):
        part = slice(HALF * j, HALF * (j + 1))
        cut.write(at_ref, outs, j, lane, dot_tn(n2_ref[...], dunits_ref[:, part]))
        cut.write(at_ref, outs, 2 + j, lane, dot_tn(dtwo_ref[...], act_ref[:, part]))


def rows_scratch(count, widths):
    return [pltpu.VMEM((count, width), BF16) for width in widths]


def block_kernel(
    at_ref, h_ref, mods_ref, w_ref,
    out_ref, q_out, own_out, other_out, att_out, lse_out, one_out, mid_out, slope_out, act_out, two_out,
    q_ref, own_ref, other_ref, att_ref, lse_ref, one_ref, mid_ref, slope_ref, act_ref, two_ref, sems,
):
    count = out_ref.shape[0]

    normed, _, _ = first_norm(h_ref[:count], mods_ref, at_ref, 0)
    qkv = project(normed, w_ref, 0, 3)
    q_ref[...] = qkv[:, :D]
    own_ref[...] = qkv[:, D:]
    normed, _, _ = first_norm(h_ref[count:], mods_ref, at_ref, 0)
    other_ref[...] = project(normed, w_ref, 1, 3)
    early = [
        pltpu.make_async_copy(ref, out, sems.at[2, i])
        for i, (ref, out) in enumerate(((q_ref, q_out), (own_ref, own_out), (other_ref, other_out)))
    ]
    for copy in early:
        copy.start()
    kept = (
        (att_ref, att_out), (lse_ref, lse_out), (one_ref, one_out), (mid_ref, mid_out),
        (slope_ref, slope_out), (act_ref, act_out), (two_ref, two_out),
    )

    slope, act = kept[4:6]
    whole = [
        pltpu.make_async_copy(ref, out, sems.at[0, k])
        for k, (ref, out) in enumerate(kept[:4] + kept[6:])
    ]
    halves = [
        [
            pltpu.make_async_copy(ref.at[:, part], out.at[:, part], sems.at[1, 2 * j + k])
            for k, (ref, out) in enumerate((slope, act))
        ]
        for j, part in enumerate((pl.ds(0, HALF), pl.ds(HALF, HALF)))
    ]

    def start(*copies):
        for copy in copies:
            copy.start()

    here = slice(0, count)
    attend(here, q_ref, own_ref, other_ref, att_ref, lse_ref)
    one = dot(att_ref[...], w_ref[3, :, :D])
    one_ref[...] = one.astype(BF16)
    start(*whole[:3])
    middle, two, out = feed_forward(
        here, h_ref[:count], one, mods_ref, at_ref, 0, w_ref, act_ref, slope_ref,
        stored=lambda j: start(*halves[j]),
    )
    mid_ref[...] = middle
    start(whole[3])
    two_ref[...] = two.astype(BF16)
    start(whole[4])
    out_ref[...] = out.astype(BF16)
    for copy in early + whole + halves[0] + halves[1]:
        copy.wait()


def block_forward(at, h, mods, weights):
    count = h.shape[0] // 2
    kept = [(D, BF16), (2 * D, BF16), (2 * D, BF16), (D, BF16), (128, F32), (D, BF16), (D, F32)]
    kept += [(FF, BF16), (FF, BF16), (D, BF16)]
    kept = [((count, width), kind) for width, kind in kept]
    return call(
        block_kernel,
        "block_forward",
        [((count, D), BF16)] + kept,
        [at, h, mods, weights],
        cost(1e6, 1e4),
        [pltpu.VMEM(shape, kind) for shape, kind in kept] + [pltpu.SemaphoreType.DMA((3, 7))],
        limit=28,
        out_spaces=[VMEM] + [HBM] * len(kept),
    )


def qkv_kernel(at_ref, h_ref, mods_ref, w_ref, q_ref, kv_ref):
    normed, _, _ = first_norm(h_ref[...], mods_ref, at_ref, 1)
    qkv = project(normed, w_ref, 0, 3)
    q_ref[...] = qkv[:, :D]
    kv_ref[...] = qkv[:, D:]


def qkv_rows(at, h, mods, weights):
    count = h.shape[0]
    return call(
        qkv_kernel,
        "qkv_rows",
        [((count, D), BF16), ((count, 2 * D), BF16)],
        [at, h, mods, weights],
        cost(1e9, 3e6),
    )


def turn_kernel(
    at_ref, h_ref, q_ref, own_ref, other_ref, mods_ref, w_ref, truth_ref, got_ref, basis_ref,
    dmid_ref, datt_ref, att_ref, lse_ref, gout_ref, dmod_ref, loss_ref, keep_ref, send_ref,
    act_ref, dunits_ref, dtwo_ref, n2_ref, done_ref, flat_ref, dpred_ref, true_ref, slope_ref,
    basis_sc, *, seed, cut,
):
    count = h_ref.shape[0]
    outs = (keep_ref, send_ref)
    entries = LATP * CHANNELS * 2 * LONP
    dmod_ref[...] = jnp.zeros_like(dmod_ref)
    loss_ref[...] = jnp.zeros_like(loss_ref)
    row = lax.broadcasted_iota(jnp.int32, (PIXELS, 256), 0)
    col = lax.broadcasted_iota(jnp.int32, (PIXELS, 256), 1)
    truth = jnp.where(at_ref[AT_OWN] == 1, truth_ref[...], got_ref[...])
    for b in range(2):
        picked = dot_tn(truth, (row == 2 * col + b).astype(BF16))
        true_ref[:, 256 * b : 256 * b + 256] = picked.astype(BF16)
    to = lax.broadcasted_iota(jnp.int32, (256, 256), 0)
    source = lax.broadcasted_iota(jnp.int32, (256, 256), 1)
    order = (source == 2 * (to % LONP) + to // LONP).astype(BF16)
    for i, p in enumerate(parts(basis_ref[...], 2)):
        basis_sc[i] = dot(order, p).astype(BF16)

    for i in range(count // SPAN):
        attend(slice(i * SPAN, (i + 1) * SPAN), q_ref, own_ref, other_ref, att_ref, lse_ref)

    def step(i, carry):
        here = rows_at(i, CHUNK)
        one = dot(att_ref[here, :], w_ref[3, :, :D])
        middle, two, h2 = feed_forward(
            here, h_ref[here, :], one, mods_ref, at_ref, 1, w_ref, act_ref, slope_ref, n2_ref
        )
        x, inverse = normal(h2.astype(BF16).astype(F32))
        flat = x.astype(BF16)
        flat_ref[here, :] = flat
        hw = [w_ref[j, :, 3 * D : 3 * D + 128] for j in range(4)]
        pred = [dot(flat, w) for w in hw]
        pred = [jnp.concatenate(pred[:2], axis=-1), jnp.concatenate(pred[2:], axis=-1)]
        hi, lo = basis_sc[0], basis_sc[1]
        grads = [[], []]
        loss = jnp.zeros((1, 1), F32)
        for p in range(CHUNK // LONP):
            part = slice(p * LONP, (p + 1) * LONP)
            fine = rows_at(i * (CHUNK // LONP) + p, LONP)
            seen = parts(jnp.concatenate([pred[0][part], pred[1][part]], axis=0), 2)
            waves = dot_tn(hi, seen[0]) + (dot_tn(hi, seen[1]) + dot_tn(lo, seen[0]))
            want = jnp.concatenate([true_ref[fine, :256], true_ref[fine, 256:]], axis=0)
            target = dot_tn(hi, want) + dot_tn(lo, want)
            top, low = waves[:LONP], waves[LONP:]
            gap = (top * top + low * low) - (
                target[:LONP] * target[:LONP] + target[LONP:] * target[LONP:]
            )
            loss = loss + jnp.sum(gap * gap, axis=(0, 1), keepdims=True)
            scaled = gap * (4.0 * seed / entries)
            d_waves = parts(jnp.concatenate([scaled * top, scaled * low], axis=0), 2)
            d_seen = dot(hi, d_waves[0]) + (dot(hi, d_waves[1]) + dot(lo, d_waves[0]))
            d_seen = d_seen.astype(BF16)
            grads[0].append(d_seen[:LONP])
            grads[1].append(d_seen[LONP:])
        loss_ref[...] += jnp.broadcast_to(loss * (seed / entries), loss_ref.shape)
        d_flat = jnp.zeros((CHUNK, D), F32)
        for b in range(2):
            whole = jnp.concatenate(grads[b], axis=0)
            dpred_ref[here, 256 * b : 256 * b + 256] = whole
            for j in range(2):
                d_flat = d_flat + dot_nt(whole[:, 128 * j : 128 * j + 128], hw[2 * b + j])
        d_h2 = normal_back(d_flat, x, inverse).astype(BF16)
        feed_back(
            here, d_h2, one, two, middle, slope_ref, mods_ref, at_ref, 1, w_ref,
            dunits_ref, dtwo_ref, done_ref, dmid_ref, datt_ref, dmod_ref,
        )
        return carry

    lax.fori_loop(0, count // CHUNK, step, 0)
    feed_gradients(at_ref, cut, outs, 0, n2_ref, dunits_ref, dtwo_ref, act_ref)
    for j in range(4):
        cut.write(at_ref, outs, j, HALF, dot_tn(flat_ref[...], dpred_ref[:, 128 * j : 128 * j + 128]))
    gout_ref[...] = dot_tn(att_ref[...], done_ref[...])


def turn(at, cut, h, q, own, other, mods, weights, truth, got, basis, seed):
    count = h.shape[0]
    return call(
        lambda *refs: turn_kernel(*refs, seed=seed, cut=cut),
        "turn",
        [
            ((count, D), F32),
            ((count, D), BF16),
            ((count, D), BF16),
            ((count, 128), F32),
            ((D, D), F32),
            ((8, D), F32),
            ((8, 128), F32),
        ]
        + cut.shapes(HALF + 128),
        [at, h, q, own, other, mods, weights, truth, got, basis],
        cost(4e9, 4e6),
        rows_scratch(count, [FF, FF, D, D, D, D, 512, 512])
        + [pltpu.VMEM((count, FF), F32), pltpu.VMEM((2, 256, 256), BF16)],
        limit=32,
    )


def attention_back_kernel(
    at_ref, q_ref, own_ref, other_ref, lse_ref, att_ref, datt_ref, dq_ref, *outs, finish,
):
    zero = jnp.zeros((), BF16)
    count = own_ref.shape[0]
    dk_sc, dv_sc = outs[-2:] if finish else outs[:2]
    assert count == SPAN

    def step(i, carry):
        rows = rows_at(i, SPAN)
        for pair in range(HEADS // 2):
            a = 128 * pair
            here = slice(a, a + 128)
            q = q_ref[rows, here]
            d_att = datt_ref[rows, here]
            keys = both(own_ref, other_ref, a)
            vals = both(own_ref, other_ref, D + a)
            dots = d_att.astype(F32) * att_ref[rows, here].astype(F32)
            d_q = jnp.zeros((SPAN, 128), F32)
            d_k = jnp.zeros((keys.shape[0], 128), F32)
            d_v = jnp.zeros((keys.shape[0], 128), F32)
            for which, mask in enumerate(pair_masks()):
                head = 2 * pair + which
                k = jnp.where(mask, keys, zero)
                v = jnp.where(mask, vals, zero)
                inner = jnp.sum(jnp.where(mask, dots, 0.0), axis=-1, keepdims=True)
                probs = jnp.exp(dot_nt(q * 0.125, k) - lse_ref[rows, head : head + 1])
                d_scores = (probs * (dot_nt(d_att, v) - inner)).astype(BF16)
                d_q = d_q + dot(d_scores, k)
                d_k = d_k + dot_tn(d_scores, jnp.where(mask, q, zero))
                d_v = d_v + dot_tn(probs.astype(BF16), jnp.where(mask, d_att, zero))
            dq_ref[rows, here] = (d_q * 0.125).astype(BF16)
            dk_sc[:, here] = (d_k * 0.125).astype(dk_sc.dtype)
            dv_sc[:, here] = d_v.astype(dv_sc.dtype)
        return carry

    lax.fori_loop(0, count // SPAN, step, 0)
    if finish:
        dk_ref, dv_ref, dk_send, dv_send = outs[:4]
        dk_ref[...] = dk_sc[:count]
        dv_ref[...] = dv_sc[:count]
        dk_send[...] = dk_sc[count:].astype(BF16)
        dv_send[...] = dv_sc[count:].astype(BF16)


def attention_back(at, q, own, other, lse, att, d_att, finish=False):
    count = q.shape[0]
    full = ((2 * count, D), F32 if finish else BF16)
    outs = [((count, D), F32)] * 2 + [((count, D), BF16)] * 2 if finish else [full] * 2
    return call(
        lambda *refs: attention_back_kernel(*refs, finish=finish),
        "attention_back",
        [((count, D), BF16)] + outs,
        [at, q, own, other, lse, att, d_att],
        cost(5e9, 1e6),
        [pltpu.VMEM(*full)] * 2 if finish else (),
    )


def qkv_back(
    at_ref, cut, outs, lane, layer, d_q, d_k, d_v, h_ref, dmid_ref, gout_ref, mods_ref, w_ref,
):
    count, rows = d_q.shape[0], d_k.shape[0]
    normed, x, inverse = first_norm(h_ref[:rows], mods_ref, at_ref, layer)
    first = dot_nt(d_q, w_ref[0, :, :D])
    rest = dot_nt(d_k, w_ref[1, :, :D]) + dot_nt(d_v, w_ref[2, :, :D])
    if rows > count:
        d_n = jnp.concatenate([rest[:count] + first, rest[count:]], axis=0)
    else:
        d_n = rest + first
    cut.write(at_ref, outs, 0, lane, dot_tn(normed[:count], d_q))
    cut.write(at_ref, outs, 1, lane, dot_tn(normed, d_k))
    cut.write(at_ref, outs, 2, lane, dot_tn(normed, d_v))
    if gout_ref is not None:
        cut.write(at_ref, outs, 3, lane, gout_ref[...])
    scale = 1.0 + mod_row(mods_ref, at_ref, layer, 1)
    d_h = normal_back(d_n * scale, x, inverse)
    if rows > count:
        d_h = jnp.concatenate([d_h[:count] + dmid_ref[...], d_h[count:]], axis=0)
    else:
        d_h = d_h + dmid_ref[...]
    return d_h.astype(BF16), column_sum(d_n), column_sum(d_n * x)


def between_kernel(
    at_ref, dq_ref, dk_ref, dv_ref, dk_got, dv_got, h_ref, dmid_ref, gout_ref, dmod_ref, mods_ref, w1_ref,
    one_ref, two_ref, mid_ref, slope_ref, act_ref, att_ref, w0_ref,
    dmid_out, datt_out, dmod_out, dmod_next, keep_ref, send_ref,
    dh_sc, dunits_ref, dtwo_ref, n2_ref, done_ref, *, cut,
):
    outs = (keep_ref, send_ref)
    d_k = (dk_ref[...] + dk_got[...].astype(F32)).astype(BF16)
    d_v = (dv_ref[...] + dv_got[...].astype(F32)).astype(BF16)
    d_h, shift, scale = qkv_back(
        at_ref, cut, outs, 0, 1, dq_ref[...], d_k, d_v, h_ref, dmid_ref, gout_ref, mods_ref, w1_ref,
    )
    dmod_out[...] = dmod_ref[...]
    dmod_out[0:1] = shift
    dmod_out[1:2] = scale
    dh_sc[...] = d_h
    dmod_next[...] = jnp.zeros_like(dmod_next)

    def step(i, carry):
        here = rows_at(i, CHUNK)
        feed_back(
            here, dh_sc[here, :], one_ref[here, :].astype(F32), two_ref[here, :].astype(F32),
            mid_ref[here, :], slope_ref, mods_ref, at_ref, 0, w0_ref,
            dunits_ref, dtwo_ref, done_ref, dmid_out, datt_out, dmod_next, n2_ref,
        )
        return carry

    lax.fori_loop(0, dh_sc.shape[0] // CHUNK, step, 0)
    feed_gradients(at_ref, cut, outs, D, n2_ref, dunits_ref, dtwo_ref, act_ref)
    g_out = dot_tn(att_ref[...], done_ref[...])
    for j in range(4):
        tile = g_out[:, 128 * j : 128 * j + 128] if j < 3 else jnp.zeros((D, 128), F32)
        cut.write(at_ref, outs, j, D + HALF, tile)


def between(at, cut, grads, h, d_mid, g_out, dmod, mods, w1, kept, w0):
    att, one, mid, slope, act, two = kept
    count = d_mid.shape[0]
    return call(
        lambda *refs: between_kernel(*refs, cut=cut),
        "between",
        [((count, D), F32), ((count, D), BF16), ((8, D), F32), ((8, D), F32)]
        + cut.shapes(D + HALF + 128),
        [at, *grads, h, d_mid, g_out, dmod, mods, w1, one, two, mid, slope, act, att, w0],
        cost(1e9, 1e6),
        rows_scratch(count, [D, FF, D, D, D]),
        limit=28,
    )


def last_kernel(
    at_ref, dq_ref, dk_ref, dv_ref, h_ref, dmid_ref, dmod0_ref, dmod1_ref, loss_ref,
    mods_ref, w_ref, x_ref, agg_ref, embk_ref, vid_ref, keep_ref, send_ref, sums_sc, *, cut,
):
    outs = (keep_ref, send_ref)
    d_q = dq_ref[...]
    d_k, d_v = dk_ref[...], dv_ref[...]
    d_h, shift, scale = qkv_back(
        at_ref, cut, outs, 0, 0, d_q, d_k, d_v, h_ref, dmid_ref, None, mods_ref, w_ref,
    )
    sums_sc[...] = jnp.zeros_like(sums_sc)
    for group in range(GROUPS):
        hot = (at_ref[AT_LABEL] == group).astype(F32)
        for layer, ref in enumerate((dmod0_ref, dmod1_ref)):
            at = 8 * (GROUPS * layer + group)
            sums_sc[at : at + 8, :D] = ref[...] * hot
        sums_sc[8 * group : 8 * group + 1, :D] = shift * hot
        sums_sc[8 * group + 1 : 8 * group + 2, :D] = scale * hot
    loss = loss_ref[0:1, 0:1]
    top = loss.astype(BF16).astype(F32)
    sums_sc[6:7, :] = jnp.broadcast_to(top, (1, ECOLS))
    sums_sc[7:8, :] = jnp.broadcast_to(loss - top, (1, ECOLS))
    cut.write_extra(outs, sums_sc[...])
    cut.write(at_ref, outs, 3, 0, embed_back(d_h, x_ref, agg_ref, embk_ref, vid_ref).T)


def last(at, cut, grads, h, d_mid, dmod0, dmod1, loss, mods, w0, x, agg, embk, vid4):
    return call(
        lambda *refs: last_kernel(*refs, cut=cut),
        "last",
        cut.shapes(ECOLS, True),
        [at, *grads, h, d_mid, dmod0, dmod1, loss, mods, w0, x, agg, embk, vid4],
        cost(1e9, 1e6),
        [pltpu.VMEM((48, ECOLS), F32)],
        limit=28,
    )


def swap(x, axis, size, by):
    return lax.ppermute(x, axis, [(i, i ^ by) for i in range(size)])


def place_kernel(at_ref, *refs, rows):
    out_ref, inputs = refs[-1], refs[:-1]
    s, z, c = at_ref[AT_S], at_ref[AT_Z], at_ref[AT_C]
    for jc in range(2):
        for js in range(4):
            source = inputs[4 * jc + js]
            for jz in range(4):
                at = rows_at((z ^ jz) * 2 + (c ^ jc), rows)
                if len(source.shape) == 3:
                    out_ref[s ^ js, at, :] = source[jz]
                    continue
                for k in range(source.shape[1]):
                    out_ref[s ^ js, at, D * k : D * (k + 1)] = source[jz, k]


def placed(at, own, got):
    rows = own[0].shape[-2]
    width = math.prod(own[0].shape[1:]) // rows
    return call(
        lambda *refs: place_kernel(*refs, rows=rows),
        "placed",
        [((4, 8 * rows, width), BF16)],
        [at, *own, *got],
        cost(0, 1e5),
        limit=8,
    )[0]


def first_kernel(at_ref, own_ref, gota_ref, gotb_ref, emb_ref, mods_ref, out_ref):
    rows = own_ref.shape[2]
    total = jnp.zeros((rows, D), F32)
    for jc in range(2):
        for jz in range(4):
            ref, i = (own_ref, jz) if jc == 0 else ((gota_ref, gotb_ref)[jz // 2], jz % 2)
            row = (at_ref[AT_Z] ^ jz) * 2 + (at_ref[AT_C] ^ jc)
            emb_ref[rows_at(row, rows), :] = ref[i, 0]
            total = total + (ref[i, 1].astype(F32) + ref[i, 2].astype(F32))
    mods_ref[...] = total
    for i in range(AT_LABEL):
        out_ref[i] = at_ref[i]
    labels = [ref[0, 1, 0:8, 0:128].astype(F32) for ref in (own_ref, gota_ref)]
    labels = jnp.where(at_ref[AT_OWN] == 1, labels[0], labels[1])
    picked = jnp.where(sublane((8, 128)) == 6 + at_ref[AT_WHICH], labels, 0.0)
    out_ref[AT_LABEL] = jnp.max(picked).astype(jnp.int32)


def pack_kernel(at_ref, labels_ref, *refs, split):
    sources, (first_ref, zero_ref, one_ref), held, sems = refs[:7], refs[7:10], refs[10:17], refs[17]
    copies = [
        pltpu.make_async_copy(source, target, sems.at[i])
        for i, (source, target) in enumerate(zip(sources, held))
    ]
    for copy in copies:
        copy.start()
    emb_ref, qkv_ref, out_ref, up_ref, down_ref, ada_ref, head_ref = held
    rows = emb_ref.shape[0]
    blocks = first_ref
    blocks[...] = jnp.zeros_like(blocks)
    for i in (1, 2, 3, 4, 6):
        copies[i].wait()
    col = lax.broadcasted_iota(jnp.int32, (PIXELS, 128), 0)
    lane = lax.broadcasted_iota(jnp.int32, (PIXELS, 128), 1)
    for j in range(4):

        def fill(j=j):
            for layer, ref in enumerate((zero_ref, one_ref)):
                part = qkv_ref[layer, :, D * j : D * (j + 1)] if j < 3 else out_ref[layer]
                source = (up_ref if j < 2 else down_ref)[layer]
                source = source[:, HALF * (j % 2) : HALF * (j % 2 + 1)].astype(BF16)
                if split and layer == 0:
                    ref[0] = part.astype(BF16)
                    ref[1] = source[:, :D]
                    ref[2] = source[:, D:]
                    continue
                at = 0 if split else j
                ref[at, :, :D] = part.astype(BF16)
                ref[at, :, D : 3 * D] = source
            wide = lane + 128 * (j % 2)
            pick = jnp.logical_and(col == 2 * wide + j // 2, wide < PIXELS // 2).astype(BF16)
            one_ref[0 if split else j, :, 3 * D :] = dot(head_ref[...].astype(BF16), pick).astype(BF16)

        if split:
            pl.when(at_ref[AT_S] == j)(fill)
        else:
            fill()
    copies[0].wait()
    copies[5].wait()
    blocks[0, :rows, :EROWS] = emb_ref[...].astype(BF16)
    silu, _ = lead_parts(emb_ref)
    for layer in range(LAYERS):
        for i in range(6):
            ada = ada_ref[layer, :, D * i : D * (i + 1)].astype(BF16).astype(F32)
            for g in range(GROUPS):
                at = 8 * (GROUPS * layer + g) + i
                value = column_sum(silu[:, g : g + 1] * ada)
                top = value.astype(BF16)
                blocks[1, at : at + 1, :] = top
                blocks[2, at : at + 1, :] = (value - top.astype(F32)).astype(BF16)
    for i in range(2):
        label = jnp.full((1, D), labels_ref[i], jnp.int32).astype(F32).astype(BF16)
        blocks[1, 6 + i : 7 + i, :] = label
    if split:
        zero_ref[3:6] = blocks[...]


def packed(at, labels, weights, split):
    rows = weights[0].shape[0]
    quarters = 1 if split else 4
    return pl.pallas_call(
        lambda *refs: pack_kernel(*refs, split=split),
        in_specs=[SMEM, SMEM] + [HBM] * 7,
        out_specs=[VMEM] * 3,
        out_shape=[
            jax.ShapeDtypeStruct((3, 48, ECOLS), BF16),
            jax.ShapeDtypeStruct((6, rows, D) if split else (4, rows, 3 * D), BF16),
            jax.ShapeDtypeStruct((quarters, rows, 3 * D + 128), BF16),
        ],
        scratch_shapes=[pltpu.VMEM(w.shape, F32) for w in weights] + [pltpu.SemaphoreType.DMA((7,))],
        compiler_params=pltpu.CompilerParams(vmem_limit_bytes=60 << 20),
        cost_estimate=cost(0, 1e6),
        name="packed",
    )(at, labels, *weights)


def two_rows(v):
    loss = v[6:7] + v[7:8]
    top = loss.astype(BF16).astype(F32)
    row = sublane(v.shape)
    return jnp.where(row == 6, top, jnp.where(row == 7, loss - top, v)).astype(BF16)


class Rows:
    def __init__(self, refs, cuts):
        self.refs, self.cuts = refs, cuts

    def fill(self, out):
        for ref, a, b in zip(self.refs, self.cuts[:-1], self.cuts[1:]):
            out[a:b] = ref[...]


def add_core_kernel(at_ref, kept_ref, pieces, own_ref, *refs):
    sends, got_ref = refs[:3], refs[3]
    pieces.fill(got_ref)
    zs = 4
    for j in range(4):
        here = pl.ds((at_ref[AT_S] ^ j) * zs, zs)
        value = kept_ref[here].astype(F32) + got_ref[here].astype(F32)
        if j == 0:
            own_ref[:zs] = value
        else:
            sends[j - 1][:zs] = value.astype(BF16)
    if own_ref.shape[0] > zs:
        value = two_rows(kept_ref[4 * zs].astype(F32) + got_ref[4 * zs].astype(F32))
        own_ref[zs] = value.astype(F32)
        for send in sends:
            send[zs] = value


def summed(refs, at):
    a, b, c, d = (ref[at].astype(F32) for ref in refs)
    return (a + b) + (c + d)


def add_segment_kernel(at_ref, own_ref, a_ref, b_ref, c_ref, kept_ref, *sends):
    refs = (own_ref, a_ref, b_ref, c_ref)
    for j in range(4):
        value = summed(refs, at_ref[AT_Z] ^ j)
        if j == 0:
            kept_ref[0] = value
        else:
            sends[j - 1][0] = value.astype(BF16)
    if kept_ref.shape[0] > 1:
        value = two_rows(summed(refs, 4))
        kept_ref[1] = value.astype(F32)
        for send in sends:
            send[1] = value


def add_plane_kernel(at_ref, own_ref, a_ref, b_ref, c_ref, out_ref, *more):
    refs = (own_ref, a_ref, b_ref, c_ref)
    out_ref[...] = summed(refs, 0).astype(BF16)
    if more:
        more[0][...] = summed(refs, 1)


def add_half_kernel(at_ref, own_ref, got_ref, kept_ref, send_ref):
    kept_ref[...] = own_ref[0] + got_ref[0].astype(F32)
    send_ref[...] = (own_ref[1] + got_ref[1].astype(F32)).astype(BF16)


def add_both_kernel(at_ref, own_ref, got_ref, out_ref):
    out_ref[...] = (own_ref[...] + got_ref[...].astype(F32)).astype(BF16)


def both_split_kernel(at_ref, kept_ref, pieces, owna_ref, ownb_ref, a_ref, b_ref, got_ref):
    pieces.fill(got_ref)
    for half, (own, send, by) in enumerate(((owna_ref, a_ref, 1), (ownb_ref, b_ref, 2))):
        for i, j in enumerate((0, 3 - by, by, 3)):
            here = pl.ds((at_ref[AT_S] ^ j) * 4 + 2 * half, 2)
            value = kept_ref[here].astype(F32) + got_ref[here].astype(F32)
            if i < 2:
                own[i] = value
            else:
                send[i - 2] = value.astype(BF16)


def both_half_kernel(at_ref, owna_ref, ownb_ref, gota_ref, gotb_ref, kept_ref, a_ref, b_ref):
    for half, (own, got, send) in enumerate(((owna_ref, gota_ref, a_ref), (ownb_ref, gotb_ref, b_ref))):
        kept_ref[2 * half : 2 * half + 2] = own[0] + got[0].astype(F32)
        send[...] = (own[1] + got[1].astype(F32)).astype(BF16)


def both_planes_kernel(at_ref, own_ref, gota_ref, gotb_ref, kept_ref, send_ref, sc):
    sc[0:2] = own_ref[0:2] + gota_ref[...].astype(F32)
    sc[2:4] = own_ref[2:4] + gotb_ref[...].astype(F32)
    for i, j in enumerate((0, 2, 1, 3)):
        value = sc[at_ref[AT_Z] ^ j]
        if i < 2:
            kept_ref[i] = value
        else:
            send_ref[i - 2] = value.astype(BF16)


class Plain:
    split = False

    def __init__(self, sizes, at):
        self.sizes, self.at = sizes, at
        self.order = at.at[AT_S].set(0)

    def first_layer(self, first, x):
        self.shares = first
        return x

    def next_layer(self, x, *wait):
        return x

    next_layer_two = next_layer

    def first(self, labels, pairs, *wait):
        x, rows = self.shares, D // (2 * self.sizes["z"])
        emb = lax.all_gather(x[0, :rows], ("z", "c"), axis=0, tiled=True)
        mods = lax.psum(x[1].astype(F32) + x[2].astype(F32), ("z", "c"))
        got = lax.ppermute(labels, CHIP, pairs)
        label = jnp.where(self.at[AT_OWN] == 1, labels, got)[self.at[AT_WHICH]]
        return emb, mods, self.at.at[AT_LABEL].set(label)

    def columns(self, stack, *wait):
        return (stack,)

    def placed(self, own, *wait):
        return lax.all_gather(own[0], ("z", "c"), axis=1, tiled=True)

    def total(self, x):
        return lax.psum(x, ("z", "c")), jnp.zeros_like(x)

    def core(self, g):
        own = lax.psum_scatter(g[0].astype(F32), ("z", "c"), scatter_dimension=1, tiled=True)
        return lax.psum(own, "s"), lax.psum(g[1][0].astype(F32), CHIP)

    def core_both(self, g, count):
        return self.core(g)

    def segment(self, x, flops=0):
        return x

    plane = both_one = both_planes = planes_one = planes_two = segment

    def shared(self, x, wait=()):
        return [x[0][j].astype(BF16) for j in range(4)]

    far_shared = shared


class Squares(Plain):
    split = True

    def __init__(self, sizes, at):
        self.sizes, self.at, self.order = sizes, at, at

    def across(self, x, axis):
        return [swap(x, axis, 4, by) for by in (1, 2, 3)]

    def doubled(self, x, axis):
        x = jnp.stack([x, swap(x, axis, 4, 1)])
        return jnp.concatenate([x, swap(x, axis, 4, 2)])

    def first_layer(self, first, x):
        pieces = [x] + self.across(x, "z")
        self.shares = jnp.stack([p[3:] for p in pieces])
        return jnp.stack([p[:3] for p in pieces])

    def next_layer(self, x, *wait):
        return jnp.stack([x[0], swap(after(x[0], *wait), "z", 4, 1)])

    def next_layer_two(self, x, *wait):
        return jnp.concatenate([x, swap(after(x, *wait), "z", 4, 2)])

    def first(self, labels, pairs, *wait):
        own = after(self.shares, *wait)
        return call(
            first_kernel,
            "first",
            [((D, ECOLS), BF16), ((48, D), F32), ((AT_LABEL + 1,), jnp.int32)],
            [self.at, own, *self.pieces(own, 2)[0]],
            cost(0, 1e4),
            out_spaces=[VMEM, VMEM, SMEM],
        )

    def columns(self, stack, *wait):
        return [stack] + self.across(after(stack, *wait), "s")

    def placed(self, own, *wait):
        got = [swap(after(x, *wait) if i else x, "c", 2, 1) for i, x in enumerate(own)]
        return placed(self.at, own, got)

    def total(self, x):
        one, two, three = self.across(x, "z")
        x = (x + one) + (two + three)
        return x, swap(x, "c", 2, 1)

    def run(self, kernel, name, outs, inputs, scratch=(), flops=0):
        return call(kernel, name, outs, [self.at, *inputs], cost(flops, 1e5), scratch)

    def pieces(self, x, parts):
        cuts = [x.shape[0] * i // parts for i in range(parts + 1)]
        return [swap(x[a:b], "c", 2, 1) for a, b in zip(cuts[:-1], cuts[1:])], cuts

    def core(self, g):
        kept, sent = g
        count, rows, width = kept.shape
        full = (4 + count % 4, rows, width)
        got, cuts = self.pieces(sent, 2)
        outs = [(full, F32)] + [(full, BF16)] * 3
        return self.run(
            lambda at, kept, *refs: add_core_kernel(at, kept, Rows(refs[:2], cuts), *refs[2:]),
            "add_core", outs, [kept, *got], [pltpu.VMEM(kept.shape, BF16)],
        )

    def planes_one(self, x):
        own, send = x
        one = own.shape[1:]
        outs = [(one, F32), (one, BF16)]
        return self.run(add_half_kernel, "add_half", outs, [own, swap(send, "z", 4, 1)])

    def planes_two(self, x):
        own, send = x
        outs = [(own.shape, BF16)]
        return self.run(add_both_kernel, "add_both", outs, [own, swap(send, "z", 4, 2)])

    def core_both(self, g, count):
        kept, sent = g
        rows, width = kept.shape[1:]
        part = (2, 2, rows, width)
        got, cuts = self.pieces(sent, count)
        n = 2 + len(got)
        return self.run(
            lambda *refs: both_split_kernel(*refs[:2], Rows(refs[2:n], cuts), *refs[n:]),
            "both_split", [(part, F32)] * 2 + [(part, BF16)] * 2,
            [kept, *got], [pltpu.VMEM(kept.shape, BF16)],
        )

    def both_one(self, x, flops=0):
        own_a, own_b, a, b = x
        part = own_a.shape[1:]
        return self.run(
            both_half_kernel, "both_half", [((4,) + part[1:], F32)] + [(part, BF16)] * 2,
            [own_a, own_b, swap(a, "s", 4, 1), swap(b, "s", 4, 2)], flops=flops,
        )

    def both_planes(self, x):
        own, a, b = x
        part = (2,) + own.shape[1:]
        return self.run(
            both_planes_kernel, "both_planes", [(part, F32), (part, BF16)],
            [own, swap(a, "s", 4, 2), swap(b, "s", 4, 1)], [pltpu.VMEM(own.shape, F32)],
        )

    def segment(self, x):
        own, *sends = x
        count, rows, width = own.shape
        one = (count - 3, rows, width)
        got = [swap(y, "s", 4, j + 1) for j, y in enumerate(sends)]
        return call(
            add_segment_kernel, "add_segment", [(one, F32)] + [(one, BF16)] * 3,
            [self.at, own, *got], cost(0, 1e5),
        )

    def plane(self, x):
        own, *sends = x
        count, rows, width = own.shape
        got = [swap(y, "z", 4, j + 1) for j, y in enumerate(sends)]
        return call(
            add_plane_kernel, "add_plane",
            [((rows, width), BF16)] + [((rows, width), F32)] * (count - 1),
            [self.at, own, *got], cost(0, 1e5),
        )

    def shared(self, x, wait=()):
        return [x[0]] + self.across(after(x[0], *wait), "s")

    def far_shared(self, x, wait=()):
        pieces = self.doubled(after(x[0], *wait), "s")
        return [pieces[j] for j in range(4)]


def lead_parts(emb_ref):
    lead = emb_ref[:, LEAD:EROWS].astype(BF16).astype(F32)
    gate = jax.nn.sigmoid(lead)
    return lead * gate, gate * (1.0 + lead * (1.0 - gate))


def ada_gradient(silu, sums_ref, layer, index):
    total = 0.0
    for group in range(GROUPS):
        at = 8 * (GROUPS * layer + group) + index
        total = total + silu[:, group : group + 1] * sums_ref[at : at + 1, :D]
    return total


def square_sum(v):
    return jnp.sum(v * v, axis=(0, 1), keepdims=True)


def gather_kernel(at_ref, *refs, widths):
    pieces, (emb_ref, ada_ref, sums_ref), outs = refs[:12], refs[12:15], refs[15:]
    ordered, (lead_ref, square_ref) = outs[:3], outs[3:]
    total = jnp.zeros((1, 1), F32)
    for k, ref in enumerate(ordered):
        squares = []
        for j in range(4):
            piece = pieces[4 * k + j][...]
            ref[at_ref[AT_S] ^ j] = piece
            squares.append(square_sum(piece.astype(F32)))
        total = total + ((squares[0] + squares[1]) + (squares[2] + squares[3]))
    silu, slope = lead_parts(emb_ref)
    rows = silu.shape[0]
    lane = lax.broadcasted_iota(jnp.int32, (rows, 128), 1)
    lead = jnp.zeros((rows, 128), F32)
    for group in range(GROUPS):
        d_silu = jnp.zeros((rows, 1), F32)
        for layer in range(LAYERS):
            for i in range(6):
                at = 8 * (GROUPS * layer + group) + i
                ada = ada_ref[layer, :, D * i : D * (i + 1)].astype(BF16).astype(F32)
                d_silu = d_silu + jnp.sum(ada * sums_ref[at : at + 1, :D], axis=-1, keepdims=True)
        value = d_silu * slope[:, group : group + 1]
        total = total + square_sum(value)
        lead = jnp.where(lane == group, value, lead)
    for layer in range(LAYERS):
        for i in range(6):
            total = total + square_sum(ada_gradient(silu, sums_ref, layer, i))
    lead_ref[...] = lead
    square_ref[...] = jnp.broadcast_to(total, square_ref.shape)


def gathered(at, pieces, emb_t, ada, sums):
    widths = [group[0].shape for group in pieces]
    return call(
        lambda *refs: gather_kernel(*refs, widths=widths),
        "gathered",
        [((4,) + shape, BF16) for shape in widths]
        + [((widths[0][0], 128), F32), ((8, 128), F32)],
        [at, *pieces[0], *pieces[1], *pieces[2], emb_t, ada, sums],
        cost(0, 4e6),
    )


def update_kernel(at_ref, *refs, rate):
    g1_ref, g2_ref, g3_ref, lead_ref, sums_ref, own_ref, got_ref = refs[:7]
    state = refs[7:28]
    outs, (loss_ref, norm_ref) = refs[28:49], refs[49:51]
    results, sems = refs[51:72], refs[72]
    squares = own_ref[0:1, 0:1] + got_ref[0:1, 0:1]
    norm = jnp.sqrt(squares)
    factor = CLIP / jnp.maximum(norm, CLIP)
    norm_ref[...] = norm
    loss_ref[...] = sums_ref[6:7, 0:1] + sums_ref[7:8, 0:1]
    silu, _ = lead_parts(state[0])
    rows = silu.shape[0]

    def advance(index, at, g):
        w_ref, m_ref, a_ref = (state[index + 7 * k] for k in range(3))
        g = g.astype(F32) * factor
        m = KEEP * m_ref[at] + g
        w = w_ref[at] - rate * (BOOST if index == 0 else 1.0) * (g + KEEP * m)
        results[index + 7][at] = m
        results[index][at] = w
        results[index + 14][at] = KEEP * a_ref[at] + (1.0 - KEEP) * w

    copies = []

    def send(index, layer=None):
        for k in range(3):
            i = index + 7 * k
            source, target = results[i], outs[i]
            if layer is not None:
                source, target = source.at[layer], target.at[layer]
            copy = pltpu.make_async_copy(source, target, sems.at[i, layer or 0])
            copy.start()
            copies.append(copy)

    every = slice(None)
    for layer in range(LAYERS):
        for i in range(6):
            g = ada_gradient(silu, sums_ref, layer, i)
            advance(5, (layer, every, slice(D * i, D * (i + 1))), g)
        send(5, layer)
    qkv = (g3_ref, g2_ref)
    ff = ((g2_ref, D), (g1_ref, 0))
    for layer in range(LAYERS):
        ref, lane = ff[layer]
        for j in range(2):
            part = slice(HALF * j, HALF * (j + 1))
            advance(3, (layer, every, part), ref[j, :, lane : lane + HALF])
            advance(4, (layer, every, part), ref[2 + j, :, lane : lane + HALF])
        send(3, layer)
        send(4, layer)
    for layer in range(LAYERS):
        for j in range(3):
            advance(1, (layer, every, slice(D * j, D * (j + 1))), qkv[layer][j, :, :D])
        send(1, layer)
    for j in range(3):
        advance(2, (0, every, slice(128 * j, 128 * (j + 1))), g2_ref[j, :, D + HALF : D + HALF + 128])
    advance(2, (1,), g2_ref[3, :, :D])
    send(2)
    col = lax.broadcasted_iota(jnp.int32, (512, PIXELS), 1)
    row = lax.broadcasted_iota(jnp.int32, (512, PIXELS), 0)
    back = jnp.logical_and(row // 256 == col % 2, row % 256 == col // 2).astype(BF16)
    g_head = jnp.concatenate([g1_ref[j, :, HALF : HALF + 128] for j in range(4)], axis=-1)
    advance(6, (every,), dot(g_head, back))
    send(6)
    lane = lax.broadcasted_iota(jnp.int32, (rows, 128), 1)
    for j in range(3):
        g = g3_ref[3, :, 128 * j : 128 * j + 128].astype(F32)
        width = min(128, EROWS - 128 * j)
        if LEAD < 128 * j + width:
            first = LEAD - 128 * j
            for group in range(GROUPS):
                g = jnp.where(lane == first + group, lead_ref[:, group : group + 1], g)
        advance(0, (every, slice(128 * j, 128 * j + width)), g[:, :width])
    send(0)
    for copy in copies:
        copy.wait()


def updated(at, g, lead, sums, own, got, state, rate):
    shapes = [(x.shape, F32) for x in state]
    scalar = [((1, 1), F32)] * 2
    inputs = [at, *g, lead, sums, own, got, *state]
    return call(
        lambda *refs: update_kernel(*refs, rate=rate),
        "updated",
        shapes + scalar,
        inputs,
        cost(0, 2e7),
        [pltpu.VMEM(shape, kind) for shape, kind in shapes] + [pltpu.SemaphoreType.DMA((21, 2))],
        limit=24,
        out_spaces=[HBM] * 21 + [VMEM] * 2,
    )


def per_device(sizes, *arrays):
    (tiles_in, truth_in, labels, var_ids, basis) = arrays[:5]
    masters = arrays[5:12]
    segments, dp = sizes["s"], sizes["z"] * 2
    micro = tiles_in.shape[0]
    assert segments == 2 * micro
    rows = D // dp
    s, z, c = (lax.axis_index(name) for name in CHIP)
    which, owner = s % micro, s // micro
    at = jnp.stack([s, z, c, c == owner, which, 0]).astype(jnp.int32)
    fast = segments == 4 and sizes["z"] == 4
    move = (Squares if fast else Plain)(sizes, at)
    cut = Cut(sizes["z"], rows, move.split)
    views = []
    for k in range(3):
        w = list(arrays[5 + 7 * k : 12 + 7 * k])
        w[0], w[4] = w[0].T, w[4].transpose(0, 2, 1)
        views += w

    pairs = []
    for a in range(segments):
        for b in range(sizes["z"]):
            base = (a * sizes["z"] + b) * 2
            pairs.append((base + a // micro, base + 1 - a // micro))
    pick = lambda x: lax.dynamic_index_in_dim(x, which, 0, keepdims=False).T

    first, *bundles = packed(at, labels, views[:7], fast)
    stack0 = move.first_layer(first, bundles[0])
    tiles = pick(tiles_in)
    tiles_got = lax.ppermute(tiles, CHIP, pairs)
    columns0 = move.columns(stack0)
    stack1 = move.next_layer(bundles[1])
    emb, mods, at = move.first(labels, pairs, tiles_got, stack1)
    stack1 = move.next_layer_two(stack1, emb)
    vid4 = jnp.pad(jnp.repeat(var_ids, 4), (0, D - PIXELS), constant_values=-1)[None].astype(
        jnp.int32
    )
    h0, agg, x_all, embk = embed(at, tiles, tiles_got, emb, vid4)
    truth = pick(after(truth_in, h0, *columns0[1:]))
    half = truth.shape[1] // 2
    lanes = lambda core: jnp.where(core == 0, truth[:, :half], truth[:, half:])
    truth_got = lax.ppermute(lanes(1 - c), CHIP, pairs)
    truth = lanes(c)
    w0 = move.placed(columns0, h0, stack1)
    columns1 = move.columns(stack1, h0, *columns0[1:])
    h1, q0, own0, other0, att0, lse0, *kept = block_forward(after(at, truth_got), h0, mods, w0)
    w1 = move.placed(columns1, h1)
    q1, own1 = qkv_rows(at, h1, mods, w1)
    other1 = swap(own1, "c", 2, 1)
    d_mid, d_att, att1, lse1, g_out, dmod1, loss, *g_first = turn(
        at, cut, h1, q1, own1, other1, mods, w1, truth, truth_got, basis, 1.0 / (micro * dp)
    )
    d_q, d_k, d_v, *sent = attention_back(at, q1, own1, other1, lse1, att1, d_att, finish=True)
    got = [swap(x, "c", 2, 1) for x in sent]
    first = move.core_both(g_first, 1)
    d_mid, d_att, dmod1, dmod0, *g_second = between(
        after(at, *first), cut, [d_q, d_k, d_v, *got], h1, d_mid, g_out, dmod1, mods, w1, [att0, *kept], w0
    )
    first = move.both_one(first, 1e10)
    second = move.core_both([after(g_second[0], *first), g_second[1]], 3)
    d_q, d_k, d_v = attention_back(after(at, *first, *second), q0, own0, other0, lse0, att0, d_att)
    first = move.both_planes([after(first[0], d_q), *first[1:]])
    g_third = last(
        after(at, *first), cut, [d_q, d_k, d_v], h0, d_mid, dmod0, dmod1, loss, mods, w0, x_all, agg, embk, vid4
    )
    first = move.planes_one(first)
    second = move.both_one(second)
    third = move.core([after(g_third[0], *first), after(g_third[1], *first, *second)])
    first = move.planes_two([after(first[0], *third), first[1]])
    second = move.planes_one(move.both_planes(second))
    third = move.segment([after(third[0], *first, *second), *third[1:]])
    second = move.planes_two(second)
    ends = [move.far_shared(first), move.shared(second)]
    third = move.plane(third)
    ends.append(move.shared(third))
    sums = third[1]

    g1, g2, g3, lead_g, squares = gathered(move.order, ends, views[0], views[5], sums)
    own, got = move.total(squares)
    count = sum(w.size for w in masters) * dp
    rate = 0.02 * math.sqrt(count) / CLIP
    *new, loss_value, norm = updated(at, (g1, g2, g3), lead_g, sums, own, got, views, rate)
    for k in range(3):
        new[7 * k] = new[7 * k].T
        new[7 * k + 4] = new[7 * k + 4].transpose(0, 2, 1)
    return (loss_value.reshape(()), norm.reshape(()), *new)


def solution(mesh):
    segments, dp = mesh.shape["segment"], mesh.shape["dp"]
    sizes = {"s": segments, "z": dp // 2, "c": 2}
    split = Mesh(mesh.devices.reshape(segments, dp // 2, 2), CHIP)
    d = ("z", "c")
    weights = (
        P(None, d),
        P(None, d, None),
        P(None, d, None),
        P(None, d, None),
        P(None, None, d),
        P(None, d, None),
        P(d, None),
    )
    return jax.shard_map(
        lambda *arrays: per_device(sizes, *arrays),
        mesh=split,
        in_specs=(P(d, None, None), P(d, None, None), P(d), P(), P()) + weights * 3,
        out_specs=(P(), P()) + weights * 3,
        check_vma=False,
    )
```
